32 devices in a mesh: rep: 8 (over y, x, core), fsdp: 4 (over z).
Axes of the slice: x: 2, y: 2, z: 4, core: 2. Of those that a mesh axis runs over, the one named last changes fastest.
Arguments:
- tokens: bfloat16 [8192, 1024], P(('rep', 'fsdp')), may hold values from -6 to 6
- doc_lengths: int32 [32, 8], P(('rep', 'fsdp')), may hold values from 0 to 256, as said below
- attn_norm: bfloat16 [1024], P('fsdp'), may hold values from 0.5 to 1.5
- w_query: bfloat16 [1024, 2048], P('fsdp'), may hold values from -0.1875 to 0.1875
- key_matrix: bfloat16 [1024, 1024], P('fsdp'), may hold values from -0.1875 to 0.1875
- value_matrix: bfloat16 [1024, 1024], P('fsdp'), may hold values from -0.1875 to 0.1875
- head_norms: bfloat16 [2, 128], replicated, may hold values from 0.25 to 1.75
- w_out: bfloat16 [2048, 1024], P('fsdp'), may hold values from -0.5 to 0.5
- ffn_norm: bfloat16 [1024], P('fsdp'), may hold values from 0.5 to 1.5
- w_gate: bfloat16 [1024, 3072], P('fsdp'), may hold values from -0.1875 to 0.1875
- w_up: bfloat16 [1024, 3072], P('fsdp'), may hold values from -0.1875 to 0.1875
- w_down: bfloat16 [3072, 1024], P('fsdp'), may hold values from -0.109375 to 0.109375
- cotangent: bfloat16 [8192, 1024], P(('rep', 'fsdp')), may hold values from -6 to 6
Outputs:
- mixed: bfloat16 [8192, 1024], P(('rep', 'fsdp'))
- d_tokens: bfloat16 [8192, 1024], P(('rep', 'fsdp'))
- d_attn_norm: float32 [1024], P('fsdp')
- d_w_query: float32 [1024, 2048], P('fsdp')
- d_w_key: float32 [1024, 1024], P('fsdp')
- d_w_value: float32 [1024, 1024], P('fsdp')
- d_head_norms: float32 [2, 128], replicated
- d_w_out: float32 [2048, 1024], P('fsdp')
- d_ffn_norm: float32 [1024], P('fsdp')
- d_w_gate: float32 [1024, 3072], P('fsdp')
- d_w_up: float32 [1024, 3072], P('fsdp')
- d_w_down: float32 [3072, 1024], P('fsdp')
The draws below stay inside these ranges and needn't reach their ends.
Inputs may be any that keep to these rules, and one draw needn't show every extreme that they name: `doc_lengths`: row j lists the sequences packed from the first token row of device block j onward; zeros are empty slots; each row sums to 128 or more and to 256 or less; in every draw some device holds one sequence of 256 tokens.
All inputs are finite; a program needn't handle non-finite values.
Results may differ from the reference program's by a relative error of at most 0.02.
Values may be sent and summed in bfloat16 or wider, within the bound.
A program may use at most 192 MiB of HBM per device.

```python
import math
import jax
import jax.numpy as jnp
from jax import lax

D = 1024
QUERY_HEADS = 16
KEY_VALUE_HEADS = 8
HEAD_WIDTH = 128
FF = 3072
TOK_DEV = 256
DOC_SLOTS = 8
QW = 2048
KW = 1024
TOKENS = 8192
N_REP = 8
N_FSDP = 4


def draw_tokens(key, part):
    noise_key = jax.random.fold_in(key, 11)
    value_rows = jnp.clip(jax.random.normal(noise_key, (TOKENS, D), jnp.float32), -6.0, 6.0)
    return value_rows.astype(jnp.bfloat16)


def draw_doc_lengths(key, part):
    device_total = N_REP * N_FSDP
    live_key = jax.random.fold_in(key, 23)
    weight_key = jax.random.fold_in(key, 29)
    keep_key = jax.random.fold_in(key, 31)
    full_key = jax.random.fold_in(key, 37)
    live_counts = jax.random.randint(live_key, (device_total, 1), TOK_DEV // 2, TOK_DEV + 1)
    slot_weights = jax.random.randint(weight_key, (device_total, DOC_SLOTS), 1, 9)
    keep_slots = jax.random.randint(keep_key, (device_total, DOC_SLOTS), 0, 2)
    slot_ids = jnp.arange(DOC_SLOTS)
    keep_slots = jnp.where(slot_ids[None, :] == 0, 1, keep_slots)
    slot_weights = slot_weights * keep_slots
    shares = live_counts * slot_weights // jnp.sum(slot_weights, axis=1, keepdims=True)
    remainder = live_counts[:, 0] - jnp.sum(shares, axis=1)
    shares = shares + jnp.where(slot_ids[None, :] == 0, remainder[:, None], 0)
    full_device = jax.random.randint(full_key, (), 0, device_total)
    single = jnp.where(slot_ids == 0, TOK_DEV, 0)
    shares = jnp.where((jnp.arange(device_total) == full_device)[:, None], single[None, :], shares)
    return shares.astype(jnp.int32)


def spiked(drawn, stream_key, source, target, shards_of, factor):
    owner, partner = [(jnp.arange(drawn.shape[axis_at]) // (drawn.shape[axis_at] // shards_of)).reshape([-1 if axis == axis_at else 1 for axis in range(drawn.ndim)]) for axis_at in (source, target)]
    chosen = jax.random.permutation(stream_key, shards_of)[partner]
    strong = (owner == chosen) | (owner == (partner + shards_of // 2) % shards_of)
    return jnp.where(strong, factor * drawn, drawn)


def block_levels(key, extent, shards, low, largest):
    def one(dim, blocks):
        steps = jax.random.uniform(jax.random.fold_in(jax.random.fold_in(key, 6), dim), (blocks,), jnp.float32, low / len(shards), largest / len(shards))
        return jnp.repeat(jnp.exp(steps), extent[dim] // blocks).reshape((-1,) + (1,) * (len(extent) - dim - 1))

    level = one(*shards[0])
    for cut in shards[1:]:
        level = level * one(*cut)
    return level


def scatter_about(stream_key, dims, scale, limit, shards=(), kind=jnp.bfloat16):
    drawn = jax.random.normal(stream_key, dims, jnp.float32) * scale
    if len(shards) > 0:
        drawn = block_levels(stream_key, dims, shards, -0.22, 0.18) * drawn
    return jnp.clip(drawn, min=-limit, max=limit).astype(kind)


def gaussian_with(key, extent, scale, limit, split, heavy, kind=jnp.bfloat16):
    array = scale * jax.random.normal(key, extent, jnp.float32)
    if split:
        array = array * block_levels(key, extent, split, -0.22, 0.18)
    return jnp.clip(spiked(array, jax.random.fold_in(key, 3), *heavy), -limit, limit).astype(kind)


def setup_inputs(seed: int = 0) -> dict:
    splits = jax.random.split(jax.random.key(seed), 14)
    return {
        "tokens": draw_tokens(jax.random.fold_in(splits[13], 71), 0),
        "doc_lengths": draw_doc_lengths(jax.random.fold_in(splits[13], 71), 0),
        "attn_norm": jnp.clip(1.0 + 0.1 * jax.random.normal(splits[2], (D,), jnp.float32), 0.5, 1.5).astype(jnp.bfloat16),
        "w_query": scatter_about(splits[3], (D, QW), D ** -0.5, 0.1875, ((0, 4),)),
        "key_matrix": scatter_about(splits[4], (D, KW), D ** -0.5, 0.1875, ((0, 4),)),
        "value_matrix": scatter_about(splits[5], (D, KW), D ** -0.5, 0.1875, ((0, 4),)),
        "head_norms": jnp.clip(1.0 + 0.15 * jax.random.normal(splits[6], (2, HEAD_WIDTH), jnp.float32), 0.25, 1.75).astype(jnp.bfloat16),
        "w_out": scatter_about(splits[7], (QW, D), (QW // 16) ** -0.5, 0.5, ((0, 4),)),
        "ffn_norm": jnp.clip(1.0 + 0.1 * jax.random.normal(splits[8], (D,), jnp.float32), 0.5, 1.5).astype(jnp.bfloat16),
        "w_gate": scatter_about(splits[9], (D, FF), D ** -0.5, 0.1875, ((0, 4),)),
        "w_up": scatter_about(splits[10], (D, FF), D ** -0.5, 0.1875, ((0, 4),)),
        "w_down": scatter_about(splits[11], (FF, D), FF ** -0.5, 0.109375, ((0, 4),)),
        "cotangent": gaussian_with(splits[12], (TOKENS, D), 1.0, 6.0, ((0, 32),), (0, 1, 32, 2.75)),
    }


EPS = 1e-06
ROPE_BASE = 1000000.0
NEG_FILL = -1e+30
HIGHEST = lax.Precision.HIGHEST

@jax.custom_vjp
def low(v):
    return lax.optimization_barrier(v.astype(jnp.bfloat16)).astype(jnp.float32)

@jax.custom_vjp
def low_back(v):
    return v

def low_keep(v):
    return (low(v), None)

def low_pass(kept, grad):
    return (grad,)

def back_keep(v):
    return (v, None)

def back_low(kept, grad):
    return (low(grad),)
low.defvjp(low_keep, low_pass)
low_back.defvjp(back_keep, back_low)

def matrix_product(left, right):
    return jnp.dot(left, right, precision=HIGHEST, preferred_element_type=jnp.float32)

def layout(lengths, count_of_rows):
    seq_ends = jnp.cumsum(lengths).astype(jnp.int32)
    seq_starts = seq_ends - lengths
    row_ids = jnp.arange(count_of_rows, dtype=jnp.int32)
    segment = lax.optimization_barrier(jnp.sum((row_ids[:, None] >= seq_ends[None, :]).astype(jnp.int32), axis=1))
    slot_ids = jnp.arange(lengths.shape[0], dtype=jnp.int32)
    member = (segment[:, None] == slot_ids[None, :]).astype(jnp.int32)
    position = row_ids - lax.optimization_barrier(jnp.sum(member * seq_starts[None, :], axis=1))
    live_rows = row_ids < seq_ends[-1]
    causal = (segment[:, None] == segment[None, :]) & (row_ids[None, :] <= row_ids[:, None]) & live_rows[:, None]
    allowed = causal | (row_ids[:, None] == row_ids[None, :])
    return (position, live_rows, allowed)

def rope_tables(position, width):
    half_width = width // 2
    index = jnp.arange(half_width, dtype=jnp.float32)
    freq_table = jnp.exp(index * (-2.0 * math.log(ROPE_BASE) / width))
    angle = position.astype(jnp.float32)[:, None] * freq_table[None, :]
    return (jnp.cos(angle), jnp.sin(angle))

def apply_rotation(values_in, cosine_table, sine_table):
    half_width = values_in.shape[-1] // 2
    first_half = values_in[..., :half_width]
    second_half = values_in[..., half_width:]
    cos_rows = cosine_table[:, None, :]
    sin_rows = sine_table[:, None, :]
    return jnp.concatenate([first_half * cos_rows - second_half * sin_rows, second_half * cos_rows + first_half * sin_rows], axis=-1)

def head_normalize(values_in, gain_row):
    head_scale = lax.rsqrt(lax.optimization_barrier(jnp.mean(values_in * values_in, axis=2, keepdims=True)) + EPS)
    return values_in * head_scale * gain_row

def layer_forward(inputs, attn_norm, w_query, key_matrix, value_matrix, head_norms, w_out, ffn_norm, w_gate, w_up, w_down, cosine_table, sine_table, live_rows, allowed):
    count_of_rows = inputs.shape[0]
    group_width = QUERY_HEADS // KEY_VALUE_HEADS
    score_scale = HEAD_WIDTH ** (-0.5)
    first_scale = lax.rsqrt(lax.optimization_barrier(jnp.mean(inputs * inputs, axis=1, keepdims=True)) + EPS)
    normalized_rows = low(inputs * first_scale * attn_norm)
    query = low_back(matrix_product(normalized_rows, w_query)).reshape(count_of_rows, QUERY_HEADS, HEAD_WIDTH)
    keys_before_rotation = low_back(matrix_product(normalized_rows, key_matrix)).reshape(count_of_rows, KEY_VALUE_HEADS, HEAD_WIDTH)
    value_rows = low(low_back(matrix_product(normalized_rows, value_matrix))).reshape(count_of_rows, KEY_VALUE_HEADS, HEAD_WIDTH)
    query_normed = head_normalize(query, head_norms[0])
    key_normed = head_normalize(keys_before_rotation, head_norms[1])
    rotated_query = low(apply_rotation(query_normed, cosine_table, sine_table))
    key_rot = low(apply_rotation(key_normed, cosine_table, sine_table))
    query_head_rows = jnp.moveaxis(rotated_query.reshape(count_of_rows, KEY_VALUE_HEADS, group_width, HEAD_WIDTH), 1, 0)
    key_heads = jnp.moveaxis(key_rot, 1, 0)
    value_head_rows = jnp.moveaxis(value_rows, 1, 0)

    def attend(parts):
        query_j, key_j, value_j = parts
        scores = low_back(jnp.einsum('tgd,sd->gts', query_j, key_j, precision=HIGHEST) * score_scale)
        scores = jnp.where(allowed[None], scores, NEG_FILL)
        highest = lax.optimization_barrier(jnp.max(scores, axis=2, keepdims=True))
        expd = jnp.exp(scores - highest)
        probs = expd / lax.optimization_barrier(jnp.sum(expd, axis=2, keepdims=True))
        return jnp.einsum('gts,sd->tgd', low(probs), value_j, precision=HIGHEST)
    mixed_heads = lax.map(jax.checkpoint(attend), (query_head_rows, key_heads, value_head_rows))
    attended = low(low_back(jnp.moveaxis(mixed_heads, 0, 1).reshape(count_of_rows, QUERY_HEADS * HEAD_WIDTH)))
    hidden = inputs + low_back(matrix_product(attended, w_out))
    second_scale = lax.rsqrt(lax.optimization_barrier(jnp.mean(hidden * hidden, axis=1, keepdims=True)) + EPS)
    normed_two = low(hidden * second_scale * ffn_norm)
    gate = low_back(matrix_product(normed_two, w_gate))
    up_part = low_back(matrix_product(normed_two, w_up))
    activated = low(jax.nn.silu(gate) * up_part)
    output = hidden + low_back(matrix_product(activated, w_down))
    return jnp.where(live_rows[:, None], output, 0.0)

def reference(tokens, doc_lengths, attn_norm, w_query, key_matrix, value_matrix, head_norms, w_out, ffn_norm, w_gate, w_up, w_down, cotangent):
    weights = tuple((matrix.astype(jnp.float32) for matrix in (attn_norm, w_query, key_matrix, value_matrix, head_norms, w_out, ffn_norm, w_gate, w_up, w_down)))
    token_blocks = tokens.reshape(N_REP * N_FSDP, TOK_DEV, D)
    cot_blocks = cotangent.reshape(N_REP * N_FSDP, TOK_DEV, D)

    def one_device(totals, scan_item):
        token_block, lengths, cot_block = scan_item
        position, live_rows, allowed = layout(lengths, TOK_DEV)
        cosine_table, sine_table = rope_tables(position, HEAD_WIDTH)

        def forward(inputs, *params):
            return layer_forward(inputs, *params, cosine_table, sine_table, live_rows, allowed)
        output, pullback = jax.vjp(forward, token_block.astype(jnp.float32), *weights)
        gradients = pullback(cot_block.astype(jnp.float32))
        totals = tuple((total + grad for total, grad in zip(totals, gradients[1:])))
        return (totals, (output.astype(jnp.bfloat16), gradients[0].astype(jnp.bfloat16)))
    start_totals = tuple((jnp.zeros(matrix.shape, jnp.float32) for matrix in weights))
    totals, (outputs, input_grads) = lax.scan(one_device, start_totals, (token_blocks, doc_lengths, cot_blocks))
    grad_scale = 1.0 / math.sqrt(TOKENS)
    return (outputs.reshape(TOKENS, D), input_grads.reshape(TOKENS, D), totals[0] * grad_scale, totals[1] * grad_scale, totals[2] * grad_scale, totals[3] * grad_scale, totals[4] * grad_scale, totals[5] * grad_scale, totals[6] * grad_scale, totals[7] * grad_scale, totals[8] * grad_scale, totals[9] * grad_scale)
```

```python
import functools
import math

import jax
import jax.numpy as jnp
import numpy as np
from jax import lax
from jax.experimental import pallas as pl
from jax.experimental.pallas import tpu as pltpu
from jax.sharding import PartitionSpec as P

EPS = 1e-06
ROPE_BASE = 1000000.0
NEG_FILL = -1e30
HEAD = 128
T = 8
MESH = pl.DeviceIdType.MESH
BF = jnp.bfloat16
F32 = jnp.float32


def mm(a, b):
    return lax.dot_general(a, b, (((1,), (0,)), ((), ())), preferred_element_type=F32)


def mm_nt(a, b):
    return lax.dot_general(a, b, (((1,), (1,)), ((), ())), preferred_element_type=F32)


def mm_tn(a, b):
    return lax.dot_general(a, b, (((0,), (0,)), ((), ())), preferred_element_type=F32)


def rope_table(rows):
    half = HEAD // 2
    freq = np.exp(np.arange(half, dtype=np.float64) * (-2.0 * math.log(ROPE_BASE) / HEAD))
    freq = freq.astype(np.float32)
    angle = (np.arange(rows, dtype=np.float32)[:, None] * freq[None, :]).astype(np.float64)
    cos, sin = np.cos(angle), np.sin(angle)
    full = np.concatenate([cos, cos, -sin, sin], axis=1).astype(np.float32)
    parts = []
    rest = full
    for _ in range(3):
        part = rest.astype(jnp.bfloat16)
        parts.append(part)
        rest = rest - part.astype(np.float32)
    return np.concatenate(parts, axis=1)


def layer_kernel(
    F,
    B,
    D,
    tok_ref,
    cot_ref,
    doc_ref,
    norms_ref,
    hn_ref,
    table_ref,
    wq_ref,
    wk_ref,
    wv_ref,
    wo_ref,
    wg_ref,
    wu_ref,
    wd_ref,
    gqkv_out,
    ggu_out,
    go_out,
    gd_out,
    vec_out,
    mixed_out,
    dtok_out,
    zr_o,
    zr_d,
    ag1,
    ag2,
    ag3,
    ag4,
    st,
    sr,
    rr,
    wqkv,
    wgu,
    wo,
    wd,
    qkpre,
    rot,
    probs,
    att,
    actd,
    hidden,
    dhid,
    normsb,
    zr_gu,
    zr_qkv,
    fq,
    fgu,
    fo,
    fd,
    vz,
    vp,
    ghead,
    ag_s,
    ag_r,
    sib_s,
    sib_r,
    rem_s,
    rem_r,
    w_s,
    w_r,
    nz_s,
    nz_r,
    loc_s,
    zg_s,
    zg_r,
    fin_s,
    fin_r,
    vz_s,
    vz_r,
    vp_s,
    vp_r,
):
    Dz = D // F
    QT = wo.shape[0]
    FT = wd.shape[0]
    GPF = T // F
    half = B // 2
    r = lax.axis_index("rep")
    f = lax.axis_index("fsdp")
    t = lax.rem(r, T)
    base = r - t
    core = lax.rem(t, 2)
    chip = t // 2
    b1 = lax.rem(chip, 2)
    b2 = chip // 2

    def flip(k):
        x = core + (k % 2) * (1 - 2 * core)
        y = b1 + ((k // 2) % 2) * (1 - 2 * b1)
        z = b2 + (k // 4) * (1 - 2 * b2)
        return x + 2 * y + 4 * z

    def unit(rank):
        return lax.rem(rank, 2) * (T // 2) + rank // 2

    g = unit(t)
    fg = g // GPF
    grow = lax.rem(g, GPF)
    sib, xn, yn, dg = base + flip(1), base + flip(2), base + flip(4), base + flip(6)

    def remote(src, dst, ssem, rsem, rep, fs):
        return pltpu.make_async_remote_copy(
            src_ref=src,
            dst_ref=dst,
            send_sem=ssem,
            recv_sem=rsem,
            device_id={"rep": rep, "fsdp": fs},
            device_id_type=MESH,
        )

    def wait_recv(dst, rsem):
        remote(dst, dst, rsem, rsem, sib, f).wait_recv()

    def wait_send(src, ssem):
        remote(src, src, ssem, ssem, sib, f).wait_send()

    barrier = pltpu.get_barrier_semaphore()
    for k in range(1, T):
        pl.semaphore_signal(
            barrier, inc=1, device_id={"rep": base + flip(k), "fsdp": f}, device_id_type=MESH
        )
    for d in range(1, F):
        pl.semaphore_signal(
            barrier, inc=1, device_id={"rep": r, "fsdp": lax.rem(f + d, F)}, device_id_type=MESH
        )

    def own(n):
        return pl.ds(pl.multiple_of(f * n, n), n)

    gq = pl.ds(pl.multiple_of(g * QT, QT), QT)
    gk = pl.ds(pl.multiple_of(g * HEAD, HEAD), HEAD)
    gf = pl.ds(pl.multiple_of(g * FT, HEAD), FT)
    loads = [
        pltpu.make_async_copy(wq_ref.at[:, gq], wqkv.at[own(Dz), pl.ds(0, QT)], loc_s.at[0]),
        pltpu.make_async_copy(wk_ref.at[:, gk], wqkv.at[own(Dz), pl.ds(QT, HEAD)], loc_s.at[1]),
        pltpu.make_async_copy(
            wv_ref.at[:, gk], wqkv.at[own(Dz), pl.ds(QT + HEAD, HEAD)], loc_s.at[2]
        ),
        pltpu.make_async_copy(wg_ref.at[:, gf], wgu.at[own(Dz), pl.ds(0, FT)], loc_s.at[3]),
        pltpu.make_async_copy(wu_ref.at[:, gf], wgu.at[own(Dz), pl.ds(FT, FT)], loc_s.at[4]),
    ]
    for c in loads:
        c.start()

    def row_load(src, dst, rows, sem):
        return pltpu.make_async_copy(
            src.at[pl.ds(pl.multiple_of(grow * rows, rows), rows), :], dst, sem
        )

    @pl.when(f == fg)
    def _():
        row_load(wo_ref, wo, QT, loc_s.at[5]).start()
        row_load(wd_ref, wd, FT, loc_s.at[6]).start()

    normsb[f] = norms_ref[...]
    pl.semaphore_wait(barrier, T - 1 + F - 1)

    def others(fn):
        for d in range(1, F):
            fn(d, lax.rem(f + d, F), lax.rem(f + F - d, F))

    def norms_send(d, to, _):
        remote(normsb.at[f], normsb.at[f], nz_s.at[d], nz_r.at[d], r, to).start()

    others(norms_send)

    def line_copy(item, buf, rows, s, up, m, to):
        part = buf.at[pl.ds(pl.multiple_of(s * rows, rows), rows), :]
        return remote(part, part, w_s.at[item, up, m], w_r.at[item, up, m], r, to)

    def cols_start(item, buf, rows):
        @pl.when(f < F - 1)
        def _():
            line_copy(item, buf, rows, f, 1, 1, f + 1).start()

        @pl.when(f > 0)
        def _():
            line_copy(item, buf, rows, f, 0, 1, f - 1).start()

    def cols_step(item, buf, rows, m):
        @pl.when(f >= m)
        def _():
            line_copy(item, buf, rows, f - m, 1, m, r * 0).wait_recv()
            if m + 1 < F:

                @pl.when(f < F - 1)
                def _():
                    line_copy(item, buf, rows, f - m, 1, m + 1, f + 1).start()

        @pl.when(f + m < F)
        def _():
            line_copy(item, buf, rows, f + m, 0, m, r * 0).wait_recv()
            if m + 1 < F:

                @pl.when(f > 0)
                def _():
                    line_copy(item, buf, rows, f + m, 0, m + 1, f - 1).start()

    def cols_done(item, buf, rows):
        for m in range(1, F):

            @pl.when((f < F - 1) & (f >= m - 1))
            def _():
                line_copy(item, buf, rows, f, 1, m, r * 0).wait_send()

            @pl.when((f > 0) & (f + m - 1 < F))
            def _():
                line_copy(item, buf, rows, f, 0, m, r * 0).wait_send()

    def row_copy(item, buf, up, to):
        return remote(buf, buf, w_s.at[item, up, 0], w_r.at[item, up, 0], r, to)

    def rows_start(item, buf):
        @pl.when((f == fg) & (f < F - 1))
        def _():
            row_copy(item, buf, 1, f + 1).start()

        @pl.when((f == fg) & (f > 0))
        def _():
            row_copy(item, buf, 0, f - 1).start()

    def rows_step(item, buf):
        @pl.when(f > fg)
        def _():
            row_copy(item, buf, 1, r * 0).wait_recv()

            @pl.when(f < F - 1)
            def _():
                row_copy(item, buf, 1, f + 1).start()

        @pl.when(f < fg)
        def _():
            row_copy(item, buf, 0, r * 0).wait_recv()

            @pl.when(f > 0)
            def _():
                row_copy(item, buf, 0, f - 1).start()

    def rows_done(item, buf):
        @pl.when((f >= fg) & (f < F - 1))
        def _():
            row_copy(item, buf, 1, r * 0).wait_send()

        @pl.when((f <= fg) & (f > 0))
        def _():
            row_copy(item, buf, 0, r * 0).wait_send()

    for c in loads[:3]:
        c.wait()
    cols_start(0, wqkv, Dz)

    @pl.when(f == fg)
    def _():
        row_load(wo_ref, wo, QT, loc_s.at[5]).wait()
        row_load(wd_ref, wd, FT, loc_s.at[6]).wait()

    rows_start(1, wo)

    def ag_start(buf, a):
        remote(buf.at[0], buf.at[2], ag_s.at[a, 2], ag_r.at[a, 2], xn, f).start()
        remote(buf.at[0], buf.at[4], ag_s.at[a, 4], ag_r.at[a, 4], yn, f).start()
        remote(buf.at[0], buf.at[1], ag_s.at[a, 1], ag_r.at[a, 1], sib, f).start()

    def ag_cut(buf, slot, lower):
        rows = buf.shape[1]
        return buf.at[slot, pl.ds(half, rows - half), :] if lower else buf.at[slot, pl.ds(0, half), :]

    def ag_pass(buf, a, slot):
        remote(
            buf.at[slot], buf.at[slot + 1], ag_s.at[a, slot + 1], ag_r.at[a, slot + 1], sib, f
        ).start()

    def ag_step(buf, a, i):
        @pl.when(i == 1)
        def _():
            wait_recv(buf.at[1], ag_r.at[a, 1])

        @pl.when(i == 2)
        def _():
            wait_recv(buf.at[2], ag_r.at[a, 2])
            remote(
                ag_cut(buf, 2, 0), ag_cut(buf, 6, 0), ag_s.at[a, 6], ag_r.at[a, 6], yn, f
            ).start()
            ag_pass(buf, a, 2)

        @pl.when(i == 3)
        def _():
            wait_recv(buf.at[4], ag_r.at[a, 4])
            remote(
                ag_cut(buf, 4, 1), ag_cut(buf, 6, 1), ag_s.at[a, 8], ag_r.at[a, 8], xn, f
            ).start()
            ag_pass(buf, a, 4)
            wait_recv(buf.at[3], ag_r.at[a, 3])

        @pl.when(i == 5)
        def _():
            wait_recv(buf.at[5], ag_r.at[a, 5])

        @pl.when(i == 6)
        def _():
            wait_recv(ag_cut(buf, 6, 0), ag_r.at[a, 6])
            wait_recv(ag_cut(buf, 6, 1), ag_r.at[a, 8])
            ag_pass(buf, a, 6)

        @pl.when(i == 7)
        def _():
            wait_recv(buf.at[7], ag_r.at[a, 7])

    def ag_done(buf, a):
        for k in (1, 2, 3, 4, 5, 7):
            wait_send(buf.at[0], ag_s.at[a, k])
        wait_send(ag_cut(buf, 6, 0), ag_s.at[a, 6])
        wait_send(ag_cut(buf, 6, 1), ag_s.at[a, 8])

    def rs_step(buf, q, s, i):
        @pl.when(lax.rem(i, 2) == 1)
        def _():
            remote(
                buf.at[i], sr.at[s, i // 2], sib_s.at[q, i // 2], sib_r.at[q, i // 2], sib, f
            ).start()

        @pl.when((lax.rem(i, 2) == 0) & (i >= 4))
        def _():
            rs_send(buf, q, s, i // 2 - 1)

    def rs_send(buf, q, s, p):
        wait_recv(sr.at[s, p], sib_r.at[q, p])
        buf[2 * p] = (buf[2 * p].astype(F32) + sr[s, p].astype(F32)).astype(BF)
        low = lax.rem(p, 2)
        high = p // 2
        to = r + low * (2 - 4 * b1) + high * (4 - 8 * b2)
        remote(buf.at[2 * p], rr.at[s, p], rem_s.at[q, p], rem_r.at[q, p], to, f).start()

    def rs_total(buf, q, s):
        wait_recv(sr.at[s, 0], sib_r.at[q, 0])
        total = buf[0].astype(F32) + sr[s, 0].astype(F32)
        for p in range(1, 4):
            wait_recv(rr.at[s, p], rem_r.at[q, p])
            total = total + rr[s, p].astype(F32)
        return total

    def rs_done(buf, q):
        for p in range(4):
            wait_send(buf.at[2 * p + 1], sib_s.at[q, p])
            if p > 0:
                wait_send(buf.at[2 * p], rem_s.at[q, p])

    row_ids = lax.broadcasted_iota(jnp.int32, (B, 1), 0)
    lanes_b = lax.broadcasted_iota(jnp.int32, (1, D), 1)
    end = doc_ref[0, 0]
    meta = jnp.where(lanes_b == 0, end, 0)
    slots = doc_ref.shape[1]
    for i in range(1, slots):
        end = end + doc_ref[0, i]
        meta = meta + jnp.where(lanes_b == i, end, 0)
    live = row_ids < end
    tokens = tok_ref[...].astype(F32)
    first_scale = lax.rsqrt(jnp.mean(tokens * tokens, axis=1, keepdims=True) + EPS)

    def norms_wait(d, _, fs):
        wait_recv(normsb.at[fs], nz_r.at[d])

    others(norms_wait)
    gain_one = jnp.concatenate([normsb[j, 0:1, :] for j in range(F)], axis=1)
    gain_two = jnp.concatenate([normsb[j, 1:2, :] for j in range(F)], axis=1)
    ag1[0, 0:B, :] = (tokens * first_scale * gain_one).astype(BF)
    ag1[0, B : B + 16, :] = jnp.broadcast_to(meta.astype(F32), (16, D)).astype(BF)
    ag_start(ag1, 0)
    ag3[0] = jnp.where(live, cot_ref[...].astype(F32), 0.0).astype(BF)
    for m in range(1, F):
        cols_step(0, wqkv, Dz, m)
    rows_step(1, wo)
    for c in loads[3:]:
        c.wait()
    cols_start(2, wgu, Dz)
    rows_start(3, wd)

    gain_q = hn_ref[0:1, :].astype(F32)
    gain_k = hn_ref[1:2, :].astype(F32)
    score_scale = HEAD ** (-0.5)

    def block_layout(i):
        ends = ag1[i, B : B + 16, :][0:1, 0:HEAD].astype(F32)
        rows = lax.broadcasted_iota(jnp.int32, (B, 1), 0).astype(F32)
        cols = lax.broadcasted_iota(jnp.int32, (1, B), 1).astype(F32)
        seg_row = jnp.zeros((B, 1), F32)
        seg_col = jnp.zeros((1, B), F32)
        start = jnp.zeros((B, 1), F32)
        for n in range(slots):
            e = ends[:, n : n + 1]
            past = rows >= e
            seg_row = seg_row + past.astype(F32)
            seg_col = seg_col + (cols >= e).astype(F32)
            start = jnp.maximum(start, jnp.where(past, e, 0.0))
        alive = rows < ends[:, slots - 1 : slots]
        position = rows - jnp.where(alive, start, 0.0)
        return rows, cols, seg_row, seg_col, alive, position

    def rope_rows(position, cols):
        pick = (cols == position).astype(F32).astype(BF)
        table = mm(pick, table_ref[...])
        w = 2 * HEAD
        table = table[:, 0:w] + table[:, w : 2 * w] + table[:, 2 * w : 3 * w]
        return table[:, 0:HEAD], table[:, HEAD:w]

    def rotate(x, cos, sin):
        return x * cos + pltpu.roll(x, HEAD // 2, 1) * sin

    def head_scale(x):
        return lax.rsqrt(jnp.mean(x * x, axis=1, keepdims=True) + EPS)

    def forward_block(i, carry):
        ag_step(ag1, 0, i)

        @pl.when(i == 2)
        def _():
            ag_start(ag3, 2)

        rows, cols, seg_row, seg_col, alive, position = block_layout(i)
        cos, sin = rope_rows(position, cols)
        pre = mm(ag1[i, 0:B, :], wqkv[...])
        qkpre[i] = pre[:, 0 : QT + HEAD]
        parts = []
        for n in range(3):
            x = pre[:, n * HEAD : (n + 1) * HEAD]
            x = x * head_scale(x) * (gain_q if n < 2 else gain_k)
            parts.append(rotate(x, cos, sin).astype(BF))
        v = pre[:, QT + HEAD : QT + 2 * HEAD].astype(BF)
        for n in range(3):
            rot[i, :, n * HEAD : (n + 1) * HEAD] = parts[n]
        rot[i, :, 3 * HEAD : 4 * HEAD] = v
        allowed = ((seg_row == seg_col) & (cols <= rows) & alive) | (cols == rows)
        for n in range(2):
            scores = mm_nt(parts[n], parts[2]) * score_scale
            scores = jnp.where(allowed, scores, NEG_FILL)
            expd = jnp.exp(scores - jnp.max(scores, axis=1, keepdims=True))
            prob = (expd / jnp.sum(expd, axis=1, keepdims=True)).astype(BF)
            probs[i, n * B : (n + 1) * B, :] = prob
            att[i, :, n * HEAD : (n + 1) * HEAD] = mm(prob, v).astype(BF)
        st[i] = mm(att[i], wo[...]).astype(BF)
        rs_step(st, 0, 0, i)
        return carry

    lax.fori_loop(0, T, forward_block, 0)
    rs_send(st, 0, 0, 3)
    cols_step(2, wgu, Dz, 1)
    for i in range(1, T):
        ag_step(ag3, 2, i)
    for m in range(2, F):
        cols_step(2, wgu, Dz, m)
    rows_step(3, wd)
    hid = tokens + rs_total(st, 0, 0)
    rs_done(st, 0)
    hidden[...] = hid
    second_scale = lax.rsqrt(jnp.mean(hid * hid, axis=1, keepdims=True) + EPS)
    ag2[0] = (hid * second_scale * gain_two).astype(BF)
    ag_start(ag2, 1)

    def ffn_block(i, carry):
        ag_step(ag2, 1, i)
        up_gate = mm(ag2[i], wgu[...])
        gate, up = up_gate[:, 0:FT], up_gate[:, FT : 2 * FT]
        sig = 1.0 / (1.0 + jnp.exp(-gate))
        silu = gate * sig
        actd[i, :, 0:FT] = (silu * up).astype(BF)
        d_act = mm_nt(ag3[i], wd[...])
        actd[i, :, FT : 2 * FT] = (d_act * up * sig * (1.0 + gate * (1.0 - sig))).astype(BF)
        actd[i, :, 2 * FT : 3 * FT] = (d_act * silu).astype(BF)
        st[i] = mm_nt(actd[i, :, FT : 3 * FT], wgu[...]).astype(BF)
        rs_step(st, 1, 1, i)
        return carry

    lax.fori_loop(0, T, ffn_block, 0)
    rs_send(st, 1, 1, 3)
    cols_done(2, wgu, Dz)

    step = 256

    def grad_gu(m, carry):
        at = pl.ds(pl.multiple_of(m * step, step), step)
        total = mm_tn(ag2[0, :, at], actd[0, :, FT : 3 * FT])
        for k in range(1, T):
            total = total + mm_tn(ag2[k, :, at], actd[k, :, FT : 3 * FT])
        wgu[at, :] = total.astype(BF)
        return carry

    lax.fori_loop(0, D // step, grad_gu, 0)

    def scatter(item, buf, slots_ref):
        def send(d, to, _):
            remote(
                buf.at[pl.ds(pl.multiple_of(to * Dz, Dz), Dz), :],
                slots_ref.at[f],
                zg_s.at[item, d],
                zg_r.at[item, d],
                r,
                to,
            ).start()

        others(send)

    def scatter_total(item, buf, slots_ref, dst):
        total = buf[own(Dz), :].astype(F32)

        def recv(d, to, fs):
            wait_recv(slots_ref.at[fs], zg_r.at[item, d])

        others(recv)
        for d in range(1, F):
            total = total + slots_ref[lax.rem(f + d, F)].astype(F32)
        dst[...] = total.astype(BF)

    def scatter_done(item, buf):
        for d in range(1, F):
            wait_send(buf.at[own(Dz), :], zg_s.at[item, d])

    scatter(0, wgu, zr_gu)
    d_out = jnp.where(live, cot_ref[...].astype(F32), 0.0)
    pre_two = rs_total(st, 1, 1)
    rs_done(st, 1)
    hid = hidden[...]
    second_scale = lax.rsqrt(jnp.mean(hid * hid, axis=1, keepdims=True) + EPS)
    second_hat = hid * second_scale
    grad_two = jnp.sum(pre_two * second_hat, axis=0, keepdims=True)
    dn_two = pre_two * gain_two
    d_hid = d_out + second_scale * (
        dn_two - second_hat * jnp.mean(dn_two * second_hat, axis=1, keepdims=True)
    )
    dhid[...] = d_hid
    ag4[0] = d_hid.astype(BF)
    ag_start(ag4, 3)

    ag_done(ag2, 1)

    def down_block(i, carry):
        ag2[i] = mm(actd[i, :, 0:FT], wd[...]).astype(BF)

        @pl.when(lax.rem(i, 2) == 1)
        def _():
            remote(
                ag2.at[i], sr.at[0, i // 2], sib_s.at[2, i // 2], sib_r.at[2, i // 2], sib, f
            ).start()

        return carry

    lax.fori_loop(0, T, down_block, 0)
    rows_done(3, wd)

    def grad_down(m, carry):
        at = pl.ds(pl.multiple_of(m * step, step), step)
        total = mm_tn(actd[0, :, 0:FT], ag3[0, :, at])
        for k in range(1, T):
            total = total + mm_tn(actd[k, :, 0:FT], ag3[k, :, at])
        wd[:, at] = total.astype(BF)
        return carry

    lax.fori_loop(0, D // step, grad_down, 0)

    def row_send(item, buf, slots_ref):
        @pl.when(f != fg)
        def _():
            remote(buf, slots_ref.at[f], zg_s.at[item, 0], zg_r.at[item, f], r, fg).start()

    row_send(1, wd, zr_d)
    ag_done(ag3, 2)
    ghead[...] = jnp.zeros_like(ghead)

    def backward_block(i, carry):
        ag_step(ag4, 3, i)
        rows, cols, _, _, _, position = block_layout(i)
        cos, sin = rope_rows(position, cols)
        d_att = mm_nt(ag4[i], wo[...]).astype(BF)
        k_rot = rot[i, :, QT : QT + HEAD]
        v = rot[i, :, QT + HEAD : QT + 2 * HEAD]
        d_v = jnp.zeros((B, HEAD), F32)
        d_k = jnp.zeros((B, HEAD), F32)
        d_pre = []
        sums = []

        def norm_back(grad, n, gain):
            x = qkpre[i, :, n * HEAD : (n + 1) * HEAD]
            scale = head_scale(x)
            hat = x * scale
            dn = rotate(grad, cos, -sin)
            total = jnp.sum(dn * hat, axis=0, keepdims=True)
            dn = dn * gain
            back = scale * (dn - hat * jnp.mean(dn * hat, axis=1, keepdims=True))
            return back.astype(BF), total

        for n in range(2):
            prob = probs[i, n * B : (n + 1) * B, :]
            q_rot = rot[i, :, n * HEAD : (n + 1) * HEAD]
            d_head = d_att[:, n * HEAD : (n + 1) * HEAD]
            d_prob = mm_nt(d_head, v)
            p32 = prob.astype(F32)
            center = jnp.sum(p32 * d_prob, axis=1, keepdims=True)
            d_score = (p32 * (d_prob - center)).astype(BF)
            d_v = d_v + mm_tn(prob, d_head)
            d_k = d_k + mm_tn(d_score, q_rot)
            back, total = norm_back(mm(d_score, k_rot) * score_scale, n, gain_q)
            d_pre.append(back)
            sums.append(total)
        back, total = norm_back(d_k * score_scale, 2, gain_k)
        d_pre.append(back)
        d_pre.append(d_v.astype(BF))
        ghead[0:1, :] += sums[0] + sums[1]
        ghead[1:2, :] += total
        for n in range(4):
            rot[i, :, n * HEAD : (n + 1) * HEAD] = d_pre[n]
        ag3[i] = mm_nt(rot[i], wqkv[...]).astype(BF)
        rs_step(ag3, 3, 1, i)
        return carry

    lax.fori_loop(0, T, backward_block, 0)
    rs_send(ag3, 3, 1, 3)
    for p in range(1, 4):
        rs_send(ag2, 2, 0, p)
    cols_done(0, wqkv, Dz)
    rows_done(1, wo)

    def grad_qkv(m, carry):
        at = pl.ds(pl.multiple_of(m * step, step), step)
        total = mm_tn(ag1[0, 0:B, at], rot[0])
        for k in range(1, T):
            total = total + mm_tn(ag1[k, 0:B, at], rot[k])
        wqkv[at, :] = total.astype(BF)
        return carry

    lax.fori_loop(0, D // step, grad_qkv, 0)
    scatter(3, wqkv, zr_qkv)

    def grad_out(m, carry):
        at = pl.ds(pl.multiple_of(m * step, step), step)
        total = mm_tn(att[0], ag4[0, :, at])
        for k in range(1, T):
            total = total + mm_tn(att[k], ag4[k, :, at])
        wo[:, at] = total.astype(BF)
        return carry

    lax.fori_loop(0, D // step, grad_out, 0)
    row_send(2, wo, zr_o)

    def piece_at(item, out, rows, rank):
        u = unit(rank)
        if item in (0, 3):
            return out.at[u]
        return out.at[pl.ds(pl.multiple_of(lax.rem(u, GPF) * rows, rows), rows), :]

    def fin_start(item, src, out, rows):
        dst = piece_at(item, out, rows, t)
        for k, to in ((2, xn), (4, yn), (6, dg), (1, sib)):
            remote(src, dst, fin_s.at[item, k], fin_r.at[item, k], to, f).start()
        pltpu.make_async_copy(src, dst, fin_s.at[item, 0]).start()

    def fin_wait(item, src, out, rows):
        dst = piece_at(item, out, rows, t)
        for k in (1, 2, 4, 6):
            wait_send(src, fin_s.at[item, k])
        pltpu.make_async_copy(src, dst, fin_s.at[item, 0]).wait()

    def has(item, rank):
        return unit(rank) // GPF == f

    def fin_pass(item, out, rows, k):
        rank = flip(k)
        dst = piece_at(item, out, rows, rank)

        def go():
            wait_recv(dst, fin_r.at[item, k])
            remote(dst, dst, fin_s.at[item, k + 1], fin_r.at[item, k + 1], sib, f).start()

        if item in (0, 3):
            go()
        else:
            pl.when(has(item, rank))(go)

    def fin_end(item, out, rows):
        for k in (1, 3, 5, 7):
            rank = flip(k)
            dst = piece_at(item, out, rows, rank)

            def go():
                wait_recv(dst, fin_r.at[item, k])

            def sent():
                wait_send(dst, fin_s.at[item, k])

            if item in (0, 3):
                go()
                if k > 1:
                    sent()
            else:
                pl.when(has(item, rank))(go)
                if k > 1:
                    pl.when(has(item, flip(k - 1)))(sent)

    scatter_total(0, wgu, zr_gu, fgu)
    fin_start(0, fgu, ggu_out, Dz)

    def row_total(item, buf, slots_ref, dst, rows):
        for d in range(1, F):
            fs = lax.rem(f + d, F)
            wait_recv(slots_ref.at[fs], zg_r.at[item, fs])
        chunk = 128
        for c in range(rows // chunk):
            copies = []
            for d in range(1, F):
                fs = lax.rem(f + d, F)
                copies.append(
                    pltpu.make_async_copy(
                        slots_ref.at[fs, pl.ds(c * chunk, chunk), :],
                        st.at[d, pl.ds(0, chunk), :],
                        loc_s.at[d],
                    )
                )
            for x in copies:
                x.start()
            for x in copies:
                x.wait()
            total = buf[c * chunk : (c + 1) * chunk, :].astype(F32)
            for d in range(1, F):
                total = total + st[d, 0:chunk, :].astype(F32)
            dst[c * chunk : (c + 1) * chunk, :] = total.astype(BF)

    @pl.when(f == fg)
    def _():
        row_total(1, wd, zr_d, fd, FT)
        fin_start(1, fd, gd_out, FT)

    pre_one = rs_total(ag3, 3, 1)
    tokens = tok_ref[...].astype(F32)
    first_scale = lax.rsqrt(jnp.mean(tokens * tokens, axis=1, keepdims=True) + EPS)
    first_hat = tokens * first_scale
    grad_one = jnp.sum(pre_one * first_hat, axis=0, keepdims=True)
    dn_one = pre_one * gain_one
    dtok_out[...] = (
        dhid[...]
        + first_scale
        * (dn_one - first_hat * jnp.mean(dn_one * first_hat, axis=1, keepdims=True))
    ).astype(BF)
    vz[f, 0:1, :] = grad_one
    vz[f, 1:2, :] = grad_two
    vz[f, 2:3, :] = jnp.concatenate(
        [ghead[0:1, :], ghead[1:2, :], jnp.zeros((1, D - 2 * HEAD), F32)], axis=1
    )
    vz[f, 3:8, :] = jnp.zeros((5, D), F32)

    def vec_send(d, to, _):
        remote(vz.at[f], vz.at[f], vz_s.at[d], vz_r.at[d], r, to).start()

    others(vec_send)
    out = hidden[...] + rs_total(ag2, 2, 0)
    mixed_out[...] = jnp.where(live, out, 0.0).astype(BF)

    def vec_recv(d, to, fs):
        wait_recv(vz.at[fs], vz_r.at[d])

    others(vec_recv)
    total = vz[0]
    for j in range(1, F):
        total = total + vz[j]
    vp[t] = total
    for k in range(1, T):
        remote(vp.at[t], vp.at[t], vp_s.at[k], vp_r.at[k], base + flip(k), f).start()

    scatter_total(3, wqkv, zr_qkv, fq)
    fin_start(3, fq, gqkv_out, Dz)

    @pl.when(f == fg)
    def _():
        row_total(2, wo, zr_o, fo, QT)
        fin_start(2, fo, go_out, QT)

    for k in range(1, T):
        wait_recv(vp.at[flip(k)], vp_r.at[k])
    total = vp[0]
    for j in range(1, T):
        total = total + vp[j]
    mine = jnp.zeros((8, Dz), F32)
    for j in range(F):
        mine = mine + jnp.where(f == j, total[:, j * Dz : (j + 1) * Dz], 0.0)
    vec_out[:, 0:Dz] = mine
    vec_out[:, Dz : Dz + 2 * HEAD] = total[:, 0 : 2 * HEAD]

    items = ((0, fgu, ggu_out, Dz), (1, fd, gd_out, FT), (3, fq, gqkv_out, Dz), (2, fo, go_out, QT))
    for k in (2, 4, 6):
        for item, _, dst, rows in items:
            fin_pass(item, dst, rows, k)
    for item, src, dst, rows in items:
        fin_end(item, dst, rows)
        if item in (0, 3):
            fin_wait(item, src, dst, rows)
        else:

            @pl.when(f == fg)
            def _():
                fin_wait(item, src, dst, rows)

    ag_done(ag1, 0)
    ag_done(ag4, 3)
    rs_done(ag2, 2)
    rs_done(ag3, 3)
    scatter_done(0, wgu)
    scatter_done(3, wqkv)

    @pl.when(f != fg)
    def _():
        wait_send(wd, zg_s.at[1, 0])
        wait_send(wo, zg_s.at[2, 0])

    for d in range(1, F):
        wait_send(normsb.at[0], nz_s.at[d])
        wait_send(vz.at[0], vz_s.at[d])
    for k in range(1, T):
        wait_send(vp.at[0], vp_s.at[k])


def finish_kernel(scale, gqkv, ggu, go, gd, oq, ok, ov, og, ou, oo, od):
    x = gqkv[0].astype(F32) * scale
    w = oq.shape[1]
    oq[...] = x[:, 0:w]
    ok[...] = x[:, w : w + HEAD]
    ov[...] = x[:, w + HEAD : w + 2 * HEAD]
    x = ggu[0].astype(F32) * scale
    w = og.shape[1]
    og[...] = x[:, 0:w]
    ou[...] = x[:, w : 2 * w]
    oo[...] = go[...].astype(F32) * scale
    od[...] = gd[...].astype(F32) * scale


def per_device(
    F,
    G,
    tokens,
    doc_lengths,
    attn_norm,
    w_query,
    key_matrix,
    value_matrix,
    head_norms,
    w_out,
    ffn_norm,
    w_gate,
    w_up,
    w_down,
    cotangent,
):
    B, D = tokens.shape
    Dz = D // F
    QW, KW, FF = w_query.shape[1], key_matrix.shape[1], w_gate.shape[1]
    QT, FT = QW // T, FF // T
    QZ, FZ = w_out.shape[0], w_down.shape[0]
    norms = jnp.zeros((8, Dz), F32)
    norms = norms.at[0].set(attn_norm.astype(F32)).at[1].set(ffn_norm.astype(F32))
    table = jnp.asarray(rope_table(B))
    vmem = pl.BlockSpec(memory_space=pltpu.VMEM)
    hbm = pl.BlockSpec(memory_space=pl.ANY)
    dma = pltpu.SemaphoreType.DMA
    sds = jax.ShapeDtypeStruct
    outs = pl.pallas_call(
        functools.partial(layer_kernel, F, B, D),
        out_shape=(
            sds((T, Dz, QT + 2 * HEAD), BF),
            sds((T, Dz, 2 * FT), BF),
            sds((QZ, D), BF),
            sds((FZ, D), BF),
            sds((8, Dz + 2 * HEAD), F32),
            sds((B, D), BF),
            sds((B, D), BF),
            sds((F, QT, D), BF),
            sds((F, FT, D), BF),
        ),
        in_specs=[vmem, vmem, pl.BlockSpec(memory_space=pltpu.SMEM), vmem, vmem, vmem] + [hbm] * 7,
        out_specs=(hbm, hbm, hbm, hbm, vmem, vmem, vmem, hbm, hbm),
        scratch_shapes=[
            pltpu.VMEM((T, B + 16, D), BF),
            pltpu.VMEM((T, B, D), BF),
            pltpu.VMEM((T, B, D), BF),
            pltpu.VMEM((T, B, D), BF),
            pltpu.VMEM((T, B, D), BF),
            pltpu.VMEM((2, 4, B, D), BF),
            pltpu.VMEM((2, 4, B, D), BF),
            pltpu.VMEM((D, QT + 2 * HEAD), BF),
            pltpu.VMEM((D, 2 * FT), BF),
            pltpu.VMEM((QT, D), BF),
            pltpu.VMEM((FT, D), BF),
            pltpu.VMEM((T, B, QT + HEAD), F32),
            pltpu.VMEM((T, B, QT + 2 * HEAD), BF),
            pltpu.VMEM((T, 2 * B, B), BF),
            pltpu.VMEM((T, B, QT), BF),
            pltpu.VMEM((T, B, 3 * FT), BF),
            pltpu.VMEM((B, D), F32),
            pltpu.VMEM((B, D), F32),
            pltpu.VMEM((F, 8, Dz), F32),
            pltpu.VMEM((F, Dz, 2 * FT), BF),
            pltpu.VMEM((F, Dz, QT + 2 * HEAD), BF),
            pltpu.VMEM((Dz, QT + 2 * HEAD), BF),
            pltpu.VMEM((Dz, 2 * FT), BF),
            pltpu.VMEM((QT, D), BF),
            pltpu.VMEM((FT, D), BF),
            pltpu.VMEM((F, 8, D), F32),
            pltpu.VMEM((T, 8, D), F32),
            pltpu.VMEM((8, HEAD), F32),
            dma((4, 9)),
            dma((4, 9)),
            dma((4, 4)),
            dma((4, 4)),
            dma((4, 4)),
            dma((4, 4)),
            dma((4, 2, F)),
            dma((4, 2, F)),
            dma((F,)),
            dma((F,)),
            dma((8,)),
            dma((4, F)),
            dma((4, F)),
            dma((4, T)),
            dma((4, T)),
            dma((F,)),
            dma((F,)),
            dma((T,)),
            dma((T,)),
        ],
        compiler_params=pltpu.CompilerParams(
            collective_id=0, has_side_effects=True, vmem_limit_bytes=62 * 2**20
        ),
    )(
        tokens,
        cotangent,
        doc_lengths,
        norms,
        head_norms,
        table,
        w_query,
        key_matrix,
        value_matrix,
        w_out,
        w_gate,
        w_up,
        w_down,
    )
    gqkv, ggu, go, gd, vec, mixed, d_tokens = outs[:7]
    if G > 1:
        groups = [[t + T * n for n in range(G)] for t in range(T)]
        gqkv, ggu, go, gd = (
            lax.psum(x, "rep", axis_index_groups=groups) for x in (gqkv, ggu, go, gd)
        )
        vec = lax.psum(vec, "rep", axis_index_groups=groups)
    scale = 1.0 / math.sqrt(B * T * G * F)

    def order(u):
        return u

    qb, fb = QZ // T, FZ // T
    oq, ok, ov, og, ou, oo, od = pl.pallas_call(
        functools.partial(finish_kernel, scale),
        grid=(T,),
        out_shape=(
            sds((Dz, QW), F32),
            sds((Dz, KW), F32),
            sds((Dz, KW), F32),
            sds((Dz, FF), F32),
            sds((Dz, FF), F32),
            sds((QZ, D), F32),
            sds((FZ, D), F32),
        ),
        in_specs=[
            pl.BlockSpec((1, Dz, QT + 2 * HEAD), lambda u: (u, 0, 0)),
            pl.BlockSpec((1, Dz, 2 * FT), lambda u: (u, 0, 0)),
            pl.BlockSpec((qb, D), lambda u: (u, 0)),
            pl.BlockSpec((fb, D), lambda u: (u, 0)),
        ],
        out_specs=(
            pl.BlockSpec((Dz, QT), lambda u: (0, u)),
            pl.BlockSpec((Dz, HEAD), lambda u: (0, u)),
            pl.BlockSpec((Dz, HEAD), lambda u: (0, u)),
            pl.BlockSpec((Dz, FT), lambda u: (0, u)),
            pl.BlockSpec((Dz, FT), lambda u: (0, u)),
            pl.BlockSpec((qb, D), lambda u: (u, 0)),
            pl.BlockSpec((fb, D), lambda u: (u, 0)),
        ),
    )(gqkv, ggu, go, gd)
    vec = vec * scale
    return (
        mixed,
        d_tokens,
        vec[0, 0:Dz],
        oq,
        ok,
        ov,
        jnp.concatenate([vec[2:3, Dz : Dz + HEAD], vec[2:3, Dz + HEAD : Dz + 2 * HEAD]], axis=0),
        oo,
        vec[1, 0:Dz],
        og,
        ou,
        od,
    )


def solution(mesh):
    F = mesh.shape["fsdp"]
    G = mesh.shape["rep"] // T
    rows = P(("rep", "fsdp"), None)
    mat = P("fsdp", None)
    vec = P("fsdp")
    return jax.shard_map(
        functools.partial(per_device, F, G),
        mesh=mesh,
        in_specs=(rows, rows, vec, mat, mat, mat, P(), mat, vec, mat, mat, mat, rows),
        out_specs=(rows, rows, vec, mat, mat, mat, P(), mat, vec, mat, mat, mat),
        check_vma=False,
    )
```

```python
import functools
import math

import jax
import jax.numpy as jnp
import numpy as np
from jax import lax
from jax.experimental import pallas as pl
from jax.experimental.pallas import tpu as pltpu
from jax.sharding import PartitionSpec as P

EPS = 1e-06
ROPE_BASE = 1000000.0
NEG_FILL = -1e30
HEAD = 128
T = 8
MESH = pl.DeviceIdType.MESH
BF = jnp.bfloat16
F32 = jnp.float32


def mm(a, b):
    return lax.dot_general(a, b, (((1,), (0,)), ((), ())), preferred_element_type=F32)


def mm_nt(a, b):
    return lax.dot_general(a, b, (((1,), (1,)), ((), ())), preferred_element_type=F32)


def mm_tn(a, b):
    return lax.dot_general(a, b, (((0,), (0,)), ((), ())), preferred_element_type=F32)


def rope_table(rows):
    half = HEAD // 2
    freq = np.exp(np.arange(half, dtype=np.float64) * (-2.0 * math.log(ROPE_BASE) / HEAD))
    freq = freq.astype(np.float32)
    angle = (np.arange(rows, dtype=np.float32)[:, None] * freq[None, :]).astype(np.float64)
    cos, sin = np.cos(angle), np.sin(angle)
    full = np.concatenate([cos, cos, -sin, sin], axis=1).astype(np.float32)
    parts = []
    rest = full
    for _ in range(3):
        part = rest.astype(jnp.bfloat16)
        parts.append(part)
        rest = rest - part.astype(np.float32)
    return np.concatenate(parts, axis=1)


def layer_kernel(
    F,
    B,
    D,
    tok_ref,
    cot_ref,
    doc_ref,
    norms_ref,
    hn_ref,
    table_ref,
    wq_ref,
    wk_ref,
    wv_ref,
    wo_ref,
    wg_ref,
    wu_ref,
    wd_ref,
    gqkv_out,
    ggu_out,
    go_out,
    gd_out,
    vec_out,
    mixed_out,
    dtok_out,
    ag1,
    ag2,
    ag3,
    ag4,
    st,
    sr,
    rr,
    wqkv,
    wgu,
    wo,
    wd,
    qkpre,
    rot,
    probs,
    att,
    actd,
    hidden,
    dhid,
    normsb,
    zr_gu,
    zr_d,
    zr_o,
    zr_qkv,
    vz,
    vp,
    ghead,
    ag_s,
    ag_r,
    sib_s,
    sib_r,
    rem_s,
    rem_r,
    w_s,
    w_r,
    nz_s,
    nz_r,
    loc_s,
    zg_s,
    zg_r,
    fin_s,
    fin_r,
    vz_s,
    vz_r,
    vp_s,
    vp_r,
):
    Dz = D // F
    QT = wo.shape[0]
    FT = wd.shape[0]
    GPF = T // F
    half = B // 2
    r = lax.axis_index("rep")
    f = lax.axis_index("fsdp")
    t = lax.rem(r, T)
    base = r - t
    core = lax.rem(t, 2)
    chip = t // 2
    b1 = lax.rem(chip, 2)
    b2 = chip // 2

    def flip(k):
        x = core + (k % 2) * (1 - 2 * core)
        y = b1 + ((k // 2) % 2) * (1 - 2 * b1)
        z = b2 + (k // 4) * (1 - 2 * b2)
        return x + 2 * y + 4 * z

    def unit(rank):
        return lax.rem(rank, 2) * (T // 2) + rank // 2

    g = unit(t)
    fg = g // GPF
    grow = lax.rem(g, GPF)
    sib, xn, yn, dg = base + flip(1), base + flip(2), base + flip(4), base + flip(6)

    def remote(src, dst, ssem, rsem, rep, fs):
        return pltpu.make_async_remote_copy(
            src_ref=src,
            dst_ref=dst,
            send_sem=ssem,
            recv_sem=rsem,
            device_id={"rep": rep, "fsdp": fs},
            device_id_type=MESH,
        )

    def wait_recv(dst, rsem):
        remote(dst, dst, rsem, rsem, sib, f).wait_recv()

    def wait_send(src, ssem):
        remote(src, src, ssem, ssem, sib, f).wait_send()

    barrier = pltpu.get_barrier_semaphore()
    for k in range(1, T):
        pl.semaphore_signal(
            barrier, inc=1, device_id={"rep": base + flip(k), "fsdp": f}, device_id_type=MESH
        )
    for d in range(1, F):
        pl.semaphore_signal(
            barrier, inc=1, device_id={"rep": r, "fsdp": lax.rem(f + d, F)}, device_id_type=MESH
        )

    def own(n):
        return pl.ds(pl.multiple_of(f * n, n), n)

    gq = pl.ds(pl.multiple_of(g * QT, QT), QT)
    gk = pl.ds(pl.multiple_of(g * HEAD, HEAD), HEAD)
    gf = pl.ds(pl.multiple_of(g * FT, HEAD), FT)
    loads = [
        pltpu.make_async_copy(wq_ref.at[:, gq], wqkv.at[own(Dz), pl.ds(0, QT)], loc_s.at[0]),
        pltpu.make_async_copy(wk_ref.at[:, gk], wqkv.at[own(Dz), pl.ds(QT, HEAD)], loc_s.at[1]),
        pltpu.make_async_copy(
            wv_ref.at[:, gk], wqkv.at[own(Dz), pl.ds(QT + HEAD, HEAD)], loc_s.at[2]
        ),
        pltpu.make_async_copy(wg_ref.at[:, gf], wgu.at[own(Dz), pl.ds(0, FT)], loc_s.at[3]),
        pltpu.make_async_copy(wu_ref.at[:, gf], wgu.at[own(Dz), pl.ds(FT, FT)], loc_s.at[4]),
    ]
    for c in loads:
        c.start()

    def row_load(src, dst, rows, sem):
        return pltpu.make_async_copy(
            src.at[pl.ds(pl.multiple_of(grow * rows, rows), rows), :], dst, sem
        )

    @pl.when(f == fg)
    def _():
        row_load(wo_ref, wo, QT, loc_s.at[5]).start()
        row_load(wd_ref, wd, FT, loc_s.at[6]).start()

    normsb[f] = norms_ref[...]
    pl.semaphore_wait(barrier, T - 1 + F - 1)

    def others(fn):
        for d in range(1, F):
            fn(d, lax.rem(f + d, F), lax.rem(f + F - d, F))

    def norms_send(d, to, _):
        remote(normsb.at[f], normsb.at[f], nz_s.at[d], nz_r.at[d], r, to).start()

    others(norms_send)

    def line_copy(item, buf, rows, s, up, m, to):
        part = buf.at[pl.ds(pl.multiple_of(s * rows, rows), rows), :]
        return remote(part, part, w_s.at[item, up, m], w_r.at[item, up, m], r, to)

    def cols_start(item, buf, rows):
        @pl.when(f < F - 1)
        def _():
            line_copy(item, buf, rows, f, 1, 1, f + 1).start()

        @pl.when(f > 0)
        def _():
            line_copy(item, buf, rows, f, 0, 1, f - 1).start()

    def cols_step(item, buf, rows, m):
        @pl.when(f >= m)
        def _():
            line_copy(item, buf, rows, f - m, 1, m, r * 0).wait_recv()
            if m + 1 < F:

                @pl.when(f < F - 1)
                def _():
                    line_copy(item, buf, rows, f - m, 1, m + 1, f + 1).start()

        @pl.when(f + m < F)
        def _():
            line_copy(item, buf, rows, f + m, 0, m, r * 0).wait_recv()
            if m + 1 < F:

                @pl.when(f > 0)
                def _():
                    line_copy(item, buf, rows, f + m, 0, m + 1, f - 1).start()

    def cols_done(item, buf, rows):
        for m in range(1, F):

            @pl.when((f < F - 1) & (f >= m - 1))
            def _():
                line_copy(item, buf, rows, f, 1, m, r * 0).wait_send()

            @pl.when((f > 0) & (f + m - 1 < F))
            def _():
                line_copy(item, buf, rows, f, 0, m, r * 0).wait_send()

    def row_copy(item, buf, up, to):
        return remote(buf, buf, w_s.at[item, up, 0], w_r.at[item, up, 0], r, to)

    def rows_start(item, buf):
        @pl.when((f == fg) & (f < F - 1))
        def _():
            row_copy(item, buf, 1, f + 1).start()

        @pl.when((f == fg) & (f > 0))
        def _():
            row_copy(item, buf, 0, f - 1).start()

    def rows_step(item, buf, m):
        @pl.when(f - fg == m)
        def _():
            row_copy(item, buf, 1, r * 0).wait_recv()

            @pl.when(f < F - 1)
            def _():
                row_copy(item, buf, 1, f + 1).start()

        @pl.when(fg - f == m)
        def _():
            row_copy(item, buf, 0, r * 0).wait_recv()

            @pl.when(f > 0)
            def _():
                row_copy(item, buf, 0, f - 1).start()

    def rows_done(item, buf):
        @pl.when((f >= fg) & (f < F - 1))
        def _():
            row_copy(item, buf, 1, r * 0).wait_send()

        @pl.when((f <= fg) & (f > 0))
        def _():
            row_copy(item, buf, 0, r * 0).wait_send()

    for c in loads[:3]:
        c.wait()
    cols_start(0, wqkv, Dz)

    @pl.when(f == fg)
    def _():
        row_load(wo_ref, wo, QT, loc_s.at[5]).wait()
        row_load(wd_ref, wd, FT, loc_s.at[6]).wait()

    rows_start(1, wo)

    def ag_start(buf, a):
        remote(buf.at[0], buf.at[2], ag_s.at[a, 2], ag_r.at[a, 2], xn, f).start()
        remote(buf.at[0], buf.at[4], ag_s.at[a, 4], ag_r.at[a, 4], yn, f).start()
        remote(buf.at[0], buf.at[1], ag_s.at[a, 1], ag_r.at[a, 1], sib, f).start()

    def ag_cut(buf, slot, lower):
        rows = buf.shape[1]
        return buf.at[slot, pl.ds(half, rows - half), :] if lower else buf.at[slot, pl.ds(0, half), :]

    def ag_pass(buf, a, slot):
        remote(
            buf.at[slot], buf.at[slot + 1], ag_s.at[a, slot + 1], ag_r.at[a, slot + 1], sib, f
        ).start()

    def ag_step(buf, a, i):
        @pl.when(i == 1)
        def _():
            wait_recv(buf.at[1], ag_r.at[a, 1])

        @pl.when(i == 2)
        def _():
            wait_recv(buf.at[2], ag_r.at[a, 2])
            remote(
                ag_cut(buf, 2, 0), ag_cut(buf, 6, 0), ag_s.at[a, 6], ag_r.at[a, 6], yn, f
            ).start()
            ag_pass(buf, a, 2)

        @pl.when(i == 3)
        def _():
            wait_recv(buf.at[4], ag_r.at[a, 4])
            remote(
                ag_cut(buf, 4, 1), ag_cut(buf, 6, 1), ag_s.at[a, 8], ag_r.at[a, 8], xn, f
            ).start()
            ag_pass(buf, a, 4)
            wait_recv(buf.at[3], ag_r.at[a, 3])

        @pl.when(i == 5)
        def _():
            wait_recv(buf.at[5], ag_r.at[a, 5])

        @pl.when(i == 6)
        def _():
            wait_recv(ag_cut(buf, 6, 0), ag_r.at[a, 6])
            wait_recv(ag_cut(buf, 6, 1), ag_r.at[a, 8])
            ag_pass(buf, a, 6)

        @pl.when(i == 7)
        def _():
            wait_recv(buf.at[7], ag_r.at[a, 7])

    def ag_done(buf, a):
        for k in (1, 2, 3, 4, 5, 7):
            wait_send(buf.at[0], ag_s.at[a, k])
        wait_send(ag_cut(buf, 6, 0), ag_s.at[a, 6])
        wait_send(ag_cut(buf, 6, 1), ag_s.at[a, 8])

    def rs_step(buf, q, s, i):
        @pl.when(lax.rem(i, 2) == 1)
        def _():
            sib_send(buf, q, s, i)

        @pl.when((lax.rem(i, 2) == 0) & (i >= 4))
        def _():
            rs_send(buf, q, s, i // 2 - 1)

    def rs_send(buf, q, s, p):
        wait_recv(sr.at[s, p], sib_r.at[q, p])
        buf[2 * p] = (buf[2 * p].astype(F32) + sr[s, p].astype(F32)).astype(BF)
        low = lax.rem(p, 2)
        high = p // 2
        to = r + low * (2 - 4 * b1) + high * (4 - 8 * b2)
        remote(buf.at[2 * p], rr.at[s, p], rem_s.at[q, p], rem_r.at[q, p], to, f).start()

    def rs_total(buf, q, s, last=3):
        wait_recv(sr.at[s, 0], sib_r.at[q, 0])
        total = buf[0].astype(F32) + sr[s, 0].astype(F32)
        for p in range(1, last + 1):
            wait_recv(rr.at[s, p], rem_r.at[q, p])
            total = total + rr[s, p].astype(F32)
        return total

    def rs_done(buf, q):
        for p in range(4):
            wait_send(buf.at[2 * p + 1], sib_s.at[q, p])
            if p > 0:
                wait_send(buf.at[2 * p], rem_s.at[q, p])

    upper, lower = pl.ds(0, half), pl.ds(half, half)

    def relay_send(buf, q, s, p):
        wait_recv(sr.at[s, p], sib_r.at[q, p])
        at = 2 * p
        if p == 3:
            buf[at] = (buf[at].astype(F32) + sr[s, p].astype(F32)).astype(BF)
            for cut, to, sem in ((upper, xn, 3), (lower, yn, 0)):
                remote(
                    buf.at[at, cut, :], rr.at[s, 3, cut, :], rem_s.at[q, sem], rem_r.at[q, sem], to, f
                ).start()
            return
        keep, add, to, sem = (upper, lower, xn, 0) if p == 1 else (lower, upper, yn, 3)
        wait_recv(rr.at[s, 3, add, :], rem_r.at[q, sem])
        buf[at, keep, :] = (buf[at, keep, :].astype(F32) + sr[s, p, keep, :].astype(F32)).astype(BF)
        buf[at, add, :] = (
            buf[at, add, :].astype(F32)
            + sr[s, p, add, :].astype(F32)
            + rr[s, 3, add, :].astype(F32)
        ).astype(BF)
        remote(buf.at[at], rr.at[s, p], rem_s.at[q, p], rem_r.at[q, p], to, f).start()

    def relay_done(buf, q):
        for p in range(4):
            wait_send(buf.at[2 * p + 1], sib_s.at[q, p])
        for p in (1, 2):
            wait_send(buf.at[2 * p], rem_s.at[q, p])
        wait_send(buf.at[6, upper, :], rem_s.at[q, 3])
        wait_send(buf.at[6, lower, :], rem_s.at[q, 0])

    def sib_send(buf, q, s, i):
        remote(
            buf.at[i], sr.at[s, i // 2], sib_s.at[q, i // 2], sib_r.at[q, i // 2], sib, f
        ).start()

    row_ids = lax.broadcasted_iota(jnp.int32, (B, 1), 0)
    lanes_b = lax.broadcasted_iota(jnp.int32, (1, D), 1)
    end = doc_ref[0, 0]
    meta = jnp.where(lanes_b == 0, end, 0)
    slots = doc_ref.shape[1]
    for i in range(1, slots):
        end = end + doc_ref[0, i]
        meta = meta + jnp.where(lanes_b == i, end, 0)
    live = row_ids < end
    tokens = tok_ref[...].astype(F32)
    first_scale = lax.rsqrt(jnp.mean(tokens * tokens, axis=1, keepdims=True) + EPS)

    def norms_wait(d, _, fs):
        wait_recv(normsb.at[fs], nz_r.at[d])

    others(norms_wait)
    gain_one = jnp.concatenate([normsb[j, 0:1, :] for j in range(F)], axis=1)
    gain_two = jnp.concatenate([normsb[j, 1:2, :] for j in range(F)], axis=1)
    ag1[0, 0:B, :] = (tokens * first_scale * gain_one).astype(BF)
    ag1[0, B : B + 16, :] = jnp.broadcast_to(meta.astype(F32), (16, D)).astype(BF)
    ag_start(ag1, 0)
    ag3[0] = jnp.where(live, cot_ref[...].astype(F32), 0.0).astype(BF)

    def wave(m, first):
        cols_step(first, (wqkv, None, wgu)[first], Dz, m)
        rows_step(first + 1, (wo, None, wd)[first], m)

    wave(1, 0)
    for i in (1, 2, 3):
        ag_step(ag1, 0, i)
    for m in range(2, min(F, 3)):
        wave(m, 0)
    ag_start(ag3, 2)
    for m in range(3, F):
        wave(m, 0)
    for c in loads[3:]:
        c.wait()
    cols_start(2, wgu, Dz)
    rows_start(3, wd)
    for i in (5, 6, 7):
        ag_step(ag1, 0, i)

    gain_q = hn_ref[0:1, :].astype(F32)
    gain_k = hn_ref[1:2, :].astype(F32)
    score_scale = HEAD ** (-0.5)

    def block_layout(i):
        ends = ag1[i, B : B + 16, :][0:1, 0:HEAD].astype(F32)
        rows = lax.broadcasted_iota(jnp.int32, (B, 1), 0).astype(F32)
        cols = lax.broadcasted_iota(jnp.int32, (1, B), 1).astype(F32)
        seg_row = jnp.zeros((B, 1), F32)
        seg_col = jnp.zeros((1, B), F32)
        start = jnp.zeros((B, 1), F32)
        for n in range(slots):
            e = ends[:, n : n + 1]
            past = rows >= e
            seg_row = seg_row + past.astype(F32)
            seg_col = seg_col + (cols >= e).astype(F32)
            start = jnp.maximum(start, jnp.where(past, e, 0.0))
        alive = rows < ends[:, slots - 1 : slots]
        position = rows - jnp.where(alive, start, 0.0)
        return rows, cols, seg_row, seg_col, alive, position

    def rope_rows(position, cols):
        pick = (cols == position).astype(F32).astype(BF)
        table = mm(pick, table_ref[...])
        w = 2 * HEAD
        table = table[:, 0:w] + table[:, w : 2 * w] + table[:, 2 * w : 3 * w]
        return table[:, 0:HEAD], table[:, HEAD:w]

    def rotate(x, cos, sin):
        return x * cos + pltpu.roll(x, HEAD // 2, 1) * sin

    def head_scale(x):
        return lax.rsqrt(jnp.mean(x * x, axis=1, keepdims=True) + EPS)

    def forward_block(j, carry):
        i = lax.rem(j + 6, T)

        @pl.when(j == 3)
        def _():
            for n in (1, 2, 3):
                ag_step(ag3, 2, n)

        @pl.when(j == 4)
        def _():
            wave(1, 2)

        rows, cols, seg_row, seg_col, alive, position = block_layout(i)
        cos, sin = rope_rows(position, cols)
        pre = mm(ag1[i, 0:B, :], wqkv[...])
        qkpre[i] = pre[:, 0 : QT + HEAD]
        parts = []
        for n in range(3):
            x = pre[:, n * HEAD : (n + 1) * HEAD]
            x = x * head_scale(x) * (gain_q if n < 2 else gain_k)
            parts.append(rotate(x, cos, sin).astype(BF))
        v = pre[:, QT + HEAD : QT + 2 * HEAD].astype(BF)
        for n in range(3):
            rot[i, :, n * HEAD : (n + 1) * HEAD] = parts[n]
        rot[i, :, 3 * HEAD : 4 * HEAD] = v
        allowed = ((seg_row == seg_col) & (cols <= rows) & alive) | (cols == rows)
        for n in range(2):
            scores = mm_nt(parts[n], parts[2]) * score_scale
            scores = jnp.where(allowed, scores, NEG_FILL)
            expd = jnp.exp(scores - jnp.max(scores, axis=1, keepdims=True))
            prob = (expd / jnp.sum(expd, axis=1, keepdims=True)).astype(BF)
            probs[i, n * B : (n + 1) * B, :] = prob
            att[i, :, n * HEAD : (n + 1) * HEAD] = mm(prob, v).astype(BF)
        st[i] = mm(att[i], wo[...]).astype(BF)

        @pl.when(lax.rem(i, 2) == 1)
        def _():
            sib_send(st, 0, 0, i)

        for when, p in ((2, 3), (5, 1), (7, 2)):

            @pl.when(j == when)
            def _():
                relay_send(st, 0, 0, p)

        return carry

    lax.fori_loop(0, T, forward_block, 0)
    wave(2, 2)
    for i in (5, 6, 7):
        ag_step(ag3, 2, i)
    hid = tokens + rs_total(st, 0, 0, 2)
    relay_done(st, 0)
    hidden[...] = hid
    second_scale = lax.rsqrt(jnp.mean(hid * hid, axis=1, keepdims=True) + EPS)
    ag2[0] = (hid * second_scale * gain_two).astype(BF)
    ag_start(ag2, 1)
    for m in range(3, F):
        wave(m, 2)

    def ffn_block(i, carry):
        ag_step(ag2, 1, i)
        up_gate = mm(ag2[i], wgu[...])
        gate, up = up_gate[:, 0:FT], up_gate[:, FT : 2 * FT]
        sig = 1.0 / (1.0 + jnp.exp(-gate))
        silu = gate * sig
        actd[i, :, 0:FT] = (silu * up).astype(BF)
        d_act = mm_nt(ag3[i], wd[...])
        actd[i, :, FT : 2 * FT] = (d_act * up * sig * (1.0 + gate * (1.0 - sig))).astype(BF)
        actd[i, :, 2 * FT : 3 * FT] = (d_act * silu).astype(BF)
        st[i] = mm_nt(actd[i, :, FT : 3 * FT], wgu[...]).astype(BF)
        rs_step(st, 1, 1, i)
        return carry

    lax.fori_loop(0, T, ffn_block, 0)
    rs_send(st, 1, 1, 3)
    cols_done(2, wgu, Dz)

    step = 256

    def grad_gu(m, carry):
        at = pl.ds(pl.multiple_of(m * step, step), step)
        total = mm_tn(ag2[0, :, at], actd[0, :, FT : 3 * FT])
        for k in range(1, T):
            total = total + mm_tn(ag2[k, :, at], actd[k, :, FT : 3 * FT])
        wgu[at, :] = total.astype(BF)
        return carry

    lax.fori_loop(0, D // step, grad_gu, 0)

    def hop(item, buf, slots_ref, s, up, to):
        slot = s if up else s + (F - s) * (1 - (to - s + F - 1) // F)
        return remote(
            buf.at[pl.ds(pl.multiple_of(s * Dz, Dz), Dz), :],
            slots_ref.at[slot],
            zg_s.at[item, up, s],
            zg_r.at[item, up, s],
            r,
            to,
        )

    def hop_add(item, buf, slots_ref, s, up, slot):
        wait_recv(slots_ref.at[slot], zg_r.at[item, up, s])
        at = pl.ds(pl.multiple_of(s * Dz, Dz), Dz)
        buf[at, :] = (buf[at, :].astype(F32) + slots_ref[slot].astype(F32)).astype(BF)

    def hops_start(item, buf, slots_ref):
        @pl.when(f == 0)
        def _():
            for s in range(F - 1, 0, -1):
                hop(item, buf, slots_ref, s, 1, f + 1).start()

        @pl.when(f == F - 1)
        def _():
            for s in range(F - 1):
                hop(item, buf, slots_ref, s, 0, f - 1).start()

    def hops_step(item, buf, slots_ref, n):
        s = F - n

        @pl.when((f > 0) & (f < s))
        def _():
            hop_add(item, buf, slots_ref, s, 1, s)
            hop(item, buf, slots_ref, s, 1, f + 1).start()

        z = n - 1

        @pl.when((f < F - 1) & (f > z))
        def _():
            hop_add(item, buf, slots_ref, z, 0, z)
            hop(item, buf, slots_ref, z, 0, f - 1).start()

    def hops_total(item, buf, slots_ref):
        @pl.when(f > 0)
        def _():
            hop_add(item, buf, slots_ref, f, 1, f)

        @pl.when(f < F - 1)
        def _():
            hop_add(item, buf, slots_ref, f, 0, F)

    def hops_done(item, buf):
        part = buf.at[pl.ds(0, Dz), :]
        for s in range(F):

            @pl.when(f < s)
            def _():
                wait_send(part, zg_s.at[item, 1, s])

            @pl.when(f > s)
            def _():
                wait_send(part, zg_s.at[item, 0, s])

    def row_hop(item, buf, slots_ref, up, to):
        return remote(buf, slots_ref.at[up], zg_s.at[item, up, 0], zg_r.at[item, up, 0], r, to)

    def row_add(item, buf, slots_ref, up):
        wait_recv(slots_ref.at[up], zg_r.at[item, up, 0])
        buf[...] = (buf[...].astype(F32) + slots_ref[up].astype(F32)).astype(BF)

    def row_hops_start(item, buf, slots_ref):
        @pl.when((f == 0) & (fg > 0))
        def _():
            row_hop(item, buf, slots_ref, 1, f + 1).start()

        @pl.when((f == F - 1) & (fg < F - 1))
        def _():
            row_hop(item, buf, slots_ref, 0, f - 1).start()

    def row_hops_step(item, buf, slots_ref, n):
        @pl.when((f < fg) & (f == n))
        def _():
            row_add(item, buf, slots_ref, 1)
            row_hop(item, buf, slots_ref, 1, f + 1).start()

        @pl.when((f > fg) & (F - 1 - f == n))
        def _():
            row_add(item, buf, slots_ref, 0)
            row_hop(item, buf, slots_ref, 0, f - 1).start()

    def row_hops_total(item, buf, slots_ref):
        @pl.when((f == fg) & (f > 0))
        def _():
            row_add(item, buf, slots_ref, 1)

        @pl.when((f == fg) & (f < F - 1))
        def _():
            row_add(item, buf, slots_ref, 0)

    def row_hops_done(item, buf):
        @pl.when(f < fg)
        def _():
            wait_send(buf, zg_s.at[item, 1, 0])

        @pl.when(f > fg)
        def _():
            wait_send(buf, zg_s.at[item, 0, 0])

    hops_start(0, wgu, zr_gu)
    d_out = jnp.where(live, cot_ref[...].astype(F32), 0.0)
    pre_two = rs_total(st, 1, 1)
    rs_done(st, 1)
    hid = hidden[...]
    second_scale = lax.rsqrt(jnp.mean(hid * hid, axis=1, keepdims=True) + EPS)
    second_hat = hid * second_scale
    grad_two = jnp.sum(pre_two * second_hat, axis=0, keepdims=True)
    dn_two = pre_two * gain_two
    d_hid = d_out + second_scale * (
        dn_two - second_hat * jnp.mean(dn_two * second_hat, axis=1, keepdims=True)
    )
    dhid[...] = d_hid
    ag4[0] = d_hid.astype(BF)
    ag_start(ag4, 3)

    ag_done(ag2, 1)

    def down_block(i, carry):
        ag2[i] = mm(actd[i, :, 0:FT], wd[...]).astype(BF)

        @pl.when(lax.rem(i, 2) == 1)
        def _():
            sib_send(ag2, 2, 0, i)

        return carry

    lax.fori_loop(0, T, down_block, 0)
    rows_done(3, wd)

    def grad_down(m, carry):
        at = pl.ds(pl.multiple_of(m * step, step), step)
        total = mm_tn(actd[0, :, 0:FT], ag3[0, :, at])
        for k in range(1, T):
            total = total + mm_tn(actd[k, :, 0:FT], ag3[k, :, at])
        wd[:, at] = total.astype(BF)
        return carry

    lax.fori_loop(0, D // step, grad_down, 0)

    row_hops_start(1, wd, zr_d)
    ag_done(ag3, 2)
    ghead[...] = jnp.zeros_like(ghead)

    def backward_block(i, carry):
        ag_step(ag4, 3, i)
        for n in range(1, min(F, 4)):

            @pl.when(i == 2 * n)
            def _():
                hops_step(0, wgu, zr_gu, n)

            @pl.when(i == 2 * n + 1)
            def _():
                row_hops_step(1, wd, zr_d, n)

        rows, cols, _, _, _, position = block_layout(i)
        cos, sin = rope_rows(position, cols)
        d_att = mm_nt(ag4[i], wo[...]).astype(BF)
        k_rot = rot[i, :, QT : QT + HEAD]
        v = rot[i, :, QT + HEAD : QT + 2 * HEAD]
        d_v = jnp.zeros((B, HEAD), F32)
        d_k = jnp.zeros((B, HEAD), F32)
        d_pre = []
        sums = []

        def norm_back(grad, n, gain):
            x = qkpre[i, :, n * HEAD : (n + 1) * HEAD]
            scale = head_scale(x)
            hat = x * scale
            dn = rotate(grad, cos, -sin)
            total = jnp.sum(dn * hat, axis=0, keepdims=True)
            dn = dn * gain
            back = scale * (dn - hat * jnp.mean(dn * hat, axis=1, keepdims=True))
            return back.astype(BF), total

        for n in range(2):
            prob = probs[i, n * B : (n + 1) * B, :]
            q_rot = rot[i, :, n * HEAD : (n + 1) * HEAD]
            d_head = d_att[:, n * HEAD : (n + 1) * HEAD]
            d_prob = mm_nt(d_head, v)
            p32 = prob.astype(F32)
            center = jnp.sum(p32 * d_prob, axis=1, keepdims=True)
            d_score = (p32 * (d_prob - center)).astype(BF)
            d_v = d_v + mm_tn(prob, d_head)
            d_k = d_k + mm_tn(d_score, q_rot)
            back, total = norm_back(mm(d_score, k_rot) * score_scale, n, gain_q)
            d_pre.append(back)
            sums.append(total)
        back, total = norm_back(d_k * score_scale, 2, gain_k)
        d_pre.append(back)
        d_pre.append(d_v.astype(BF))
        ghead[0:1, :] += sums[0] + sums[1]
        ghead[1:2, :] += total
        for n in range(4):
            rot[i, :, n * HEAD : (n + 1) * HEAD] = d_pre[n]
        ag3[i] = mm_nt(rot[i], wqkv[...]).astype(BF)
        rs_step(ag3, 3, 1, i)
        for when, p in ((4, 3), (6, 1), (7, 2)):

            @pl.when(i == when)
            def _():
                relay_send(ag2, 2, 0, p)

        return carry

    lax.fori_loop(0, T, backward_block, 0)
    rs_send(ag3, 3, 1, 3)
    for n in range(4, F):
        hops_step(0, wgu, zr_gu, n)
        row_hops_step(1, wd, zr_d, n)
    cols_done(0, wqkv, Dz)
    rows_done(1, wo)

    def grad_out(m, carry):
        at = pl.ds(pl.multiple_of(m * step, step), step)
        total = mm_tn(att[0], ag4[0, :, at])
        for k in range(1, T):
            total = total + mm_tn(att[k], ag4[k, :, at])
        wo[:, at] = total.astype(BF)
        return carry

    lax.fori_loop(0, D // step, grad_out, 0)
    row_hops_start(2, wo, zr_o)

    def grad_qkv(m, carry):
        at = pl.ds(pl.multiple_of(m * step, step), step)
        total = mm_tn(ag1[0, 0:B, at], rot[0])
        for k in range(1, T):
            total = total + mm_tn(ag1[k, 0:B, at], rot[k])
        wqkv[at, :] = total.astype(BF)
        return carry

    lax.fori_loop(0, D // step, grad_qkv, 0)
    hops_start(3, wqkv, zr_qkv)

    def piece_at(item, out, rows, rank, cut=None):
        u = unit(rank)
        start, size = (0, rows) if cut is None else (cut * (rows // 2), rows // 2)
        if item in (0, 3):
            return out.at[u, pl.ds(start, size), :]
        first = pl.multiple_of(lax.rem(u, GPF) * rows + start, rows // 2)
        return out.at[pl.ds(first, size), :]

    def has(item, rank, fn):
        if item in (0, 3):
            fn()
        else:
            pl.when(unit(rank) // GPF == f)(fn)

    def fin_copy(item, src, dst, sem, to):
        return remote(src, dst, fin_s.at[item, sem], fin_r.at[item, sem], to, f)

    def fin_start(item, src, out, rows):
        def go():
            dst = piece_at(item, out, rows, t)
            fin_copy(item, src, dst, 2, xn).start()
            fin_copy(item, src, dst, 4, yn).start()
            fin_copy(item, src, dst, 1, sib).start()
            pltpu.make_async_copy(src, dst, fin_s.at[item, 0]).start()

        has(item, t, go)

    def fin_step(item, out, rows, k):
        rank = flip(k)
        full = piece_at(item, out, rows, rank)

        def go():
            if k < 6:
                wait_recv(full, fin_r.at[item, k])
                part = piece_at(item, out, rows, rank, k // 4)
                fin_copy(item, part, part, 4 + k, yn if k == 2 else xn).start()
            else:
                wait_recv(piece_at(item, out, rows, rank, 0), fin_r.at[item, 6])
                wait_recv(piece_at(item, out, rows, rank, 1), fin_r.at[item, 8])
            fin_copy(item, full, full, k + 1, sib).start()

        has(item, rank, go)

    def fin_end(item, src, out, rows):
        for k in (1, 3, 5, 7):
            full = piece_at(item, out, rows, flip(k))
            has(item, flip(k), lambda: wait_recv(full, fin_r.at[item, k]))

        def mine():
            for k in (1, 2, 4):
                wait_send(src, fin_s.at[item, k])
            pltpu.make_async_copy(src, piece_at(item, out, rows, t), fin_s.at[item, 0]).wait()

        has(item, t, mine)
        for k in (2, 4, 6):
            full = piece_at(item, out, rows, flip(k))
            part = piece_at(item, out, rows, flip(k), 0)

            def passed():
                wait_send(full, fin_s.at[item, k + 1])
                if k < 6:
                    wait_send(part, fin_s.at[item, 4 + k])

            has(item, flip(k), passed)

    gu_piece, qkv_piece = wgu.at[own(Dz), :], wqkv.at[own(Dz), :]
    hops_total(0, wgu, zr_gu)
    fin_start(0, gu_piece, ggu_out, Dz)
    row_hops_total(1, wd, zr_d)
    fin_start(1, wd, gd_out, FT)
    hops_step(3, wqkv, zr_qkv, 1)
    row_hops_step(2, wo, zr_o, 1)

    pre_one = rs_total(ag3, 3, 1)
    tokens = tok_ref[...].astype(F32)
    first_scale = lax.rsqrt(jnp.mean(tokens * tokens, axis=1, keepdims=True) + EPS)
    first_hat = tokens * first_scale
    grad_one = jnp.sum(pre_one * first_hat, axis=0, keepdims=True)
    dn_one = pre_one * gain_one
    dtok_out[...] = (
        dhid[...]
        + first_scale
        * (dn_one - first_hat * jnp.mean(dn_one * first_hat, axis=1, keepdims=True))
    ).astype(BF)
    vz[f, 0:1, :] = grad_one
    vz[f, 1:2, :] = grad_two
    vz[f, 2:3, :] = jnp.concatenate(
        [ghead[0:1, :], ghead[1:2, :], jnp.zeros((1, D - 2 * HEAD), F32)], axis=1
    )
    vz[f, 3:8, :] = jnp.zeros((5, D), F32)

    def vec_send(d, to, _):
        remote(vz.at[f], vz.at[f], vz_s.at[d], vz_r.at[d], r, to).start()

    others(vec_send)
    for n in range(2, F):
        hops_step(3, wqkv, zr_qkv, n)
        row_hops_step(2, wo, zr_o, n)
        if n == 2:
            for k in (2, 4):
                fin_step(0, ggu_out, Dz, k)
                fin_step(1, gd_out, FT, k)
            out = hidden[...] + rs_total(ag2, 2, 0, 2)
            mixed_out[...] = jnp.where(live, out, 0.0).astype(BF)
    hops_total(3, wqkv, zr_qkv)
    fin_start(3, qkv_piece, gqkv_out, Dz)
    row_hops_total(2, wo, zr_o)
    fin_start(2, wo, go_out, QT)

    def vec_recv(d, to, fs):
        wait_recv(vz.at[fs], vz_r.at[d])

    others(vec_recv)
    total = vz[0]
    for j in range(1, F):
        total = total + vz[j]
    vp[t] = total
    for k in range(1, T):
        remote(vp.at[t], vp.at[t], vp_s.at[k], vp_r.at[k], base + flip(k), f).start()
    fin_step(0, ggu_out, Dz, 6)
    fin_step(1, gd_out, FT, 6)
    for k in range(1, T):
        wait_recv(vp.at[flip(k)], vp_r.at[k])
    total = vp[0]
    for j in range(1, T):
        total = total + vp[j]
    mine = jnp.zeros((8, Dz), F32)
    for j in range(F):
        mine = mine + jnp.where(f == j, total[:, j * Dz : (j + 1) * Dz], 0.0)
    vec_out[:, 0:Dz] = mine
    vec_out[:, Dz : Dz + 2 * HEAD] = total[:, 0 : 2 * HEAD]
    for k in (2, 4, 6):
        fin_step(3, gqkv_out, Dz, k)
        fin_step(2, go_out, QT, k)
    fin_end(0, gu_piece, ggu_out, Dz)
    fin_end(1, wd, gd_out, FT)
    fin_end(3, qkv_piece, gqkv_out, Dz)
    fin_end(2, wo, go_out, QT)

    ag_done(ag1, 0)
    ag_done(ag4, 3)
    relay_done(ag2, 2)
    rs_done(ag3, 3)
    hops_done(0, wgu)
    hops_done(3, wqkv)
    row_hops_done(1, wd)
    row_hops_done(2, wo)
    for d in range(1, F):
        wait_send(normsb.at[0], nz_s.at[d])
        wait_send(vz.at[0], vz_s.at[d])
    for k in range(1, T):
        wait_send(vp.at[0], vp_s.at[k])


def finish_kernel(scale, gqkv, ggu, go, gd, oq, ok, ov, og, ou, oo, od):
    x = gqkv[0].astype(F32) * scale
    w = oq.shape[1]
    oq[...] = x[:, 0:w]
    ok[...] = x[:, w : w + HEAD]
    ov[...] = x[:, w + HEAD : w + 2 * HEAD]
    x = ggu[0].astype(F32) * scale
    w = og.shape[1]
    og[...] = x[:, 0:w]
    ou[...] = x[:, w : 2 * w]
    oo[...] = go[...].astype(F32) * scale
    od[...] = gd[...].astype(F32) * scale


def per_device(
    F,
    G,
    tokens,
    doc_lengths,
    attn_norm,
    w_query,
    key_matrix,
    value_matrix,
    head_norms,
    w_out,
    ffn_norm,
    w_gate,
    w_up,
    w_down,
    cotangent,
):
    B, D = tokens.shape
    Dz = D // F
    QW, KW, FF = w_query.shape[1], key_matrix.shape[1], w_gate.shape[1]
    QT, FT = QW // T, FF // T
    QZ, FZ = w_out.shape[0], w_down.shape[0]
    norms = jnp.zeros((8, Dz), F32)
    norms = norms.at[0].set(attn_norm.astype(F32)).at[1].set(ffn_norm.astype(F32))
    table = jnp.asarray(rope_table(B))
    vmem = pl.BlockSpec(memory_space=pltpu.VMEM)
    hbm = pl.BlockSpec(memory_space=pl.ANY)
    dma = pltpu.SemaphoreType.DMA
    sds = jax.ShapeDtypeStruct
    outs = pl.pallas_call(
        functools.partial(layer_kernel, F, B, D),
        out_shape=(
            sds((T, Dz, QT + 2 * HEAD), BF),
            sds((T, Dz, 2 * FT), BF),
            sds((QZ, D), BF),
            sds((FZ, D), BF),
            sds((8, Dz + 2 * HEAD), F32),
            sds((B, D), BF),
            sds((B, D), BF),
        ),
        in_specs=[vmem, vmem, pl.BlockSpec(memory_space=pltpu.SMEM), vmem, vmem, vmem] + [hbm] * 7,
        out_specs=(hbm, hbm, hbm, hbm, vmem, vmem, vmem),
        scratch_shapes=[
            pltpu.VMEM((T, B + 16, D), BF),
            pltpu.VMEM((T, B, D), BF),
            pltpu.VMEM((T, B, D), BF),
            pltpu.VMEM((T, B, D), BF),
            pltpu.VMEM((T, B, D), BF),
            pltpu.VMEM((2, 4, B, D), BF),
            pltpu.VMEM((2, 4, B, D), BF),
            pltpu.VMEM((D, QT + 2 * HEAD), BF),
            pltpu.VMEM((D, 2 * FT), BF),
            pltpu.VMEM((QT, D), BF),
            pltpu.VMEM((FT, D), BF),
            pltpu.VMEM((T, B, QT + HEAD), F32),
            pltpu.VMEM((T, B, QT + 2 * HEAD), BF),
            pltpu.VMEM((T, 2 * B, B), BF),
            pltpu.VMEM((T, B, QT), BF),
            pltpu.VMEM((T, B, 3 * FT), BF),
            pltpu.VMEM((B, D), F32),
            pltpu.VMEM((B, D), F32),
            pltpu.VMEM((F, 8, Dz), F32),
            pltpu.VMEM((F + 1, Dz, 2 * FT), BF),
            pltpu.VMEM((2, FT, D), BF),
            pltpu.VMEM((2, QT, D), BF),
            pltpu.VMEM((F + 1, Dz, QT + 2 * HEAD), BF),
            pltpu.VMEM((F, 8, D), F32),
            pltpu.VMEM((T, 8, D), F32),
            pltpu.VMEM((8, HEAD), F32),
            dma((4, 9)),
            dma((4, 9)),
            dma((4, 4)),
            dma((4, 4)),
            dma((4, 4)),
            dma((4, 4)),
            dma((4, 2, F)),
            dma((4, 2, F)),
            dma((F,)),
            dma((F,)),
            dma((8,)),
            dma((4, 2, F)),
            dma((4, 2, F)),
            dma((4, 9)),
            dma((4, 9)),
            dma((F,)),
            dma((F,)),
            dma((T,)),
            dma((T,)),
        ],
        compiler_params=pltpu.CompilerParams(
            collective_id=0, has_side_effects=True, vmem_limit_bytes=62 * 2**20
        ),
    )(
        tokens,
        cotangent,
        doc_lengths,
        norms,
        head_norms,
        table,
        w_query,
        key_matrix,
        value_matrix,
        w_out,
        w_gate,
        w_up,
        w_down,
    )
    gqkv, ggu, go, gd, vec, mixed, d_tokens = outs
    if G > 1:
        groups = [[t + T * n for n in range(G)] for t in range(T)]
        gqkv, ggu, go, gd = (
            lax.psum(x, "rep", axis_index_groups=groups) for x in (gqkv, ggu, go, gd)
        )
        vec = lax.psum(vec, "rep", axis_index_groups=groups)
    scale = 1.0 / math.sqrt(B * T * G * F)

    def order(u):
        return u

    qb, fb = QZ // T, FZ // T
    oq, ok, ov, og, ou, oo, od = pl.pallas_call(
        functools.partial(finish_kernel, scale),
        grid=(T,),
        out_shape=(
            sds((Dz, QW), F32),
            sds((Dz, KW), F32),
            sds((Dz, KW), F32),
            sds((Dz, FF), F32),
            sds((Dz, FF), F32),
            sds((QZ, D), F32),
            sds((FZ, D), F32),
        ),
        in_specs=[
            pl.BlockSpec((1, Dz, QT + 2 * HEAD), lambda u: (u, 0, 0)),
            pl.BlockSpec((1, Dz, 2 * FT), lambda u: (u, 0, 0)),
            pl.BlockSpec((qb, D), lambda u: (u, 0)),
            pl.BlockSpec((fb, D), lambda u: (u, 0)),
        ],
        out_specs=(
            pl.BlockSpec((Dz, QT), lambda u: (0, u)),
            pl.BlockSpec((Dz, HEAD), lambda u: (0, u)),
            pl.BlockSpec((Dz, HEAD), lambda u: (0, u)),
            pl.BlockSpec((Dz, FT), lambda u: (0, u)),
            pl.BlockSpec((Dz, FT), lambda u: (0, u)),
            pl.BlockSpec((qb, D), lambda u: (u, 0)),
            pl.BlockSpec((fb, D), lambda u: (u, 0)),
        ),
    )(gqkv, ggu, go, gd)
    vec = vec * scale
    return (
        mixed,
        d_tokens,
        vec[0, 0:Dz],
        oq,
        ok,
        ov,
        jnp.concatenate([vec[2:3, Dz : Dz + HEAD], vec[2:3, Dz + HEAD : Dz + 2 * HEAD]], axis=0),
        oo,
        vec[1, 0:Dz],
        og,
        ou,
        od,
    )


def solution(mesh):
    F = mesh.shape["fsdp"]
    G = mesh.shape["rep"] // T
    rows = P(("rep", "fsdp"), None)
    mat = P("fsdp", None)
    vec = P("fsdp")
    return jax.shard_map(
        functools.partial(per_device, F, G),
        mesh=mesh,
        in_specs=(rows, rows, vec, mat, mat, mat, P(), mat, vec, mat, mat, mat, rows),
        out_specs=(rows, rows, vec, mat, mat, mat, P(), mat, vec, mat, mat, mat),
        check_vma=False,
    )
```

```python
import functools
import math

import jax
import jax.numpy as jnp
import numpy as np
from jax import lax
from jax.experimental import pallas as pl
from jax.experimental.pallas import tpu as pltpu
from jax.sharding import PartitionSpec as P

EPS = 1e-06
ROPE_BASE = 1000000.0
NEG_FILL = -1e30
HEAD = 128
T = 8
MESH = pl.DeviceIdType.MESH
BF = jnp.bfloat16
F32 = jnp.float32


def mm(a, b):
    return lax.dot_general(a, b, (((1,), (0,)), ((), ())), preferred_element_type=F32)


def mm_nt(a, b):
    return lax.dot_general(a, b, (((1,), (1,)), ((), ())), preferred_element_type=F32)


def mm_tn(a, b):
    return lax.dot_general(a, b, (((0,), (0,)), ((), ())), preferred_element_type=F32)


def rope_table(rows):
    half = HEAD // 2
    freq = np.exp(np.arange(half, dtype=np.float64) * (-2.0 * math.log(ROPE_BASE) / HEAD))
    freq = freq.astype(np.float32)
    angle = (np.arange(rows, dtype=np.float32)[:, None] * freq[None, :]).astype(np.float64)
    cos, sin = np.cos(angle), np.sin(angle)
    full = np.concatenate([cos, sin], axis=1).astype(np.float32)
    parts = []
    rest = full
    for _ in range(3):
        part = rest.astype(jnp.bfloat16)
        parts.append(part)
        rest = rest - part.astype(np.float32)
    return np.concatenate(parts, axis=1)


def layer_kernel(
    F,
    B,
    D,
    tok_ref,
    cot_ref,
    doc_ref,
    norms_ref,
    hn_ref,
    table_ref,
    wq_ref,
    wk_ref,
    wv_ref,
    wo_ref,
    wg_ref,
    wu_ref,
    wd_ref,
    gqkv_out,
    ggu_out,
    go_out,
    gd_out,
    vec_out,
    mixed_out,
    dtok_out,
    ag1,
    ag2,
    ag3,
    ag4,
    st,
    sr,
    rr,
    wqkv,
    wgu,
    wo,
    wd,
    qkpre,
    rot,
    probs,
    att,
    actd,
    hidden,
    dhid,
    normsb,
    zr_gu,
    zr_d,
    zr_o,
    zr_qkv,
    vz,
    vp,
    ghead,
    turn,
    ag_s,
    ag_r,
    sib_s,
    sib_r,
    rem_s,
    rem_r,
    w_s,
    w_r,
    nz_s,
    nz_r,
    loc_s,
    zg_s,
    zg_r,
    fin_s,
    fin_r,
    vz_s,
    vz_r,
    vp_s,
    vp_r,
):
    Dz = D // F
    QT = wo.shape[0]
    FT = wd.shape[0]
    GPF = T // F
    half = B // 2
    r = lax.axis_index("rep")
    f = lax.axis_index("fsdp")
    t = lax.rem(r, T)
    base = r - t
    core = lax.rem(t, 2)
    chip = t // 2
    b1 = lax.rem(chip, 2)
    b2 = chip // 2

    def flip(k):
        x = core + (k % 2) * (1 - 2 * core)
        y = b1 + ((k // 2) % 2) * (1 - 2 * b1)
        z = b2 + (k // 4) * (1 - 2 * b2)
        return x + 2 * y + 4 * z

    def unit(rank):
        return lax.rem(rank, 2) * (T // 2) + rank // 2

    g = unit(t)
    fg = g // GPF
    grow = lax.rem(g, GPF)
    sib, xn, yn, dg = base + flip(1), base + flip(2), base + flip(4), base + flip(6)

    def remote(src, dst, ssem, rsem, rep, fs):
        return pltpu.make_async_remote_copy(
            src_ref=src,
            dst_ref=dst,
            send_sem=ssem,
            recv_sem=rsem,
            device_id={"rep": rep, "fsdp": fs},
            device_id_type=MESH,
        )

    def wait_recv(dst, rsem):
        remote(dst, dst, rsem, rsem, sib, f).wait_recv()

    def wait_send(src, ssem):
        remote(src, src, ssem, ssem, sib, f).wait_send()

    barrier = pltpu.get_barrier_semaphore()
    for k in range(1, T):
        pl.semaphore_signal(
            barrier, inc=1, device_id={"rep": base + flip(k), "fsdp": f}, device_id_type=MESH
        )
    for d in range(1, F):
        pl.semaphore_signal(
            barrier, inc=1, device_id={"rep": r, "fsdp": lax.rem(f + d, F)}, device_id_type=MESH
        )

    def own(n):
        return pl.ds(pl.multiple_of(f * n, n), n)

    gq = pl.ds(pl.multiple_of(g * QT, QT), QT)
    gk = pl.ds(pl.multiple_of(g * HEAD, HEAD), HEAD)
    gf = pl.ds(pl.multiple_of(g * FT, HEAD), FT)
    loads = [
        pltpu.make_async_copy(wq_ref.at[:, gq], wqkv.at[own(Dz), pl.ds(0, QT)], loc_s.at[0]),
        pltpu.make_async_copy(wk_ref.at[:, gk], wqkv.at[own(Dz), pl.ds(QT, HEAD)], loc_s.at[1]),
        pltpu.make_async_copy(
            wv_ref.at[:, gk], wqkv.at[own(Dz), pl.ds(QT + HEAD, HEAD)], loc_s.at[2]
        ),
        pltpu.make_async_copy(wg_ref.at[:, gf], wgu.at[own(Dz), pl.ds(0, FT)], loc_s.at[3]),
        pltpu.make_async_copy(wu_ref.at[:, gf], wgu.at[own(Dz), pl.ds(FT, FT)], loc_s.at[4]),
    ]
    for c in loads:
        c.start()

    def row_load(src, dst, rows, sem):
        return pltpu.make_async_copy(
            src.at[pl.ds(pl.multiple_of(grow * rows, rows), rows), :], dst, sem
        )

    @pl.when(f == fg)
    def _():
        row_load(wo_ref, wo, QT, loc_s.at[5]).start()
        row_load(wd_ref, wd, FT, loc_s.at[6]).start()

    normsb[f] = norms_ref[...]
    pl.semaphore_wait(barrier, T - 1 + F - 1)

    def others(fn):
        for d in range(1, F):
            fn(d, lax.rem(f + d, F), lax.rem(f + F - d, F))

    def norms_send(d, to, _):
        remote(normsb.at[f], normsb.at[f], nz_s.at[d], nz_r.at[d], r, to).start()

    others(norms_send)

    def line_copy(item, buf, rows, s, up, m, to):
        part = buf.at[pl.ds(pl.multiple_of(s * rows, rows), rows), :]
        return remote(part, part, w_s.at[item, up, m], w_r.at[item, up, m], r, to)

    def cols_start(item, buf, rows):
        @pl.when(f < F - 1)
        def _():
            line_copy(item, buf, rows, f, 1, 1, f + 1).start()

        @pl.when(f > 0)
        def _():
            line_copy(item, buf, rows, f, 0, 1, f - 1).start()

    def cols_step(item, buf, rows, m):
        @pl.when(f >= m)
        def _():
            line_copy(item, buf, rows, f - m, 1, m, r * 0).wait_recv()
            if m + 1 < F:

                @pl.when(f < F - 1)
                def _():
                    line_copy(item, buf, rows, f - m, 1, m + 1, f + 1).start()

        @pl.when(f + m < F)
        def _():
            line_copy(item, buf, rows, f + m, 0, m, r * 0).wait_recv()
            if m + 1 < F:

                @pl.when(f > 0)
                def _():
                    line_copy(item, buf, rows, f + m, 0, m + 1, f - 1).start()

    def cols_done(item, buf, rows):
        for m in range(1, F):

            @pl.when((f < F - 1) & (f >= m - 1))
            def _():
                line_copy(item, buf, rows, f, 1, m, r * 0).wait_send()

            @pl.when((f > 0) & (f + m - 1 < F))
            def _():
                line_copy(item, buf, rows, f, 0, m, r * 0).wait_send()

    def row_copy(item, buf, up, to):
        return remote(buf, buf, w_s.at[item, up, 0], w_r.at[item, up, 0], r, to)

    def rows_start(item, buf):
        @pl.when((f == fg) & (f < F - 1))
        def _():
            row_copy(item, buf, 1, f + 1).start()

        @pl.when((f == fg) & (f > 0))
        def _():
            row_copy(item, buf, 0, f - 1).start()

    def rows_step(item, buf, m):
        @pl.when(f - fg == m)
        def _():
            row_copy(item, buf, 1, r * 0).wait_recv()

            @pl.when(f < F - 1)
            def _():
                row_copy(item, buf, 1, f + 1).start()

        @pl.when(fg - f == m)
        def _():
            row_copy(item, buf, 0, r * 0).wait_recv()

            @pl.when(f > 0)
            def _():
                row_copy(item, buf, 0, f - 1).start()

    def rows_done(item, buf):
        @pl.when((f >= fg) & (f < F - 1))
        def _():
            row_copy(item, buf, 1, r * 0).wait_send()

        @pl.when((f <= fg) & (f > 0))
        def _():
            row_copy(item, buf, 0, r * 0).wait_send()

    for c in loads[:3]:
        c.wait()
    cols_start(0, wqkv, Dz)

    @pl.when(f == fg)
    def _():
        row_load(wo_ref, wo, QT, loc_s.at[5]).wait()
        row_load(wd_ref, wd, FT, loc_s.at[6]).wait()

    rows_start(1, wo)

    def ag_start(buf, a):
        remote(buf.at[0], buf.at[2], ag_s.at[a, 2], ag_r.at[a, 2], xn, f).start()
        remote(buf.at[0], buf.at[4], ag_s.at[a, 4], ag_r.at[a, 4], yn, f).start()
        remote(buf.at[0], buf.at[1], ag_s.at[a, 1], ag_r.at[a, 1], sib, f).start()

    def ag_cut(buf, slot, lower):
        rows = buf.shape[1]
        return buf.at[slot, pl.ds(half, rows - half), :] if lower else buf.at[slot, pl.ds(0, half), :]

    def ag_pass(buf, a, slot):
        remote(
            buf.at[slot], buf.at[slot + 1], ag_s.at[a, slot + 1], ag_r.at[a, slot + 1], sib, f
        ).start()

    def ag_step(buf, a, i):
        @pl.when(i == 1)
        def _():
            wait_recv(buf.at[1], ag_r.at[a, 1])

        @pl.when(i == 2)
        def _():
            wait_recv(buf.at[2], ag_r.at[a, 2])
            remote(
                ag_cut(buf, 2, 0), ag_cut(buf, 6, 0), ag_s.at[a, 6], ag_r.at[a, 6], yn, f
            ).start()
            ag_pass(buf, a, 2)

        @pl.when(i == 3)
        def _():
            wait_recv(buf.at[4], ag_r.at[a, 4])
            remote(
                ag_cut(buf, 4, 1), ag_cut(buf, 6, 1), ag_s.at[a, 8], ag_r.at[a, 8], xn, f
            ).start()
            ag_pass(buf, a, 4)
            wait_recv(buf.at[3], ag_r.at[a, 3])

        @pl.when(i == 5)
        def _():
            wait_recv(buf.at[5], ag_r.at[a, 5])

        @pl.when(i == 6)
        def _():
            wait_recv(ag_cut(buf, 6, 0), ag_r.at[a, 6])
            wait_recv(ag_cut(buf, 6, 1), ag_r.at[a, 8])
            ag_pass(buf, a, 6)

        @pl.when(i == 7)
        def _():
            wait_recv(buf.at[7], ag_r.at[a, 7])

    def ag_done(buf, a):
        for k in (1, 2, 3, 4, 5, 7):
            wait_send(buf.at[0], ag_s.at[a, k])
        wait_send(ag_cut(buf, 6, 0), ag_s.at[a, 6])
        wait_send(ag_cut(buf, 6, 1), ag_s.at[a, 8])

    def rs_step(buf, q, s, i):
        @pl.when(lax.rem(i, 2) == 1)
        def _():
            sib_send(buf, q, s, i)

        @pl.when((lax.rem(i, 2) == 0) & (i >= 4))
        def _():
            rs_send(buf, q, s, i // 2 - 1)

    def rs_send(buf, q, s, p):
        wait_recv(sr.at[s, p], sib_r.at[q, p])
        buf[2 * p] = (buf[2 * p].astype(F32) + sr[s, p].astype(F32)).astype(BF)
        low = lax.rem(p, 2)
        high = p // 2
        to = r + low * (2 - 4 * b1) + high * (4 - 8 * b2)
        remote(buf.at[2 * p], rr.at[s, p - 1], rem_s.at[q, p], rem_r.at[q, p], to, f).start()

    def rs_total(buf, q, s):
        wait_recv(sr.at[s, 0], sib_r.at[q, 0])
        total = buf[0].astype(F32) + sr[s, 0].astype(F32)
        for p in range(1, 4):
            wait_recv(rr.at[s, p - 1], rem_r.at[q, p])
            total = total + rr[s, p - 1].astype(F32)
        return total

    def rs_done(buf, q):
        for p in range(4):
            wait_send(buf.at[2 * p + 1], sib_s.at[q, p])
            if p > 0:
                wait_send(buf.at[2 * p], rem_s.at[q, p])

    upper, lower = pl.ds(0, half), pl.ds(half, half)

    def relay_send(buf, q, s, p, own):
        at = 2 * p
        if p == 3:
            wait_recv(sr.at[s, p], sib_r.at[q, p])
            buf[at] = (buf[at].astype(F32) + sr[s, p].astype(F32)).astype(BF)
            for cut, to, sem in ((upper, xn, 3), (lower, yn, 0)):
                remote(
                    buf.at[at, cut, :], rr.at[s, 2, cut, :], rem_s.at[q, sem], rem_r.at[q, sem], to, f
                ).start()
            return
        keep, add, to, sem = (upper, lower, xn, 0) if p == 1 else (lower, upper, yn, 3)
        cut = keep if own else add
        if own:
            wait_recv(sr.at[s, p], sib_r.at[q, p])
        else:
            wait_recv(rr.at[s, 2, add, :], rem_r.at[q, sem])
        total = buf[at, cut, :].astype(F32) + sr[s, p, cut, :].astype(F32)
        if not own:
            total = total + rr[s, 2, add, :].astype(F32)
        buf[at, cut, :] = total.astype(BF)
        sem = p if own else p + 3
        remote(
            buf.at[at, cut, :], rr.at[s, p - 1, cut, :], rem_s.at[q, sem], rem_r.at[q, sem], to, f
        ).start()

    def relay_total(buf, q, s):
        wait_recv(sr.at[s, 0], sib_r.at[q, 0])
        for sem in (1, 2, 4, 5):
            wait_recv(rr.at[s, 0, upper, :], rem_r.at[q, sem])
        return (
            buf[0].astype(F32)
            + sr[s, 0].astype(F32)
            + rr[s, 0].astype(F32)
            + rr[s, 1].astype(F32)
        )

    def relay_done(buf, q):
        for p in range(4):
            wait_send(buf.at[2 * p + 1], sib_s.at[q, p])
        for sem in range(6):
            wait_send(buf.at[6, upper, :], rem_s.at[q, sem])

    def sib_send(buf, q, s, i):
        remote(
            buf.at[i], sr.at[s, i // 2], sib_s.at[q, i // 2], sib_r.at[q, i // 2], sib, f
        ).start()

    row_ids = lax.broadcasted_iota(jnp.int32, (B, 1), 0)
    lanes_b = lax.broadcasted_iota(jnp.int32, (1, D), 1)
    end = doc_ref[0, 0]
    meta = jnp.where(lanes_b == 0, end, 0)
    slots = doc_ref.shape[1]
    for i in range(1, slots):
        end = end + doc_ref[0, i]
        meta = meta + jnp.where(lanes_b == i, end, 0)
    live = row_ids < end
    tokens = tok_ref[...].astype(F32)
    first_scale = lax.rsqrt(jnp.mean(tokens * tokens, axis=1, keepdims=True) + EPS)

    def norms_wait(d, _, fs):
        wait_recv(normsb.at[fs], nz_r.at[d])

    others(norms_wait)
    gain_one = jnp.concatenate([normsb[j, 0:1, :] for j in range(F)], axis=1)
    gain_two = jnp.concatenate([normsb[j, 1:2, :] for j in range(F)], axis=1)
    ag1[0, 0:B, :] = (tokens * first_scale * gain_one).astype(BF)
    ag1[0, B : B + 16, :] = jnp.broadcast_to(meta.astype(F32), (16, D)).astype(BF)
    ag_start(ag1, 0)
    ag3[0] = jnp.where(live, cot_ref[...].astype(F32), 0.0).astype(BF)

    gain_q = hn_ref[0:1, :].astype(F32)
    gain_k = hn_ref[1:2, :].astype(F32)
    score_scale = HEAD ** (-0.5)

    def block_layout(i):
        ends = ag1[i, B : B + 16, :][0:1, 0:HEAD].astype(F32)
        rows = lax.broadcasted_iota(jnp.int32, (B, 1), 0).astype(F32)
        cols = lax.broadcasted_iota(jnp.int32, (1, B), 1).astype(F32)
        seg_row = jnp.zeros((B, 1), F32)
        seg_col = jnp.zeros((1, B), F32)
        start = jnp.zeros((B, 1), F32)
        for n in range(slots):
            e = ends[:, n : n + 1]
            past = rows >= e
            seg_row = seg_row + past.astype(F32)
            seg_col = seg_col + (cols >= e).astype(F32)
            start = jnp.maximum(start, jnp.where(past, e, 0.0))
        alive = rows < ends[:, slots - 1 : slots]
        position = rows - jnp.where(alive, start, 0.0)
        return rows, cols, seg_row, seg_col, alive, position

    def rope_rows(position, cols):
        pick = (cols == position).astype(F32).astype(BF)
        table = mm(pick, table_ref[...])
        return table[:, 0:HEAD] + table[:, HEAD : 2 * HEAD] + table[:, 2 * HEAD : 3 * HEAD]

    def turns(i):
        x = turn[i]
        y = pltpu.roll(x, HEAD // 2, 1)
        first = lax.broadcasted_iota(jnp.int32, x.shape, 1) < HEAD // 2
        return jnp.where(first, x, y), jnp.where(first, -y, x)

    def rotate(x, cos, sin):
        return x * cos + pltpu.roll(x, HEAD // 2, 1) * sin

    def head_scale(x):
        return lax.rsqrt(jnp.mean(x * x, axis=1, keepdims=True) + EPS)

    def prepare(i, carry):
        rows, cols, seg_row, seg_col, alive, position = block_layout(i)
        turn[i] = rope_rows(position, cols)
        allowed = ((seg_row == seg_col) & (cols <= rows) & alive) | (cols == rows)
        ag4[i, :, 0:B] = jnp.where(allowed, 0.0, NEG_FILL).astype(BF)
        return carry

    def wave(m, first):
        cols_step(first, (wqkv, None, wgu)[first], Dz, m)
        rows_step(first + 1, (wo, None, wd)[first], m)

    wave(1, 0)
    for i in (1, 2, 3):
        ag_step(ag1, 0, i)
    for m in range(2, min(F, 3)):
        wave(m, 0)
    ag_start(ag3, 2)
    lax.fori_loop(0, 5, prepare, 0)
    for m in range(3, F):
        wave(m, 0)
    for c in loads[3:]:
        c.wait()
    cols_start(2, wgu, Dz)
    rows_start(3, wd)
    for i in (5, 6, 7):
        ag_step(ag1, 0, i)
    lax.fori_loop(5, T, prepare, 0)

    def forward_block(j, carry):
        pair = j // 2
        pair = pair + 3 * ((3 - pair) // 3) - 3 * (pair // 3)
        i = 2 * pair + lax.rem(j, 2)

        @pl.when(j == 3)
        def _():
            for n in (1, 2, 3):
                ag_step(ag3, 2, n)

        @pl.when(j == 4)
        def _():
            wave(1, 2)

        cos, sin = turns(i)
        pre = mm(ag1[i, 0:B, :], wqkv[...])
        qkpre[i] = pre[:, 0 : QT + HEAD]
        parts = []
        for n in range(3):
            x = pre[:, n * HEAD : (n + 1) * HEAD]
            x = x * head_scale(x) * (gain_q if n < 2 else gain_k)
            parts.append(rotate(x, cos, sin).astype(BF))
        v = pre[:, QT + HEAD : QT + 2 * HEAD].astype(BF)
        for n in range(3):
            rot[i, :, n * HEAD : (n + 1) * HEAD] = parts[n]
        rot[i, :, 3 * HEAD : 4 * HEAD] = v
        mask = ag4[i, :, 0:B].astype(F32)
        for n in range(2):
            scores = mm_nt(parts[n], parts[2]) * score_scale + mask
            expd = jnp.exp(scores - jnp.max(scores, axis=1, keepdims=True))
            prob = (expd / jnp.sum(expd, axis=1, keepdims=True)).astype(BF)
            probs[i, n * B : (n + 1) * B, :] = prob
            att[i, :, n * HEAD : (n + 1) * HEAD] = mm(prob, v).astype(BF)
        st[i] = mm(att[i], wo[...]).astype(BF)

        @pl.when(lax.rem(i, 2) == 1)
        def _():
            sib_send(st, 0, 0, i)

        for when, p, first in ((2, 3, 1), (4, 1, 1), (6, 2, 1), (6, 1, 0), (7, 2, 0)):

            @pl.when(j == when)
            def _():
                relay_send(st, 0, 0, p, first)

        return carry

    lax.fori_loop(0, T, forward_block, 0)
    wave(2, 2)
    for i in (5, 6, 7):
        ag_step(ag3, 2, i)
    hid = tokens + relay_total(st, 0, 0)
    relay_done(st, 0)
    hidden[...] = hid
    second_scale = lax.rsqrt(jnp.mean(hid * hid, axis=1, keepdims=True) + EPS)
    ag2[0] = (hid * second_scale * gain_two).astype(BF)
    ag_start(ag2, 1)
    for m in range(3, F):
        wave(m, 2)

    def ffn_block(i, carry):
        ag_step(ag2, 1, i)
        up_gate = mm(ag2[i], wgu[...])
        gate, up = up_gate[:, 0:FT], up_gate[:, FT : 2 * FT]
        sig = 1.0 / (1.0 + jnp.exp(-gate))
        silu = gate * sig
        actd[i, :, 0:FT] = (silu * up).astype(BF)
        d_act = mm_nt(ag3[i], wd[...])
        actd[i, :, FT : 2 * FT] = (d_act * up * sig * (1.0 + gate * (1.0 - sig))).astype(BF)
        actd[i, :, 2 * FT : 3 * FT] = (d_act * silu).astype(BF)
        st[i] = mm_nt(actd[i, :, FT : 3 * FT], wgu[...]).astype(BF)
        rs_step(st, 1, 1, i)
        return carry

    lax.fori_loop(0, T, ffn_block, 0)
    rs_send(st, 1, 1, 3)
    cols_done(2, wgu, Dz)

    step = 256

    def grad_gu(m, carry):
        at = pl.ds(pl.multiple_of(m * step, step), step)
        total = mm_tn(ag2[0, :, at], actd[0, :, FT : 3 * FT])
        for k in range(1, T):
            total = total + mm_tn(ag2[k, :, at], actd[k, :, FT : 3 * FT])
        wgu[at, :] = total.astype(BF)
        return carry

    lax.fori_loop(0, D // step, grad_gu, 0)

    def scatter(item, buf, slots_ref, cut):
        def send(d, to, _):
            at = pl.ds(pl.multiple_of(to * Dz, Dz), Dz)
            remote(
                buf.at[at, cut],
                slots_ref.at[f, :, cut],
                zg_s.at[item, 0, d],
                zg_r.at[item, 0, d],
                r,
                to,
            ).start()

        others(send)

    def scatter_total(item, buf, slots_ref, cut):
        total = buf[own(Dz), cut].astype(F32)
        others(lambda d, to, fs: wait_recv(slots_ref.at[fs, :, cut], zg_r.at[item, 0, d]))
        for d in range(1, F):
            total = total + slots_ref[lax.rem(f + d, F), :, cut].astype(F32)
        buf[own(Dz), cut] = total.astype(BF)

    def scatter_done(item, buf, cut):
        others(lambda d, to, fs: wait_send(buf.at[own(Dz), cut], zg_s.at[item, 0, d]))

    def hop(item, buf, slots_ref, s, up, to):
        slot = s if up else s + (F - s) * (1 - (to - s + F - 1) // F)
        return remote(
            buf.at[pl.ds(pl.multiple_of(s * Dz, Dz), Dz), :],
            slots_ref.at[slot],
            zg_s.at[item, up, s],
            zg_r.at[item, up, s],
            r,
            to,
        )

    def hop_add(item, buf, slots_ref, s, up, slot):
        wait_recv(slots_ref.at[slot], zg_r.at[item, up, s])
        at = pl.ds(pl.multiple_of(s * Dz, Dz), Dz)
        buf[at, :] = (buf[at, :].astype(F32) + slots_ref[slot].astype(F32)).astype(BF)

    def hops_start(item, buf, slots_ref):
        @pl.when(f == 0)
        def _():
            for s in range(F - 1, 0, -1):
                hop(item, buf, slots_ref, s, 1, f + 1).start()

        @pl.when(f == F - 1)
        def _():
            for s in range(F - 1):
                hop(item, buf, slots_ref, s, 0, f - 1).start()

    def hops_step(item, buf, slots_ref, n):
        s = F - n

        @pl.when((f > 0) & (f < s))
        def _():
            hop_add(item, buf, slots_ref, s, 1, s)
            hop(item, buf, slots_ref, s, 1, f + 1).start()

        z = n - 1

        @pl.when((f < F - 1) & (f > z))
        def _():
            hop_add(item, buf, slots_ref, z, 0, z)
            hop(item, buf, slots_ref, z, 0, f - 1).start()

    def hops_total(item, buf, slots_ref):
        @pl.when(f > 0)
        def _():
            hop_add(item, buf, slots_ref, f, 1, f)

        @pl.when(f < F - 1)
        def _():
            hop_add(item, buf, slots_ref, f, 0, F)

    def hops_done(item, buf):
        part = buf.at[pl.ds(0, Dz), :]
        for s in range(F):

            @pl.when(f < s)
            def _():
                wait_send(part, zg_s.at[item, 1, s])

            @pl.when(f > s)
            def _():
                wait_send(part, zg_s.at[item, 0, s])

    def row_hop(item, buf, slots_ref, up, to):
        return remote(buf, slots_ref.at[up], zg_s.at[item, up, 0], zg_r.at[item, up, 0], r, to)

    def row_add(item, buf, slots_ref, up):
        wait_recv(slots_ref.at[up], zg_r.at[item, up, 0])
        buf[...] = (buf[...].astype(F32) + slots_ref[up].astype(F32)).astype(BF)

    def row_hops_start(item, buf, slots_ref):
        @pl.when((f == 0) & (fg > 0))
        def _():
            row_hop(item, buf, slots_ref, 1, f + 1).start()

        @pl.when((f == F - 1) & (fg < F - 1))
        def _():
            row_hop(item, buf, slots_ref, 0, f - 1).start()

    def row_hops_step(item, buf, slots_ref, n):
        @pl.when((f < fg) & (f == n))
        def _():
            row_add(item, buf, slots_ref, 1)
            row_hop(item, buf, slots_ref, 1, f + 1).start()

        @pl.when((f > fg) & (F - 1 - f == n))
        def _():
            row_add(item, buf, slots_ref, 0)
            row_hop(item, buf, slots_ref, 0, f - 1).start()

    def row_hops_total(item, buf, slots_ref):
        @pl.when((f == fg) & (f > 0))
        def _():
            row_add(item, buf, slots_ref, 1)

        @pl.when((f == fg) & (f < F - 1))
        def _():
            row_add(item, buf, slots_ref, 0)

    def row_hops_done(item, buf):
        @pl.when(f < fg)
        def _():
            wait_send(buf, zg_s.at[item, 1, 0])

        @pl.when(f > fg)
        def _():
            wait_send(buf, zg_s.at[item, 0, 0])

    all_q, all_kv = pl.ds(0, QT), pl.ds(QT, 2 * HEAD)
    hops_start(0, wgu, zr_gu)
    ag_done(ag2, 1)

    def down_block(i, carry):
        ag2[i] = mm(actd[i, :, 0:FT], wd[...]).astype(BF)

        @pl.when(lax.rem(i, 2) == 1)
        def _():
            sib_send(ag2, 2, 0, i)

        return carry

    lax.fori_loop(0, T, down_block, 0)
    rows_done(3, wd)

    def grad_down(m, carry):
        at = pl.ds(pl.multiple_of(m * step, step), step)
        total = mm_tn(actd[0, :, 0:FT], ag3[0, :, at])
        for k in range(1, T):
            total = total + mm_tn(actd[k, :, 0:FT], ag3[k, :, at])
        wd[:, at] = total.astype(BF)
        return carry

    lax.fori_loop(0, D // step, grad_down, 0)

    row_hops_start(1, wd, zr_d)
    d_out = jnp.where(live, cot_ref[...].astype(F32), 0.0)
    pre_two = rs_total(st, 1, 1)
    hops_step(0, wgu, zr_gu, 1)
    rs_done(st, 1)
    hid = hidden[...]
    second_scale = lax.rsqrt(jnp.mean(hid * hid, axis=1, keepdims=True) + EPS)
    second_hat = hid * second_scale
    grad_two = jnp.sum(pre_two * second_hat, axis=0, keepdims=True)
    dn_two = pre_two * gain_two
    d_hid = d_out + second_scale * (
        dn_two - second_hat * jnp.mean(dn_two * second_hat, axis=1, keepdims=True)
    )
    dhid[...] = d_hid
    ag4[0] = d_hid.astype(BF)
    ag_start(ag4, 3)

    ag_done(ag3, 2)
    ghead[...] = jnp.zeros_like(ghead)

    def piece_at(item, out, rows, rank, cut=None):
        u = unit(rank)
        start, size = (0, rows) if cut is None else (cut * (rows // 2), rows // 2)
        if item == 0:
            return out.at[u, pl.ds(start, size), :]
        if item > 2:
            return out.at[u, pl.ds(start, size), all_q if item == 3 else all_kv]
        first = pl.multiple_of(lax.rem(u, GPF) * rows + start, rows // 2)
        return out.at[pl.ds(first, size), :]

    def has(item, rank, fn):
        if item in (0, 3, 4):
            fn()
        else:
            pl.when(unit(rank) // GPF == f)(fn)

    def fin_copy(item, src, dst, sem, to):
        return remote(src, dst, fin_s.at[item, sem], fin_r.at[item, sem], to, f)

    def fin_start(item, src, out, rows):
        def go():
            dst = piece_at(item, out, rows, t)
            fin_copy(item, src, dst, 2, xn).start()
            fin_copy(item, src, dst, 4, yn).start()
            fin_copy(item, src, dst, 1, sib).start()
            pltpu.make_async_copy(src, dst, fin_s.at[item, 0]).start()

        has(item, t, go)

    def fin_step(item, out, rows, k):
        rank = flip(k)
        full = piece_at(item, out, rows, rank)

        def go():
            if k < 6:
                wait_recv(full, fin_r.at[item, k])
                part = piece_at(item, out, rows, rank, k // 4)
                fin_copy(item, part, part, 4 + k, yn if k == 2 else xn).start()
            else:
                wait_recv(piece_at(item, out, rows, rank, 0), fin_r.at[item, 6])
                wait_recv(piece_at(item, out, rows, rank, 1), fin_r.at[item, 8])
            fin_copy(item, full, full, k + 1, sib).start()

        has(item, rank, go)

    def fin_end(item, src, out, rows):
        for k in (1, 3, 5, 7):
            full = piece_at(item, out, rows, flip(k))
            has(item, flip(k), lambda: wait_recv(full, fin_r.at[item, k]))

        def mine():
            for k in (1, 2, 4):
                wait_send(src, fin_s.at[item, k])
            pltpu.make_async_copy(src, piece_at(item, out, rows, t), fin_s.at[item, 0]).wait()

        has(item, t, mine)
        for k in (2, 4, 6):
            full = piece_at(item, out, rows, flip(k))
            part = piece_at(item, out, rows, flip(k), 0)

            def passed():
                wait_send(full, fin_s.at[item, k + 1])
                if k < 6:
                    wait_send(part, fin_s.at[item, 4 + k])

            has(item, flip(k), passed)

    gu_piece = wgu.at[own(Dz), :]
    q_piece, kv_piece = wqkv.at[own(Dz), all_q], wqkv.at[own(Dz), all_kv]
    go_piece = st.at[0]

    def grad_out(m, carry):
        at = pl.ds(pl.multiple_of(m * step, step), step)
        total = mm_tn(att[0], ag4[0, :, at])
        for k in range(1, T):
            total = total + mm_tn(att[k], ag4[k, :, at])
        st[0, :, at] = total.astype(BF)
        return carry

    def backward_block(i, carry):
        ag_step(ag4, 3, i)

        @pl.when(i == 1)
        def _():
            if F > 2:
                hops_step(0, wgu, zr_gu, 2)

        @pl.when(i == 3)
        def _():
            row_hops_step(1, wd, zr_d, 1)
            for n in range(3, F):
                hops_step(0, wgu, zr_gu, n)

        @pl.when(i == 7)
        def _():
            for n in range(2, F - 1):
                row_hops_step(1, wd, zr_d, n)
            lax.fori_loop(0, D // step, grad_out, 0)
            row_hops_start(2, go_piece, zr_o)

        cos, sin = turns(i)
        d_att = mm_nt(ag4[i], wo[...]).astype(BF)
        k_rot = rot[i, :, QT : QT + HEAD]
        v = rot[i, :, QT + HEAD : QT + 2 * HEAD]
        d_v = jnp.zeros((B, HEAD), F32)
        d_k = jnp.zeros((B, HEAD), F32)
        d_pre = []
        sums = []

        def norm_back(grad, n, gain):
            x = qkpre[i, :, n * HEAD : (n + 1) * HEAD]
            scale = head_scale(x)
            hat = x * scale
            dn = rotate(grad, cos, -sin)
            total = jnp.sum(dn * hat, axis=0, keepdims=True)
            dn = dn * gain
            back = scale * (dn - hat * jnp.mean(dn * hat, axis=1, keepdims=True))
            return back.astype(BF), total

        for n in range(2):
            prob = probs[i, n * B : (n + 1) * B, :]
            q_rot = rot[i, :, n * HEAD : (n + 1) * HEAD]
            d_head = d_att[:, n * HEAD : (n + 1) * HEAD]
            d_prob = mm_nt(d_head, v)
            p32 = prob.astype(F32)
            center = jnp.sum(p32 * d_prob, axis=1, keepdims=True)
            d_score = (p32 * (d_prob - center)).astype(BF)
            d_v = d_v + mm_tn(prob, d_head)
            d_k = d_k + mm_tn(d_score, q_rot)
            back, total = norm_back(mm(d_score, k_rot) * score_scale, n, gain_q)
            d_pre.append(back)
            sums.append(total)
        back, total = norm_back(d_k * score_scale, 2, gain_k)
        d_pre.append(back)
        d_pre.append(d_v.astype(BF))
        ghead[0:1, :] += sums[0] + sums[1]
        ghead[1:2, :] += total
        for n in range(4):
            rot[i, :, n * HEAD : (n + 1) * HEAD] = d_pre[n]
        ag3[i] = mm_nt(rot[i], wqkv[...]).astype(BF)
        @pl.when(lax.rem(i, 2) == 1)
        def _():
            sib_send(ag3, 3, 1, i)

        for when, p in ((4, 1), (6, 2)):

            @pl.when(i == when)
            def _():
                relay_send(ag3, 3, 1, p, 1)

        for when, p, first in ((4, 3, 1), (5, 1, 1), (6, 2, 1), (7, 1, 0), (7, 2, 0)):

            @pl.when(i == when)
            def _():
                relay_send(ag2, 2, 0, p, first)

        return carry

    lax.fori_loop(0, T, backward_block, 0)
    relay_send(ag3, 3, 1, 3, 1)
    cols_done(0, wqkv, Dz)
    rows_done(1, wo)

    def grad_qkv(m, carry):
        at = pl.ds(pl.multiple_of(m * step, step), step)
        total = mm_tn(ag1[0, 0:B, at], rot[0])
        for k in range(1, T):
            total = total + mm_tn(ag1[k, 0:B, at], rot[k])
        wqkv[at, :] = total.astype(BF)
        return carry

    lax.fori_loop(0, D // step, grad_qkv, 0)
    scatter(3, wqkv, zr_qkv, all_q)
    scatter(4, wqkv, zr_qkv, all_kv)
    relay_send(ag3, 3, 1, 1, 0)
    relay_send(ag3, 3, 1, 2, 0)

    hops_total(0, wgu, zr_gu)
    fin_start(0, gu_piece, ggu_out, Dz)
    row_hops_total(1, wd, zr_d)
    fin_start(1, wd, gd_out, FT)
    row_hops_step(2, go_piece, zr_o, 1)
    for k in (2, 4):
        fin_step(0, ggu_out, Dz, k)

    pre_one = relay_total(ag3, 3, 1)
    tokens = tok_ref[...].astype(F32)
    first_scale = lax.rsqrt(jnp.mean(tokens * tokens, axis=1, keepdims=True) + EPS)
    first_hat = tokens * first_scale
    grad_one = jnp.sum(pre_one * first_hat, axis=0, keepdims=True)
    dn_one = pre_one * gain_one
    dtok_out[...] = (
        dhid[...]
        + first_scale
        * (dn_one - first_hat * jnp.mean(dn_one * first_hat, axis=1, keepdims=True))
    ).astype(BF)
    vz[f, 0:1, :] = grad_one
    vz[f, 1:2, :] = grad_two
    vz[f, 2:3, :] = jnp.concatenate(
        [ghead[0:1, :], ghead[1:2, :], jnp.zeros((1, D - 2 * HEAD), F32)], axis=1
    )
    vz[f, 3:8, :] = jnp.zeros((5, D), F32)

    def vec_send(d, to, _):
        remote(vz.at[f], vz.at[f], vz_s.at[d], vz_r.at[d], r, to).start()

    others(vec_send)
    for n in range(2, F - 1):
        row_hops_step(2, go_piece, zr_o, n)
    fin_step(0, ggu_out, Dz, 6)
    for k in (2, 4):
        fin_step(1, gd_out, FT, k)
    out = hidden[...] + relay_total(ag2, 2, 0)
    mixed_out[...] = jnp.where(live, out, 0.0).astype(BF)
    scatter_total(3, wqkv, zr_qkv, all_q)
    fin_start(3, q_piece, gqkv_out, Dz)

    def vec_recv(d, to, fs):
        wait_recv(vz.at[fs], vz_r.at[d])

    others(vec_recv)
    total = vz[0]
    for j in range(1, F):
        total = total + vz[j]
    vp[t] = total
    for k in range(1, T):
        remote(vp.at[t], vp.at[t], vp_s.at[k], vp_r.at[k], base + flip(k), f).start()
    row_hops_total(2, go_piece, zr_o)
    fin_start(2, go_piece, go_out, QT)
    fin_step(1, gd_out, FT, 6)
    scatter_total(4, wqkv, zr_qkv, all_kv)
    fin_start(4, kv_piece, gqkv_out, Dz)
    for k in range(1, T):
        wait_recv(vp.at[flip(k)], vp_r.at[k])
    total = vp[0]
    for j in range(1, T):
        total = total + vp[j]
    mine = jnp.zeros((8, Dz), F32)
    for j in range(F):
        mine = mine + jnp.where(f == j, total[:, j * Dz : (j + 1) * Dz], 0.0)
    vec_out[:, 0:Dz] = mine
    vec_out[:, Dz : Dz + 2 * HEAD] = total[:, 0 : 2 * HEAD]
    for k in (2, 4, 6):
        fin_step(3, gqkv_out, Dz, k)
        fin_step(2, go_out, QT, k)
        fin_step(4, gqkv_out, Dz, k)
    fin_end(0, gu_piece, ggu_out, Dz)
    fin_end(1, wd, gd_out, FT)
    fin_end(3, q_piece, gqkv_out, Dz)
    fin_end(2, go_piece, go_out, QT)
    fin_end(4, kv_piece, gqkv_out, Dz)

    ag_done(ag1, 0)
    ag_done(ag4, 3)
    relay_done(ag2, 2)
    relay_done(ag3, 3)
    hops_done(0, wgu)
    scatter_done(3, wqkv, all_q)
    scatter_done(4, wqkv, all_kv)
    row_hops_done(1, wd)
    row_hops_done(2, go_piece)
    for d in range(1, F):
        wait_send(normsb.at[0], nz_s.at[d])
        wait_send(vz.at[0], vz_s.at[d])
    for k in range(1, T):
        wait_send(vp.at[0], vp_s.at[k])


def finish_kernel(
    scale, gqkv, ggu, go, gd, vec, mixed, dtok, oq, ok, ov, og, ou, oo, od, o1, o2, oh, om, ot
):
    x = gqkv[0].astype(F32) * scale
    w = oq.shape[1]
    oq[...] = x[:, 0:w]
    ok[...] = x[:, w : w + HEAD]
    ov[...] = x[:, w + HEAD : w + 2 * HEAD]
    x = ggu[0].astype(F32) * scale
    w = og.shape[1]
    og[...] = x[:, 0:w]
    ou[...] = x[:, w : 2 * w]
    oo[...] = go[...].astype(F32) * scale
    od[...] = gd[...].astype(F32) * scale
    om[...] = mixed[...]
    ot[...] = dtok[...]

    @pl.when(pl.program_id(0) == 0)
    def _():
        w = o1.shape[1]
        o1[...] = vec[0:1, 0:w] * scale
        o2[...] = vec[1:2, 0:w] * scale
        oh[0:1, :] = vec[2:3, w : w + HEAD] * scale
        oh[1:2, :] = vec[2:3, w + HEAD : w + 2 * HEAD] * scale


def per_device(
    F,
    G,
    tokens,
    doc_lengths,
    attn_norm,
    w_query,
    key_matrix,
    value_matrix,
    head_norms,
    w_out,
    ffn_norm,
    w_gate,
    w_up,
    w_down,
    cotangent,
):
    B, D = tokens.shape
    Dz = D // F
    QW, KW, FF = w_query.shape[1], key_matrix.shape[1], w_gate.shape[1]
    QT, FT = QW // T, FF // T
    QZ, FZ = w_out.shape[0], w_down.shape[0]
    norms = jnp.zeros((8, Dz), F32)
    norms = norms.at[0].set(attn_norm.astype(F32)).at[1].set(ffn_norm.astype(F32))
    table = jnp.asarray(rope_table(B))
    vmem = pl.BlockSpec(memory_space=pltpu.VMEM)
    hbm = pl.BlockSpec(memory_space=pl.ANY)
    dma = pltpu.SemaphoreType.DMA
    sds = jax.ShapeDtypeStruct
    outs = pl.pallas_call(
        functools.partial(layer_kernel, F, B, D),
        out_shape=(
            sds((T, Dz, QT + 2 * HEAD), BF),
            sds((T, Dz, 2 * FT), BF),
            sds((QZ, D), BF),
            sds((FZ, D), BF),
            sds((8, Dz + 2 * HEAD), F32),
            sds((B, D), BF),
            sds((B, D), BF),
        ),
        in_specs=[vmem, vmem, pl.BlockSpec(memory_space=pltpu.SMEM), vmem, vmem, vmem] + [hbm] * 7,
        out_specs=(hbm, hbm, hbm, hbm, vmem, vmem, vmem),
        scratch_shapes=[
            pltpu.VMEM((T, B + 16, D), BF),
            pltpu.VMEM((T, B, D), BF),
            pltpu.VMEM((T, B, D), BF),
            pltpu.VMEM((T, B, D), BF),
            pltpu.VMEM((T, B, D), BF),
            pltpu.VMEM((2, 4, B, D), BF),
            pltpu.VMEM((2, 3, B, D), BF),
            pltpu.VMEM((D, QT + 2 * HEAD), BF),
            pltpu.VMEM((D, 2 * FT), BF),
            pltpu.VMEM((QT, D), BF),
            pltpu.VMEM((FT, D), BF),
            pltpu.VMEM((T, B, QT + HEAD), F32),
            pltpu.VMEM((T, B, QT + 2 * HEAD), BF),
            pltpu.VMEM((T, 2 * B, B), BF),
            pltpu.VMEM((T, B, QT), BF),
            pltpu.VMEM((T, B, 3 * FT), BF),
            pltpu.VMEM((B, D), F32),
            pltpu.VMEM((B, D), F32),
            pltpu.VMEM((F, 8, Dz), F32),
            pltpu.VMEM((F + 1, Dz, 2 * FT), BF),
            pltpu.VMEM((2, FT, D), BF),
            pltpu.VMEM((2, QT, D), BF),
            pltpu.VMEM((F, Dz, QT + 2 * HEAD), BF),
            pltpu.VMEM((F, 8, D), F32),
            pltpu.VMEM((T, 8, D), F32),
            pltpu.VMEM((8, HEAD), F32),
            pltpu.VMEM((T, B, HEAD), F32),
            dma((4, 9)),
            dma((4, 9)),
            dma((4, 4)),
            dma((4, 4)),
            dma((4, 6)),
            dma((4, 6)),
            dma((4, 2, F)),
            dma((4, 2, F)),
            dma((F,)),
            dma((F,)),
            dma((8,)),
            dma((5, 2, F)),
            dma((5, 2, F)),
            dma((5, 9)),
            dma((5, 9)),
            dma((F,)),
            dma((F,)),
            dma((T,)),
            dma((T,)),
        ],
        compiler_params=pltpu.CompilerParams(
            collective_id=0, has_side_effects=True, vmem_limit_bytes=62 * 2**20
        ),
    )(
        tokens,
        cotangent,
        doc_lengths,
        norms,
        head_norms,
        table,
        w_query,
        key_matrix,
        value_matrix,
        w_out,
        w_gate,
        w_up,
        w_down,
    )
    gqkv, ggu, go, gd, vec, mixed, d_tokens = outs
    if G > 1:
        groups = [[t + T * n for n in range(G)] for t in range(T)]
        gqkv, ggu, go, gd = (
            lax.psum(x, "rep", axis_index_groups=groups) for x in (gqkv, ggu, go, gd)
        )
        vec = lax.psum(vec, "rep", axis_index_groups=groups)
    scale = 1.0 / math.sqrt(B * T * G * F)

    qb, fb = QZ // T, FZ // T
    bb = B // T
    oq, ok, ov, og, ou, oo, od, o1, o2, oh, mixed, d_tokens = pl.pallas_call(
        functools.partial(finish_kernel, scale),
        grid=(T,),
        out_shape=(
            sds((Dz, QW), F32),
            sds((Dz, KW), F32),
            sds((Dz, KW), F32),
            sds((Dz, FF), F32),
            sds((Dz, FF), F32),
            sds((QZ, D), F32),
            sds((FZ, D), F32),
            sds((1, Dz), F32),
            sds((1, Dz), F32),
            sds((2, HEAD), F32),
            sds((B, D), BF),
            sds((B, D), BF),
        ),
        in_specs=[
            pl.BlockSpec((1, Dz, QT + 2 * HEAD), lambda u: (u, 0, 0)),
            pl.BlockSpec((1, Dz, 2 * FT), lambda u: (u, 0, 0)),
            pl.BlockSpec((qb, D), lambda u: (u, 0)),
            pl.BlockSpec((fb, D), lambda u: (u, 0)),
            pl.BlockSpec((8, Dz + 2 * HEAD), lambda u: (0, 0)),
            pl.BlockSpec((bb, D), lambda u: (u, 0)),
            pl.BlockSpec((bb, D), lambda u: (u, 0)),
        ],
        out_specs=(
            pl.BlockSpec((Dz, QT), lambda u: (0, u)),
            pl.BlockSpec((Dz, HEAD), lambda u: (0, u)),
            pl.BlockSpec((Dz, HEAD), lambda u: (0, u)),
            pl.BlockSpec((Dz, FT), lambda u: (0, u)),
            pl.BlockSpec((Dz, FT), lambda u: (0, u)),
            pl.BlockSpec((qb, D), lambda u: (u, 0)),
            pl.BlockSpec((fb, D), lambda u: (u, 0)),
            pl.BlockSpec((1, Dz), lambda u: (0, 0)),
            pl.BlockSpec((1, Dz), lambda u: (0, 0)),
            pl.BlockSpec((2, HEAD), lambda u: (0, 0)),
            pl.BlockSpec((bb, D), lambda u: (u, 0)),
            pl.BlockSpec((bb, D), lambda u: (u, 0)),
        ),
    )(gqkv, ggu, go, gd, vec, mixed, d_tokens)
    return (
        mixed,
        d_tokens,
        o1.reshape(Dz),
        oq,
        ok,
        ov,
        oh,
        oo,
        o2.reshape(Dz),
        og,
        ou,
        od,
    )


def solution(mesh):
    F = mesh.shape["fsdp"]
    G = mesh.shape["rep"] // T
    rows = P(("rep", "fsdp"), None)
    mat = P("fsdp", None)
    vec = P("fsdp")
    return jax.shard_map(
        functools.partial(per_device, F, G),
        mesh=mesh,
        in_specs=(rows, rows, vec, mat, mat, mat, P(), mat, vec, mat, mat, mat, rows),
        out_specs=(rows, rows, vec, mat, mat, mat, P(), mat, vec, mat, mat, mat),
        check_vma=False,
    )
```

```python
import functools
import math

import jax
import jax.numpy as jnp
import numpy as np
from jax import lax
from jax.experimental import pallas as pl
from jax.experimental.pallas import tpu as pltpu
from jax.sharding import PartitionSpec as P

EPS = 1e-06
ROPE_BASE = 1000000.0
NEG_FILL = -1e30
HEAD = 128
T = 8
MESH = pl.DeviceIdType.MESH
BF = jnp.bfloat16
F32 = jnp.float32


def mm(a, b):
    return lax.dot_general(a, b, (((1,), (0,)), ((), ())), preferred_element_type=F32)


def mm_nt(a, b):
    return lax.dot_general(a, b, (((1,), (1,)), ((), ())), preferred_element_type=F32)


def mm_tn(a, b):
    return lax.dot_general(a, b, (((0,), (0,)), ((), ())), preferred_element_type=F32)


def rope_table(rows):
    half = HEAD // 2
    freq = np.exp(np.arange(half, dtype=np.float64) * (-2.0 * math.log(ROPE_BASE) / HEAD))
    freq = freq.astype(np.float32)
    angle = (np.arange(rows, dtype=np.float32)[:, None] * freq[None, :]).astype(np.float64)
    cos, sin = np.cos(angle), np.sin(angle)
    full = np.concatenate([cos, sin], axis=1).astype(np.float32)
    parts = []
    rest = full
    for _ in range(3):
        part = rest.astype(jnp.bfloat16)
        parts.append(part)
        rest = rest - part.astype(np.float32)
    return np.concatenate(parts, axis=1)


def layer_kernel(
    F,
    B,
    D,
    tok_ref,
    cot_ref,
    doc_ref,
    norms_ref,
    hn_ref,
    table_ref,
    wq_ref,
    wk_ref,
    wv_ref,
    wo_ref,
    wg_ref,
    wu_ref,
    wd_ref,
    gqkv_out,
    ggu_out,
    go_out,
    gd_out,
    vec_out,
    mixed_out,
    dtok_out,
    ag1,
    ag2,
    ag3,
    ag4,
    st,
    sr,
    rr,
    wqkv,
    wgu,
    wo,
    wd,
    qkpre,
    rot,
    probs,
    att,
    actd,
    hidden,
    dhid,
    normsb,
    zr_gu,
    zr_d,
    zr_o,
    zr_qkv,
    vz,
    vp,
    ghead,
    turn,
    ag_s,
    ag_r,
    sib_s,
    sib_r,
    rem_s,
    rem_r,
    w_s,
    w_r,
    nz_s,
    nz_r,
    loc_s,
    zg_s,
    zg_r,
    fin_s,
    fin_r,
    vz_s,
    vz_r,
    vp_s,
    vp_r,
):
    Dz = D // F
    QT = wo.shape[0]
    FT = wd.shape[0]
    GPF = T // F
    half = B // 2
    r = lax.axis_index("rep")
    f = lax.axis_index("fsdp")
    t = lax.rem(r, T)
    base = r - t
    core = lax.rem(t, 2)
    chip = t // 2
    b1 = lax.rem(chip, 2)
    b2 = chip // 2

    def flip(k):
        x = core + (k % 2) * (1 - 2 * core)
        y = b1 + ((k // 2) % 2) * (1 - 2 * b1)
        z = b2 + (k // 4) * (1 - 2 * b2)
        return x + 2 * y + 4 * z

    def unit(rank):
        return lax.rem(rank, 2) * (T // 2) + rank // 2

    g = unit(t)
    fg = g // GPF
    grow = lax.rem(g, GPF)
    sib, xn, yn, dg = base + flip(1), base + flip(2), base + flip(4), base + flip(6)

    def remote(src, dst, ssem, rsem, rep, fs):
        return pltpu.make_async_remote_copy(
            src_ref=src,
            dst_ref=dst,
            send_sem=ssem,
            recv_sem=rsem,
            device_id={"rep": rep, "fsdp": fs},
            device_id_type=MESH,
        )

    def wait_recv(dst, rsem):
        remote(dst, dst, rsem, rsem, sib, f).wait_recv()

    def wait_send(src, ssem):
        remote(src, src, ssem, ssem, sib, f).wait_send()

    barrier = pltpu.get_barrier_semaphore()
    for k in range(1, T):
        pl.semaphore_signal(
            barrier, inc=1, device_id={"rep": base + flip(k), "fsdp": f}, device_id_type=MESH
        )
    for d in range(1, F):
        pl.semaphore_signal(
            barrier, inc=1, device_id={"rep": r, "fsdp": lax.rem(f + d, F)}, device_id_type=MESH
        )

    def own(n):
        return pl.ds(pl.multiple_of(f * n, n), n)

    gq = pl.ds(pl.multiple_of(g * QT, QT), QT)
    gk = pl.ds(pl.multiple_of(g * HEAD, HEAD), HEAD)
    gf = pl.ds(pl.multiple_of(g * FT, HEAD), FT)
    loads = [
        pltpu.make_async_copy(wq_ref.at[:, gq], wqkv.at[own(Dz), pl.ds(0, QT)], loc_s.at[0]),
        pltpu.make_async_copy(wk_ref.at[:, gk], wqkv.at[own(Dz), pl.ds(QT, HEAD)], loc_s.at[1]),
        pltpu.make_async_copy(
            wv_ref.at[:, gk], wqkv.at[own(Dz), pl.ds(QT + HEAD, HEAD)], loc_s.at[2]
        ),
        pltpu.make_async_copy(wg_ref.at[:, gf], wgu.at[own(Dz), pl.ds(0, FT)], loc_s.at[3]),
        pltpu.make_async_copy(wu_ref.at[:, gf], wgu.at[own(Dz), pl.ds(FT, FT)], loc_s.at[4]),
    ]
    for c in loads:
        c.start()

    def row_load(src, dst, rows, sem):
        return pltpu.make_async_copy(
            src.at[pl.ds(pl.multiple_of(grow * rows, rows), rows), :], dst, sem
        )

    @pl.when(f == fg)
    def _():
        row_load(wo_ref, wo, QT, loc_s.at[5]).start()
        row_load(wd_ref, wd, FT, loc_s.at[6]).start()

    normsb[f] = norms_ref[...]
    pl.semaphore_wait(barrier, T - 1 + F - 1)

    def others(fn):
        for d in range(1, F):
            fn(d, lax.rem(f + d, F), lax.rem(f + F - d, F))

    def norms_send(d, to, _):
        remote(normsb.at[f], normsb.at[f], nz_s.at[d], nz_r.at[d], r, to).start()

    others(norms_send)

    def line_copy(item, buf, rows, s, up, m, to):
        part = buf.at[pl.ds(pl.multiple_of(s * rows, rows), rows), :]
        return remote(part, part, w_s.at[item, up, m], w_r.at[item, up, m], r, to)

    def cols_start(item, buf, rows):
        @pl.when(f < F - 1)
        def _():
            line_copy(item, buf, rows, f, 1, 1, f + 1).start()

        @pl.when(f > 0)
        def _():
            line_copy(item, buf, rows, f, 0, 1, f - 1).start()

    def cols_step(item, buf, rows, m):
        @pl.when(f >= m)
        def _():
            line_copy(item, buf, rows, f - m, 1, m, r * 0).wait_recv()
            if m + 1 < F:

                @pl.when(f < F - 1)
                def _():
                    line_copy(item, buf, rows, f - m, 1, m + 1, f + 1).start()

        @pl.when(f + m < F)
        def _():
            line_copy(item, buf, rows, f + m, 0, m, r * 0).wait_recv()
            if m + 1 < F:

                @pl.when(f > 0)
                def _():
                    line_copy(item, buf, rows, f + m, 0, m + 1, f - 1).start()

    def cols_done(item, buf, rows):
        for m in range(1, F):

            @pl.when((f < F - 1) & (f >= m - 1))
            def _():
                line_copy(item, buf, rows, f, 1, m, r * 0).wait_send()

            @pl.when((f > 0) & (f + m - 1 < F))
            def _():
                line_copy(item, buf, rows, f, 0, m, r * 0).wait_send()

    def row_copy(item, buf, up, to):
        return remote(buf, buf, w_s.at[item, up, 0], w_r.at[item, up, 0], r, to)

    def rows_start(item, buf):
        @pl.when((f == fg) & (f < F - 1))
        def _():
            row_copy(item, buf, 1, f + 1).start()

        @pl.when((f == fg) & (f > 0))
        def _():
            row_copy(item, buf, 0, f - 1).start()

    def rows_step(item, buf, m):
        @pl.when(f - fg == m)
        def _():
            row_copy(item, buf, 1, r * 0).wait_recv()

            @pl.when(f < F - 1)
            def _():
                row_copy(item, buf, 1, f + 1).start()

        @pl.when(fg - f == m)
        def _():
            row_copy(item, buf, 0, r * 0).wait_recv()

            @pl.when(f > 0)
            def _():
                row_copy(item, buf, 0, f - 1).start()

    def rows_done(item, buf):
        @pl.when((f >= fg) & (f < F - 1))
        def _():
            row_copy(item, buf, 1, r * 0).wait_send()

        @pl.when((f <= fg) & (f > 0))
        def _():
            row_copy(item, buf, 0, r * 0).wait_send()

    for c in loads[:3]:
        c.wait()
    cols_start(0, wqkv, Dz)

    @pl.when(f == fg)
    def _():
        row_load(wo_ref, wo, QT, loc_s.at[5]).wait()
        row_load(wd_ref, wd, FT, loc_s.at[6]).wait()

    rows_start(1, wo)

    def ag_start(buf, a):
        remote(buf.at[0], buf.at[2], ag_s.at[a, 2], ag_r.at[a, 2], xn, f).start()
        remote(buf.at[0], buf.at[4], ag_s.at[a, 4], ag_r.at[a, 4], yn, f).start()
        remote(buf.at[0], buf.at[1], ag_s.at[a, 1], ag_r.at[a, 1], sib, f).start()

    def ag_cut(buf, slot, lower):
        rows = buf.shape[1]
        return buf.at[slot, pl.ds(half, rows - half), :] if lower else buf.at[slot, pl.ds(0, half), :]

    def ag_pass(buf, a, slot):
        remote(
            buf.at[slot], buf.at[slot + 1], ag_s.at[a, slot + 1], ag_r.at[a, slot + 1], sib, f
        ).start()

    def ag_step(buf, a, i):
        @pl.when(i == 1)
        def _():
            wait_recv(buf.at[1], ag_r.at[a, 1])

        @pl.when(i == 2)
        def _():
            wait_recv(buf.at[2], ag_r.at[a, 2])
            remote(
                ag_cut(buf, 2, 0), ag_cut(buf, 6, 0), ag_s.at[a, 6], ag_r.at[a, 6], yn, f
            ).start()
            ag_pass(buf, a, 2)

        @pl.when(i == 3)
        def _():
            wait_recv(buf.at[4], ag_r.at[a, 4])
            remote(
                ag_cut(buf, 4, 1), ag_cut(buf, 6, 1), ag_s.at[a, 8], ag_r.at[a, 8], xn, f
            ).start()
            ag_pass(buf, a, 4)
            wait_recv(buf.at[3], ag_r.at[a, 3])

        @pl.when(i == 5)
        def _():
            wait_recv(buf.at[5], ag_r.at[a, 5])

        @pl.when(i == 6)
        def _():
            wait_recv(ag_cut(buf, 6, 0), ag_r.at[a, 6])
            wait_recv(ag_cut(buf, 6, 1), ag_r.at[a, 8])
            ag_pass(buf, a, 6)

        @pl.when(i == 7)
        def _():
            wait_recv(buf.at[7], ag_r.at[a, 7])

    def ag_done(buf, a):
        for k in (1, 2, 3, 4, 5, 7):
            wait_send(buf.at[0], ag_s.at[a, k])
        wait_send(ag_cut(buf, 6, 0), ag_s.at[a, 6])
        wait_send(ag_cut(buf, 6, 1), ag_s.at[a, 8])

    def rs_step(buf, q, s, i):
        @pl.when(lax.rem(i, 2) == 1)
        def _():
            sib_send(buf, q, s, i)

        @pl.when((lax.rem(i, 2) == 0) & (i >= 4))
        def _():
            rs_send(buf, q, s, i // 2 - 1)

    def rs_send(buf, q, s, p):
        wait_recv(sr.at[s, p], sib_r.at[q, p])
        buf[2 * p] = (buf[2 * p].astype(F32) + sr[s, p].astype(F32)).astype(BF)
        low = lax.rem(p, 2)
        high = p // 2
        to = r + low * (2 - 4 * b1) + high * (4 - 8 * b2)
        remote(buf.at[2 * p], rr.at[s, p - 1], rem_s.at[q, p], rem_r.at[q, p], to, f).start()

    def rs_total(buf, q, s):
        wait_recv(sr.at[s, 0], sib_r.at[q, 0])
        total = buf[0].astype(F32) + sr[s, 0].astype(F32)
        for p in range(1, 4):
            wait_recv(rr.at[s, p - 1], rem_r.at[q, p])
            total = total + rr[s, p - 1].astype(F32)
        return total

    def rs_done(buf, q):
        for p in range(4):
            wait_send(buf.at[2 * p + 1], sib_s.at[q, p])
            if p > 0:
                wait_send(buf.at[2 * p], rem_s.at[q, p])

    upper, lower = pl.ds(0, half), pl.ds(half, half)

    def relay_send(buf, q, s, p, own):
        at = 2 * p
        if p == 3:
            wait_recv(sr.at[s, p], sib_r.at[q, p])
            buf[at] = (buf[at].astype(F32) + sr[s, p].astype(F32)).astype(BF)
            for cut, to, sem in ((upper, xn, 3), (lower, yn, 0)):
                remote(
                    buf.at[at, cut, :], rr.at[s, 2, cut, :], rem_s.at[q, sem], rem_r.at[q, sem], to, f
                ).start()
            return
        keep, add, to, sem = (upper, lower, xn, 0) if p == 1 else (lower, upper, yn, 3)
        cut = keep if own else add
        if own:
            wait_recv(sr.at[s, p], sib_r.at[q, p])
        else:
            wait_recv(rr.at[s, 2, add, :], rem_r.at[q, sem])
        total = buf[at, cut, :].astype(F32) + sr[s, p, cut, :].astype(F32)
        if not own:
            total = total + rr[s, 2, add, :].astype(F32)
        buf[at, cut, :] = total.astype(BF)
        sem = p if own else p + 3
        remote(
            buf.at[at, cut, :], rr.at[s, p - 1, cut, :], rem_s.at[q, sem], rem_r.at[q, sem], to, f
        ).start()

    def relay_total(buf, q, s):
        wait_recv(sr.at[s, 0], sib_r.at[q, 0])
        for sem in (1, 2, 4, 5):
            wait_recv(rr.at[s, 0, upper, :], rem_r.at[q, sem])
        return (
            buf[0].astype(F32)
            + sr[s, 0].astype(F32)
            + rr[s, 0].astype(F32)
            + rr[s, 1].astype(F32)
        )

    def relay_done(buf, q):
        for p in range(4):
            wait_send(buf.at[2 * p + 1], sib_s.at[q, p])
        for sem in range(6):
            wait_send(buf.at[6, upper, :], rem_s.at[q, sem])

    def sib_send(buf, q, s, i):
        remote(
            buf.at[i], sr.at[s, i // 2], sib_s.at[q, i // 2], sib_r.at[q, i // 2], sib, f
        ).start()

    row_ids = lax.broadcasted_iota(jnp.int32, (B, 1), 0)
    lanes_b = lax.broadcasted_iota(jnp.int32, (1, D), 1)
    end = doc_ref[0, 0]
    meta = jnp.where(lanes_b == 0, end, 0)
    slots = doc_ref.shape[1]
    for i in range(1, slots):
        end = end + doc_ref[0, i]
        meta = meta + jnp.where(lanes_b == i, end, 0)
    live = row_ids < end
    tokens = tok_ref[...].astype(F32)
    first_scale = lax.rsqrt(jnp.mean(tokens * tokens, axis=1, keepdims=True) + EPS)

    def norms_wait(d, _, fs):
        wait_recv(normsb.at[fs], nz_r.at[d])

    others(norms_wait)
    gain_one = jnp.concatenate([normsb[j, 0:1, :] for j in range(F)], axis=1)
    gain_two = jnp.concatenate([normsb[j, 1:2, :] for j in range(F)], axis=1)
    ag1[0, 0:B, :] = (tokens * first_scale * gain_one).astype(BF)
    ag1[0, B : B + 16, :] = jnp.broadcast_to(meta.astype(F32), (16, D)).astype(BF)
    ag_start(ag1, 0)
    ag3[0] = jnp.where(live, cot_ref[...].astype(F32), 0.0).astype(BF)

    gain_q = hn_ref[0:1, :].astype(F32)
    gain_k = hn_ref[1:2, :].astype(F32)
    score_scale = HEAD ** (-0.5)

    def block_layout(i):
        ends = ag1[i, B : B + 16, :][0:1, 0:HEAD].astype(F32)
        rows = lax.broadcasted_iota(jnp.int32, (B, 1), 0).astype(F32)
        cols = lax.broadcasted_iota(jnp.int32, (1, B), 1).astype(F32)
        seg_row = jnp.zeros((B, 1), F32)
        seg_col = jnp.zeros((1, B), F32)
        start = jnp.zeros((B, 1), F32)
        for n in range(slots):
            e = ends[:, n : n + 1]
            past = rows >= e
            seg_row = seg_row + past.astype(F32)
            seg_col = seg_col + (cols >= e).astype(F32)
            start = jnp.maximum(start, jnp.where(past, e, 0.0))
        alive = rows < ends[:, slots - 1 : slots]
        position = rows - jnp.where(alive, start, 0.0)
        return rows, cols, seg_row, seg_col, alive, position

    def rope_rows(position, cols):
        pick = (cols == position).astype(F32).astype(BF)
        table = mm(pick, table_ref[...])
        return table[:, 0:HEAD] + table[:, HEAD : 2 * HEAD] + table[:, 2 * HEAD : 3 * HEAD]

    def turns(i):
        x = turn[i]
        y = pltpu.roll(x, HEAD // 2, 1)
        first = lax.broadcasted_iota(jnp.int32, x.shape, 1) < HEAD // 2
        return jnp.where(first, x, y), jnp.where(first, -y, x)

    def rotate(x, cos, sin):
        return x * cos + pltpu.roll(x, HEAD // 2, 1) * sin

    def head_scale(x):
        return lax.rsqrt(jnp.mean(x * x, axis=1, keepdims=True) + EPS)

    def prepare(i, carry):
        rows, cols, seg_row, seg_col, alive, position = block_layout(i)
        turn[i] = rope_rows(position, cols)
        allowed = ((seg_row == seg_col) & (cols <= rows) & alive) | (cols == rows)
        ag4[i, :, 0:B] = jnp.where(allowed, 0.0, NEG_FILL).astype(BF)
        return carry

    def wave(m, first):
        cols_step(first, (wqkv, None, wgu)[first], Dz, m)
        rows_step(first + 1, (wo, None, wd)[first], m)

    wave(1, 0)
    for i in (1, 2, 3):
        ag_step(ag1, 0, i)
    for m in range(2, min(F, 3)):
        wave(m, 0)
    ag_start(ag3, 2)
    lax.fori_loop(0, 5, prepare, 0)
    for m in range(3, F):
        wave(m, 0)
    for c in loads[3:]:
        c.wait()
    cols_start(2, wgu, Dz)
    rows_start(3, wd)
    for i in (5, 6, 7):
        ag_step(ag1, 0, i)
    lax.fori_loop(5, T, prepare, 0)

    def forward_block(j, carry):
        pair = j // 2
        pair = pair + 3 * ((3 - pair) // 3) - 3 * (pair // 3)
        i = 2 * pair + lax.rem(j, 2)

        @pl.when(j == 4)
        def _():
            wave(1, 2)

        cos, sin = turns(i)
        pre = mm(ag1[i, 0:B, :], wqkv[...])
        qkpre[i] = pre[:, 0 : QT + HEAD]
        parts = []
        for n in range(3):
            x = pre[:, n * HEAD : (n + 1) * HEAD]
            x = x * head_scale(x) * (gain_q if n < 2 else gain_k)
            parts.append(rotate(x, cos, sin).astype(BF))
        v = pre[:, QT + HEAD : QT + 2 * HEAD].astype(BF)
        for n in range(3):
            rot[i, :, n * HEAD : (n + 1) * HEAD] = parts[n]
        rot[i, :, 3 * HEAD : 4 * HEAD] = v
        mask = ag4[i, :, 0:B].astype(F32)
        for n in range(2):
            scores = mm_nt(parts[n], parts[2]) * score_scale + mask
            expd = jnp.exp(scores - jnp.max(scores, axis=1, keepdims=True))
            prob = (expd * (1.0 / jnp.sum(expd, axis=1, keepdims=True))).astype(BF)
            probs[i, n * B : (n + 1) * B, :] = prob
            att[i, :, n * HEAD : (n + 1) * HEAD] = mm(prob, v).astype(BF)
        st[i] = mm(att[i], wo[...]).astype(BF)

        @pl.when(lax.rem(i, 2) == 1)
        def _():
            sib_send(st, 0, 0, i)

        for when, p, first in ((2, 3, 1), (4, 1, 1), (6, 2, 1), (6, 1, 0), (7, 2, 0)):

            @pl.when(j == when)
            def _():
                relay_send(st, 0, 0, p, first)

        return carry

    lax.fori_loop(0, T, forward_block, 0)
    for i in (1, 2, 3):
        ag_step(ag3, 2, i)
    wave(2, 2)
    hid = tokens + relay_total(st, 0, 0)
    relay_done(st, 0)
    hidden[...] = hid
    second_scale = lax.rsqrt(jnp.mean(hid * hid, axis=1, keepdims=True) + EPS)
    ag2[0] = (hid * second_scale * gain_two).astype(BF)
    ag_start(ag2, 1)
    for i in (5, 6, 7):
        ag_step(ag3, 2, i)
    for m in range(3, F):
        wave(m, 2)

    def ffn_block(i, carry):
        ag_step(ag2, 1, i)
        up_gate = mm(ag2[i], wgu[...])
        gate, up = up_gate[:, 0:FT], up_gate[:, FT : 2 * FT]
        sig = 1.0 / (1.0 + jnp.exp(-gate))
        silu = gate * sig
        actd[i, :, 0:FT] = (silu * up).astype(BF)
        d_act = mm_nt(ag3[i], wd[...])
        actd[i, :, FT : 2 * FT] = (d_act * up * (sig + silu * (1.0 - sig))).astype(BF)
        actd[i, :, 2 * FT : 3 * FT] = (d_act * silu).astype(BF)
        st[i] = mm_nt(actd[i, :, FT : 3 * FT], wgu[...]).astype(BF)
        @pl.when(lax.rem(i, 2) == 1)
        def _():
            sib_send(st, 1, 1, i)

        for when, p in ((4, 1), (6, 2)):

            @pl.when(i == when)
            def _():
                relay_send(st, 1, 1, p, 1)

        return carry

    lax.fori_loop(0, T, ffn_block, 0)
    relay_send(st, 1, 1, 3, 1)
    cols_done(2, wgu, Dz)

    step = 256

    def grad_gu(m, carry):
        at = pl.ds(pl.multiple_of(m * step, step), step)
        left, right = ag2[:, :, at], actd[:, :, FT : 3 * FT]
        total = mm_tn(
            left.reshape(T * B, left.shape[2]), right.reshape(T * B, right.shape[2])
        )
        wgu[at, :] = total.astype(BF)
        return carry

    lax.fori_loop(0, D // step, grad_gu, 0)

    def scatter(item, buf, slots_ref, cut):
        def send(d, to, _):
            at = pl.ds(pl.multiple_of(to * Dz, Dz), Dz)
            remote(
                buf.at[at, cut],
                slots_ref.at[f, :, cut],
                zg_s.at[item, 0, d],
                zg_r.at[item, 0, d],
                r,
                to,
            ).start()

        others(send)

    def scatter_total(item, buf, slots_ref, cut):
        total = buf[own(Dz), cut].astype(F32)
        others(lambda d, to, fs: wait_recv(slots_ref.at[fs, :, cut], zg_r.at[item, 0, d]))
        for d in range(1, F):
            total = total + slots_ref[lax.rem(f + d, F), :, cut].astype(F32)
        buf[own(Dz), cut] = total.astype(BF)

    def scatter_done(item, buf, cut):
        others(lambda d, to, fs: wait_send(buf.at[own(Dz), cut], zg_s.at[item, 0, d]))

    def hop(item, buf, slots_ref, s, up, to):
        slot = s if up else s + (F - s) * (1 - (to - s + F - 1) // F)
        return remote(
            buf.at[pl.ds(pl.multiple_of(s * Dz, Dz), Dz), :],
            slots_ref.at[slot],
            zg_s.at[item, up, s],
            zg_r.at[item, up, s],
            r,
            to,
        )

    def hop_add(item, buf, slots_ref, s, up, slot):
        wait_recv(slots_ref.at[slot], zg_r.at[item, up, s])
        at = pl.ds(pl.multiple_of(s * Dz, Dz), Dz)
        buf[at, :] = (buf[at, :].astype(F32) + slots_ref[slot].astype(F32)).astype(BF)

    def hops_start(item, buf, slots_ref):
        @pl.when(f == 0)
        def _():
            for s in range(F - 1, 0, -1):
                hop(item, buf, slots_ref, s, 1, f + 1).start()

        @pl.when(f == F - 1)
        def _():
            for s in range(F - 1):
                hop(item, buf, slots_ref, s, 0, f - 1).start()

    def hops_step(item, buf, slots_ref, n):
        s = F - n

        @pl.when((f > 0) & (f < s))
        def _():
            hop_add(item, buf, slots_ref, s, 1, s)
            hop(item, buf, slots_ref, s, 1, f + 1).start()

        z = n - 1

        @pl.when((f < F - 1) & (f > z))
        def _():
            hop_add(item, buf, slots_ref, z, 0, z)
            hop(item, buf, slots_ref, z, 0, f - 1).start()

    def hops_total(item, buf, slots_ref):
        @pl.when(f > 0)
        def _():
            hop_add(item, buf, slots_ref, f, 1, f)

        @pl.when(f < F - 1)
        def _():
            hop_add(item, buf, slots_ref, f, 0, F)

    def hops_done(item, buf):
        part = buf.at[pl.ds(0, Dz), :]
        for s in range(F):

            @pl.when(f < s)
            def _():
                wait_send(part, zg_s.at[item, 1, s])

            @pl.when(f > s)
            def _():
                wait_send(part, zg_s.at[item, 0, s])

    def row_hop(item, buf, slots_ref, up, to):
        return remote(buf, slots_ref.at[up], zg_s.at[item, up, 0], zg_r.at[item, up, 0], r, to)

    def row_add(item, buf, slots_ref, up):
        wait_recv(slots_ref.at[up], zg_r.at[item, up, 0])
        buf[...] = (buf[...].astype(F32) + slots_ref[up].astype(F32)).astype(BF)

    def row_hops_start(item, buf, slots_ref):
        @pl.when((f == 0) & (fg > 0))
        def _():
            row_hop(item, buf, slots_ref, 1, f + 1).start()

        @pl.when((f == F - 1) & (fg < F - 1))
        def _():
            row_hop(item, buf, slots_ref, 0, f - 1).start()

    def row_hops_step(item, buf, slots_ref, n):
        @pl.when((f < fg) & (f == n))
        def _():
            row_add(item, buf, slots_ref, 1)
            row_hop(item, buf, slots_ref, 1, f + 1).start()

        @pl.when((f > fg) & (F - 1 - f == n))
        def _():
            row_add(item, buf, slots_ref, 0)
            row_hop(item, buf, slots_ref, 0, f - 1).start()

    def row_hops_total(item, buf, slots_ref):
        @pl.when((f == fg) & (f > 0))
        def _():
            row_add(item, buf, slots_ref, 1)

        @pl.when((f == fg) & (f < F - 1))
        def _():
            row_add(item, buf, slots_ref, 0)

    def row_hops_done(item, buf):
        @pl.when(f < fg)
        def _():
            wait_send(buf, zg_s.at[item, 1, 0])

        @pl.when(f > fg)
        def _():
            wait_send(buf, zg_s.at[item, 0, 0])

    all_q, all_kv = pl.ds(0, QT), pl.ds(QT, 2 * HEAD)
    hops_start(0, wgu, zr_gu)
    ag_done(ag2, 1)

    def down_block(i, carry):
        ag2[i] = mm(actd[i, :, 0:FT], wd[...]).astype(BF)

        @pl.when(lax.rem(i, 2) == 1)
        def _():
            sib_send(ag2, 2, 0, i)

        return carry

    lax.fori_loop(0, T, down_block, 0)
    relay_send(st, 1, 1, 1, 0)
    relay_send(st, 1, 1, 2, 0)
    rows_done(3, wd)

    def grad_down(m, carry):
        at = pl.ds(pl.multiple_of(m * step, step), step)
        left, right = actd[:, :, 0:FT], ag3[:, :, at]
        total = mm_tn(
            left.reshape(T * B, left.shape[2]), right.reshape(T * B, right.shape[2])
        )
        wd[:, at] = total.astype(BF)
        return carry

    lax.fori_loop(0, D // step, grad_down, 0)

    row_hops_start(1, wd, zr_d)
    d_out = jnp.where(live, cot_ref[...].astype(F32), 0.0)
    for p in (3, 1, 2):
        relay_send(ag2, 2, 0, p, 1)
    pre_two = relay_total(st, 1, 1)
    hops_step(0, wgu, zr_gu, 1)
    relay_done(st, 1)
    hid = hidden[...]
    second_scale = lax.rsqrt(jnp.mean(hid * hid, axis=1, keepdims=True) + EPS)
    second_hat = hid * second_scale
    grad_two = jnp.sum(pre_two * second_hat, axis=0, keepdims=True)
    dn_two = pre_two * gain_two
    d_hid = d_out + second_scale * (
        dn_two - second_hat * jnp.mean(dn_two * second_hat, axis=1, keepdims=True)
    )
    dhid[...] = d_hid
    ag4[0] = d_hid.astype(BF)
    ag_start(ag4, 3)

    ag_done(ag3, 2)
    ghead[...] = jnp.zeros_like(ghead)

    def piece_at(item, out, rows, rank, cut=None):
        u = unit(rank)
        start, size = (0, rows) if cut is None else (cut * (rows // 2), rows // 2)
        if item == 0:
            return out.at[u, pl.ds(start, size), :]
        if item > 2:
            return out.at[u, pl.ds(start, size), all_q if item == 3 else all_kv]
        first = pl.multiple_of(lax.rem(u, GPF) * rows + start, rows // 2)
        return out.at[pl.ds(first, size), :]

    def has(item, rank, fn):
        if item in (0, 3, 4):
            fn()
        else:
            pl.when(unit(rank) // GPF == f)(fn)

    def fin_copy(item, src, dst, sem, to):
        return remote(src, dst, fin_s.at[item, sem], fin_r.at[item, sem], to, f)

    def fin_start(item, src, out, rows):
        def go():
            dst = piece_at(item, out, rows, t)
            fin_copy(item, src, dst, 2, xn).start()
            fin_copy(item, src, dst, 4, yn).start()
            fin_copy(item, src, dst, 1, sib).start()
            pltpu.make_async_copy(src, dst, fin_s.at[item, 0]).start()

        has(item, t, go)

    def fin_step(item, out, rows, k):
        rank = flip(k)
        full = piece_at(item, out, rows, rank)

        def go():
            if k < 6:
                wait_recv(full, fin_r.at[item, k])
                part = piece_at(item, out, rows, rank, k // 4)
                fin_copy(item, part, part, 4 + k, yn if k == 2 else xn).start()
            else:
                wait_recv(piece_at(item, out, rows, rank, 0), fin_r.at[item, 6])
                wait_recv(piece_at(item, out, rows, rank, 1), fin_r.at[item, 8])
            fin_copy(item, full, full, k + 1, sib).start()

        has(item, rank, go)

    def fin_end(item, src, out, rows):
        for k in (1, 3, 5, 7):
            full = piece_at(item, out, rows, flip(k))
            has(item, flip(k), lambda: wait_recv(full, fin_r.at[item, k]))

        def mine():
            for k in (1, 2, 4):
                wait_send(src, fin_s.at[item, k])
            pltpu.make_async_copy(src, piece_at(item, out, rows, t), fin_s.at[item, 0]).wait()

        has(item, t, mine)
        for k in (2, 4, 6):
            full = piece_at(item, out, rows, flip(k))
            part = piece_at(item, out, rows, flip(k), 0)

            def passed():
                wait_send(full, fin_s.at[item, k + 1])
                if k < 6:
                    wait_send(part, fin_s.at[item, 4 + k])

            has(item, flip(k), passed)

    gu_piece = wgu.at[own(Dz), :]
    q_piece, kv_piece = wqkv.at[own(Dz), all_q], wqkv.at[own(Dz), all_kv]
    go_piece = st.at[0]

    def grad_out(m, carry):
        at = pl.ds(pl.multiple_of(m * step, step), step)
        left, right = att[...], ag4[:, :, at]
        total = mm_tn(
            left.reshape(T * B, left.shape[2]), right.reshape(T * B, right.shape[2])
        )
        st[0, :, at] = total.astype(BF)
        return carry

    def backward_block(i, carry):
        ag_step(ag4, 3, i)

        @pl.when(i == 0)
        def _():
            if F > 2:
                hops_step(0, wgu, zr_gu, 2)

        @pl.when(i == 2)
        def _():
            for n in range(3, F):
                hops_step(0, wgu, zr_gu, n)

        @pl.when(i == 3)
        def _():
            row_hops_step(1, wd, zr_d, 1)

        @pl.when(i == 6)
        def _():
            hops_total(0, wgu, zr_gu)
            fin_start(0, gu_piece, ggu_out, Dz)

        @pl.when(i == 6)
        def _():
            for n in range(2, F - 1):
                row_hops_step(1, wd, zr_d, n)

        @pl.when(i == 7)
        def _():
            lax.fori_loop(0, D // step, grad_out, 0)
            row_hops_start(2, go_piece, zr_o)

        cos, sin = turns(i)
        d_att = mm_nt(ag4[i], wo[...]).astype(BF)
        k_rot = rot[i, :, QT : QT + HEAD]
        v = rot[i, :, QT + HEAD : QT + 2 * HEAD]
        d_v = jnp.zeros((B, HEAD), F32)
        d_k = jnp.zeros((B, HEAD), F32)
        d_pre = []
        sums = []

        def norm_back(grad, n, gain):
            x = qkpre[i, :, n * HEAD : (n + 1) * HEAD]
            scale = head_scale(x)
            hat = x * scale
            dn = rotate(grad, cos, -sin)
            total = jnp.sum(dn * hat, axis=0, keepdims=True)
            dn = dn * gain
            back = scale * (dn - hat * jnp.mean(dn * hat, axis=1, keepdims=True))
            return back.astype(BF), total

        for n in range(2):
            prob = probs[i, n * B : (n + 1) * B, :]
            q_rot = rot[i, :, n * HEAD : (n + 1) * HEAD]
            d_head = d_att[:, n * HEAD : (n + 1) * HEAD]
            d_prob = mm_nt(d_head, v)
            p32 = prob.astype(F32)
            center = jnp.sum(p32 * d_prob, axis=1, keepdims=True)
            d_score = (p32 * (d_prob - center)).astype(BF)
            d_v = d_v + mm_tn(prob, d_head)
            d_k = d_k + mm_tn(d_score, q_rot)
            back, total = norm_back(mm(d_score, k_rot) * score_scale, n, gain_q)
            d_pre.append(back)
            sums.append(total)
        back, total = norm_back(d_k * score_scale, 2, gain_k)
        d_pre.append(back)
        d_pre.append(d_v.astype(BF))
        ghead[0:1, :] += sums[0] + sums[1]
        ghead[1:2, :] += total
        for n in range(4):
            rot[i, :, n * HEAD : (n + 1) * HEAD] = d_pre[n]
        ag3[i] = mm_nt(rot[i], wqkv[...]).astype(BF)
        @pl.when(lax.rem(i, 2) == 1)
        def _():
            sib_send(ag3, 3, 1, i)

        for when, p in ((4, 1), (6, 2)):

            @pl.when(i == when)
            def _():
                relay_send(ag3, 3, 1, p, 1)

        for when, p, first in ((3, 1, 0), (3, 2, 0)):

            @pl.when(i == when)
            def _():
                relay_send(ag2, 2, 0, p, first)

        return carry

    lax.fori_loop(0, T, backward_block, 0)
    relay_send(ag3, 3, 1, 3, 1)
    cols_done(0, wqkv, Dz)
    rows_done(1, wo)

    def grad_qkv(m, carry):
        at = pl.ds(pl.multiple_of(m * step, step), step)
        left, right = ag1[:, 0:B, at], rot[...]
        total = mm_tn(
            left.reshape(T * B, left.shape[2]), right.reshape(T * B, right.shape[2])
        )
        wqkv[at, :] = total.astype(BF)
        return carry

    lax.fori_loop(0, D // step, grad_qkv, 0)
    scatter(3, wqkv, zr_qkv, all_q)
    scatter(4, wqkv, zr_qkv, all_kv)
    relay_send(ag3, 3, 1, 1, 0)
    relay_send(ag3, 3, 1, 2, 0)

    row_hops_total(1, wd, zr_d)
    fin_start(1, wd, gd_out, FT)
    row_hops_step(2, go_piece, zr_o, 1)
    for k in (2, 4):
        fin_step(0, ggu_out, Dz, k)

    pre_one = relay_total(ag3, 3, 1)
    tokens = tok_ref[...].astype(F32)
    first_scale = lax.rsqrt(jnp.mean(tokens * tokens, axis=1, keepdims=True) + EPS)
    first_hat = tokens * first_scale
    grad_one = jnp.sum(pre_one * first_hat, axis=0, keepdims=True)
    dn_one = pre_one * gain_one
    dtok_out[...] = (
        dhid[...]
        + first_scale
        * (dn_one - first_hat * jnp.mean(dn_one * first_hat, axis=1, keepdims=True))
    ).astype(BF)
    vz[f, 0:1, :] = grad_one
    vz[f, 1:2, :] = grad_two
    vz[f, 2:3, :] = jnp.concatenate(
        [ghead[0:1, :], ghead[1:2, :], jnp.zeros((1, D - 2 * HEAD), F32)], axis=1
    )
    vz[f, 3:8, :] = jnp.zeros((5, D), F32)

    def vec_send(d, to, _):
        remote(vz.at[f], vz.at[f], vz_s.at[d], vz_r.at[d], r, to).start()

    others(vec_send)
    for n in range(2, F - 1):
        row_hops_step(2, go_piece, zr_o, n)
    fin_step(0, ggu_out, Dz, 6)
    for k in (2, 4):
        fin_step(1, gd_out, FT, k)
    out = hidden[...] + relay_total(ag2, 2, 0)
    mixed_out[...] = jnp.where(live, out, 0.0).astype(BF)
    scatter_total(3, wqkv, zr_qkv, all_q)
    fin_start(3, q_piece, gqkv_out, Dz)

    def vec_recv(d, to, fs):
        wait_recv(vz.at[fs], vz_r.at[d])

    others(vec_recv)
    total = vz[0]
    for j in range(1, F):
        total = total + vz[j]
    vp[t] = total
    for k in range(1, T):
        remote(vp.at[t], vp.at[t], vp_s.at[k], vp_r.at[k], base + flip(k), f).start()
    row_hops_total(2, go_piece, zr_o)
    fin_start(2, go_piece, go_out, QT)
    fin_step(1, gd_out, FT, 6)
    scatter_total(4, wqkv, zr_qkv, all_kv)
    fin_start(4, kv_piece, gqkv_out, Dz)
    for k in range(1, T):
        wait_recv(vp.at[flip(k)], vp_r.at[k])
    total = vp[0]
    for j in range(1, T):
        total = total + vp[j]
    mine = jnp.zeros((8, Dz), F32)
    for j in range(F):
        mine = mine + jnp.where(f == j, total[:, j * Dz : (j + 1) * Dz], 0.0)
    vec_out[:, 0:Dz] = mine
    vec_out[:, Dz : Dz + 2 * HEAD] = total[:, 0 : 2 * HEAD]
    for k in (2, 4, 6):
        fin_step(3, gqkv_out, Dz, k)
        fin_step(2, go_out, QT, k)
        fin_step(4, gqkv_out, Dz, k)
    fin_end(0, gu_piece, ggu_out, Dz)
    fin_end(1, wd, gd_out, FT)
    fin_end(3, q_piece, gqkv_out, Dz)
    fin_end(2, go_piece, go_out, QT)
    fin_end(4, kv_piece, gqkv_out, Dz)

    ag_done(ag1, 0)
    ag_done(ag4, 3)
    relay_done(ag2, 2)
    relay_done(ag3, 3)
    hops_done(0, wgu)
    scatter_done(3, wqkv, all_q)
    scatter_done(4, wqkv, all_kv)
    row_hops_done(1, wd)
    row_hops_done(2, go_piece)
    for d in range(1, F):
        wait_send(normsb.at[0], nz_s.at[d])
        wait_send(vz.at[0], vz_s.at[d])
    for k in range(1, T):
        wait_send(vp.at[0], vp_s.at[k])


def finish_kernel(
    scale, gqkv, ggu, go, gd, vec, mixed, dtok, oq, ok, ov, og, ou, oo, od, o1, o2, oh, om, ot
):
    n = gqkv.shape[0]
    w, v = oq.shape[1] // n, og.shape[1] // n
    for i in range(n):
        x = gqkv[i].astype(F32) * scale
        oq[:, i * w : (i + 1) * w] = x[:, 0:w]
        ok[:, i * HEAD : (i + 1) * HEAD] = x[:, w : w + HEAD]
        ov[:, i * HEAD : (i + 1) * HEAD] = x[:, w + HEAD : w + 2 * HEAD]
        x = ggu[i].astype(F32) * scale
        og[:, i * v : (i + 1) * v] = x[:, 0:v]
        ou[:, i * v : (i + 1) * v] = x[:, v : 2 * v]
    oo[...] = go[...].astype(F32) * scale
    od[...] = gd[...].astype(F32) * scale
    om[...] = mixed[...]
    ot[...] = dtok[...]

    @pl.when(pl.program_id(0) == 0)
    def _():
        w = o1.shape[1]
        o1[...] = vec[0:1, 0:w] * scale
        o2[...] = vec[1:2, 0:w] * scale
        oh[0:1, :] = vec[2:3, w : w + HEAD] * scale
        oh[1:2, :] = vec[2:3, w + HEAD : w + 2 * HEAD] * scale


def per_device(
    F,
    G,
    tokens,
    doc_lengths,
    attn_norm,
    w_query,
    key_matrix,
    value_matrix,
    head_norms,
    w_out,
    ffn_norm,
    w_gate,
    w_up,
    w_down,
    cotangent,
):
    B, D = tokens.shape
    Dz = D // F
    QW, KW, FF = w_query.shape[1], key_matrix.shape[1], w_gate.shape[1]
    QT, FT = QW // T, FF // T
    QZ, FZ = w_out.shape[0], w_down.shape[0]
    norms = jnp.zeros((8, Dz), F32)
    norms = norms.at[0].set(attn_norm.astype(F32)).at[1].set(ffn_norm.astype(F32))
    table = jnp.asarray(rope_table(B))
    vmem = pl.BlockSpec(memory_space=pltpu.VMEM)
    hbm = pl.BlockSpec(memory_space=pl.ANY)
    dma = pltpu.SemaphoreType.DMA
    sds = jax.ShapeDtypeStruct
    outs = pl.pallas_call(
        functools.partial(layer_kernel, F, B, D),
        out_shape=(
            sds((T, Dz, QT + 2 * HEAD), BF),
            sds((T, Dz, 2 * FT), BF),
            sds((QZ, D), BF),
            sds((FZ, D), BF),
            sds((8, Dz + 2 * HEAD), F32),
            sds((B, D), BF),
            sds((B, D), BF),
        ),
        in_specs=[vmem, vmem, pl.BlockSpec(memory_space=pltpu.SMEM), vmem, vmem, vmem] + [hbm] * 7,
        out_specs=(hbm, hbm, hbm, hbm, vmem, vmem, vmem),
        scratch_shapes=[
            pltpu.VMEM((T, B + 16, D), BF),
            pltpu.VMEM((T, B, D), BF),
            pltpu.VMEM((T, B, D), BF),
            pltpu.VMEM((T, B, D), BF),
            pltpu.VMEM((T, B, D), BF),
            pltpu.VMEM((2, 4, B, D), BF),
            pltpu.VMEM((2, 3, B, D), BF),
            pltpu.VMEM((D, QT + 2 * HEAD), BF),
            pltpu.VMEM((D, 2 * FT), BF),
            pltpu.VMEM((QT, D), BF),
            pltpu.VMEM((FT, D), BF),
            pltpu.VMEM((T, B, QT + HEAD), F32),
            pltpu.VMEM((T, B, QT + 2 * HEAD), BF),
            pltpu.VMEM((T, 2 * B, B), BF),
            pltpu.VMEM((T, B, QT), BF),
            pltpu.VMEM((T, B, 3 * FT), BF),
            pltpu.VMEM((B, D), F32),
            pltpu.VMEM((B, D), F32),
            pltpu.VMEM((F, 8, Dz), F32),
            pltpu.VMEM((F + 1, Dz, 2 * FT), BF),
            pltpu.VMEM((2, FT, D), BF),
            pltpu.VMEM((2, QT, D), BF),
            pltpu.VMEM((F, Dz, QT + 2 * HEAD), BF),
            pltpu.VMEM((F, 8, D), F32),
            pltpu.VMEM((T, 8, D), F32),
            pltpu.VMEM((8, HEAD), F32),
            pltpu.VMEM((T, B, HEAD), F32),
            dma((4, 9)),
            dma((4, 9)),
            dma((4, 4)),
            dma((4, 4)),
            dma((4, 6)),
            dma((4, 6)),
            dma((4, 2, F)),
            dma((4, 2, F)),
            dma((F,)),
            dma((F,)),
            dma((8,)),
            dma((5, 2, F)),
            dma((5, 2, F)),
            dma((5, 9)),
            dma((5, 9)),
            dma((F,)),
            dma((F,)),
            dma((T,)),
            dma((T,)),
        ],
        compiler_params=pltpu.CompilerParams(
            collective_id=0, has_side_effects=True, vmem_limit_bytes=62 * 2**20
        ),
    )(
        tokens,
        cotangent,
        doc_lengths,
        norms,
        head_norms,
        table,
        w_query,
        key_matrix,
        value_matrix,
        w_out,
        w_gate,
        w_up,
        w_down,
    )
    gqkv, ggu, go, gd, vec, mixed, d_tokens = outs
    if G > 1:
        groups = [[t + T * n for n in range(G)] for t in range(T)]
        gqkv, ggu, go, gd = (
            lax.psum(x, "rep", axis_index_groups=groups) for x in (gqkv, ggu, go, gd)
        )
        vec = lax.psum(vec, "rep", axis_index_groups=groups)
    scale = 1.0 / math.sqrt(B * T * G * F)

    steps = 4
    n = T // steps
    qb, fb = QZ // steps, FZ // steps
    bb = B // steps
    oq, ok, ov, og, ou, oo, od, o1, o2, oh, mixed, d_tokens = pl.pallas_call(
        functools.partial(finish_kernel, scale),
        grid=(steps,),
        out_shape=(
            sds((Dz, QW), F32),
            sds((Dz, KW), F32),
            sds((Dz, KW), F32),
            sds((Dz, FF), F32),
            sds((Dz, FF), F32),
            sds((QZ, D), F32),
            sds((FZ, D), F32),
            sds((1, Dz), F32),
            sds((1, Dz), F32),
            sds((2, HEAD), F32),
            sds((B, D), BF),
            sds((B, D), BF),
        ),
        in_specs=[
            pl.BlockSpec((n, Dz, QT + 2 * HEAD), lambda u: (u, 0, 0)),
            pl.BlockSpec((n, Dz, 2 * FT), lambda u: (u, 0, 0)),
            pl.BlockSpec((qb, D), lambda u: (u, 0)),
            pl.BlockSpec((fb, D), lambda u: (u, 0)),
            pl.BlockSpec((8, Dz + 2 * HEAD), lambda u: (0, 0)),
            pl.BlockSpec((bb, D), lambda u: (u, 0)),
            pl.BlockSpec((bb, D), lambda u: (u, 0)),
        ],
        out_specs=(
            pl.BlockSpec((Dz, n * QT), lambda u: (0, u)),
            pl.BlockSpec((Dz, n * HEAD), lambda u: (0, u)),
            pl.BlockSpec((Dz, n * HEAD), lambda u: (0, u)),
            pl.BlockSpec((Dz, n * FT), lambda u: (0, u)),
            pl.BlockSpec((Dz, n * FT), lambda u: (0, u)),
            pl.BlockSpec((qb, D), lambda u: (u, 0)),
            pl.BlockSpec((fb, D), lambda u: (u, 0)),
            pl.BlockSpec((1, Dz), lambda u: (0, 0)),
            pl.BlockSpec((1, Dz), lambda u: (0, 0)),
            pl.BlockSpec((2, HEAD), lambda u: (0, 0)),
            pl.BlockSpec((bb, D), lambda u: (u, 0)),
            pl.BlockSpec((bb, D), lambda u: (u, 0)),
        ),
    )(gqkv, ggu, go, gd, vec, mixed, d_tokens)
    return (
        mixed,
        d_tokens,
        o1.reshape(Dz),
        oq,
        ok,
        ov,
        oh,
        oo,
        o2.reshape(Dz),
        og,
        ou,
        od,
    )


def solution(mesh):
    F = mesh.shape["fsdp"]
    G = mesh.shape["rep"] // T
    rows = P(("rep", "fsdp"), None)
    mat = P("fsdp", None)
    vec = P("fsdp")
    return jax.shard_map(
        functools.partial(per_device, F, G),
        mesh=mesh,
        in_specs=(rows, rows, vec, mat, mat, mat, P(), mat, vec, mat, mat, mat, rows),
        out_specs=(rows, rows, vec, mat, mat, mat, P(), mat, vec, mat, mat, mat),
        check_vma=False,
    )
```

```python
import functools
import math

import jax
import jax.numpy as jnp
import numpy as np
from jax import lax
from jax.experimental import pallas as pl
from jax.experimental.pallas import tpu as pltpu
from jax.sharding import PartitionSpec as P

EPS = 1e-06
ROPE_BASE = 1000000.0
NEG_FILL = -1e30
HEAD = 128
T = 8
MESH = pl.DeviceIdType.MESH
BF = jnp.bfloat16
F32 = jnp.float32


def mm(a, b):
    return lax.dot_general(a, b, (((1,), (0,)), ((), ())), preferred_element_type=F32)


def mm_nt(a, b):
    return lax.dot_general(a, b, (((1,), (1,)), ((), ())), preferred_element_type=F32)


def mm_tn(a, b):
    return lax.dot_general(a, b, (((0,), (0,)), ((), ())), preferred_element_type=F32)


def rope_table(rows):
    half = HEAD // 2
    freq = np.exp(np.arange(half, dtype=np.float64) * (-2.0 * math.log(ROPE_BASE) / HEAD))
    freq = freq.astype(np.float32)
    angle = (np.arange(rows, dtype=np.float32)[:, None] * freq[None, :]).astype(np.float64)
    cos, sin = np.cos(angle), np.sin(angle)
    full = np.concatenate([cos, sin], axis=1).astype(np.float32)
    parts = []
    rest = full
    for _ in range(3):
        part = rest.astype(jnp.bfloat16)
        parts.append(part)
        rest = rest - part.astype(np.float32)
    return np.concatenate(parts, axis=1)


def layer_kernel(
    F,
    B,
    D,
    tok_ref,
    cot_ref,
    doc_ref,
    norms_ref,
    hn_ref,
    table_ref,
    wq_ref,
    wk_ref,
    wv_ref,
    wo_ref,
    wg_ref,
    wu_ref,
    wd_ref,
    gqkv_out,
    ggu_out,
    go_out,
    gd_out,
    vec_out,
    mixed_out,
    dtok_out,
    ag1,
    ag2,
    ag3,
    ag4,
    st,
    sr,
    rr,
    wqkv,
    wgu,
    wo,
    wd,
    qkpre,
    rot,
    probs,
    att,
    actd,
    hidden,
    dhid,
    normsb,
    zr_gu,
    zr_d,
    zr_o,
    zr_qkv,
    vz,
    vp,
    ghead,
    turn,
    ag_s,
    ag_r,
    sib_s,
    sib_r,
    rem_s,
    rem_r,
    w_s,
    w_r,
    nz_s,
    nz_r,
    loc_s,
    zg_s,
    zg_r,
    fin_s,
    fin_r,
    vz_s,
    vz_r,
    vp_s,
    vp_r,
):
    Dz = D // F
    QT = wo.shape[0]
    FT = wd.shape[0]
    GPF = T // F
    half = B // 2
    r = lax.axis_index("rep")
    f = lax.axis_index("fsdp")
    t = lax.rem(r, T)
    base = r - t
    core = lax.rem(t, 2)
    chip = t // 2
    b1 = lax.rem(chip, 2)
    b2 = chip // 2

    def flip(k):
        x = core + (k % 2) * (1 - 2 * core)
        y = b1 + ((k // 2) % 2) * (1 - 2 * b1)
        z = b2 + (k // 4) * (1 - 2 * b2)
        return x + 2 * y + 4 * z

    def unit(rank):
        return lax.rem(rank, 2) * (T // 2) + rank // 2

    g = unit(t)
    fg = g // GPF
    grow = lax.rem(g, GPF)
    sib, xn, yn, dg = base + flip(1), base + flip(2), base + flip(4), base + flip(6)

    def remote(src, dst, ssem, rsem, rep, fs):
        return pltpu.make_async_remote_copy(
            src_ref=src,
            dst_ref=dst,
            send_sem=ssem,
            recv_sem=rsem,
            device_id={"rep": rep, "fsdp": fs},
            device_id_type=MESH,
        )

    def wait_recv(dst, rsem):
        remote(dst, dst, rsem, rsem, sib, f).wait_recv()

    def wait_send(src, ssem):
        remote(src, src, ssem, ssem, sib, f).wait_send()

    barrier = pltpu.get_barrier_semaphore()
    for k in range(1, T):
        pl.semaphore_signal(
            barrier, inc=1, device_id={"rep": base + flip(k), "fsdp": f}, device_id_type=MESH
        )
    for d in range(1, F):
        pl.semaphore_signal(
            barrier, inc=1, device_id={"rep": r, "fsdp": lax.rem(f + d, F)}, device_id_type=MESH
        )

    def own(n):
        return pl.ds(pl.multiple_of(f * n, n), n)

    gq = pl.ds(pl.multiple_of(g * QT, QT), QT)
    gk = pl.ds(pl.multiple_of(g * HEAD, HEAD), HEAD)
    gf = pl.ds(pl.multiple_of(g * FT, HEAD), FT)
    loads = [
        pltpu.make_async_copy(wq_ref.at[:, gq], wqkv.at[own(Dz), pl.ds(0, QT)], loc_s.at[0]),
        pltpu.make_async_copy(wk_ref.at[:, gk], wqkv.at[own(Dz), pl.ds(QT, HEAD)], loc_s.at[1]),
        pltpu.make_async_copy(
            wv_ref.at[:, gk], wqkv.at[own(Dz), pl.ds(QT + HEAD, HEAD)], loc_s.at[2]
        ),
        pltpu.make_async_copy(wg_ref.at[:, gf], wgu.at[own(Dz), pl.ds(0, FT)], loc_s.at[3]),
        pltpu.make_async_copy(wu_ref.at[:, gf], wgu.at[own(Dz), pl.ds(FT, FT)], loc_s.at[4]),
    ]
    for c in loads:
        c.start()

    def row_load(src, dst, rows, sem):
        return pltpu.make_async_copy(
            src.at[pl.ds(pl.multiple_of(grow * rows, rows), rows), :], dst, sem
        )

    @pl.when(f == fg)
    def _():
        row_load(wo_ref, wo, QT, loc_s.at[5]).start()
        row_load(wd_ref, wd, FT, loc_s.at[6]).start()

    normsb[f] = norms_ref[...]
    pl.semaphore_wait(barrier, T - 1 + F - 1)

    def others(fn):
        for d in range(1, F):
            fn(d, lax.rem(f + d, F), lax.rem(f + F - d, F))

    def norms_send(d, to, _):
        remote(normsb.at[f], normsb.at[f], nz_s.at[d], nz_r.at[d], r, to).start()

    others(norms_send)

    def line_copy(item, buf, rows, s, up, m, to):
        part = buf.at[pl.ds(pl.multiple_of(s * rows, rows), rows), :]
        return remote(part, part, w_s.at[item, up, m], w_r.at[item, up, m], r, to)

    def cols_start(item, buf, rows):
        @pl.when(f < F - 1)
        def _():
            line_copy(item, buf, rows, f, 1, 1, f + 1).start()

        @pl.when(f > 0)
        def _():
            line_copy(item, buf, rows, f, 0, 1, f - 1).start()

    def cols_step(item, buf, rows, m):
        @pl.when(f >= m)
        def _():
            line_copy(item, buf, rows, f - m, 1, m, r * 0).wait_recv()
            if m + 1 < F:

                @pl.when(f < F - 1)
                def _():
                    line_copy(item, buf, rows, f - m, 1, m + 1, f + 1).start()

        @pl.when(f + m < F)
        def _():
            line_copy(item, buf, rows, f + m, 0, m, r * 0).wait_recv()
            if m + 1 < F:

                @pl.when(f > 0)
                def _():
                    line_copy(item, buf, rows, f + m, 0, m + 1, f - 1).start()

    def cols_done(item, buf, rows):
        for m in range(1, F):

            @pl.when((f < F - 1) & (f >= m - 1))
            def _():
                line_copy(item, buf, rows, f, 1, m, r * 0).wait_send()

            @pl.when((f > 0) & (f + m - 1 < F))
            def _():
                line_copy(item, buf, rows, f, 0, m, r * 0).wait_send()

    def row_copy(item, buf, up, to):
        return remote(buf, buf, w_s.at[item, up, 0], w_r.at[item, up, 0], r, to)

    def rows_start(item, buf):
        @pl.when((f == fg) & (f < F - 1))
        def _():
            row_copy(item, buf, 1, f + 1).start()

        @pl.when((f == fg) & (f > 0))
        def _():
            row_copy(item, buf, 0, f - 1).start()

    def rows_step(item, buf, m):
        @pl.when(f - fg == m)
        def _():
            row_copy(item, buf, 1, r * 0).wait_recv()

            @pl.when(f < F - 1)
            def _():
                row_copy(item, buf, 1, f + 1).start()

        @pl.when(fg - f == m)
        def _():
            row_copy(item, buf, 0, r * 0).wait_recv()

            @pl.when(f > 0)
            def _():
                row_copy(item, buf, 0, f - 1).start()

    def rows_done(item, buf):
        @pl.when((f >= fg) & (f < F - 1))
        def _():
            row_copy(item, buf, 1, r * 0).wait_send()

        @pl.when((f <= fg) & (f > 0))
        def _():
            row_copy(item, buf, 0, r * 0).wait_send()

    for c in loads[:3]:
        c.wait()
    cols_start(0, wqkv, Dz)

    @pl.when(f == fg)
    def _():
        row_load(wo_ref, wo, QT, loc_s.at[5]).wait()
        row_load(wd_ref, wd, FT, loc_s.at[6]).wait()

    rows_start(1, wo)

    def ag_start(buf, a):
        remote(buf.at[0], buf.at[2], ag_s.at[a, 2], ag_r.at[a, 2], xn, f).start()
        remote(buf.at[0], buf.at[4], ag_s.at[a, 4], ag_r.at[a, 4], yn, f).start()
        remote(buf.at[0], buf.at[1], ag_s.at[a, 1], ag_r.at[a, 1], sib, f).start()

    def ag_cut(buf, slot, lower):
        rows = buf.shape[1]
        return buf.at[slot, pl.ds(half, rows - half), :] if lower else buf.at[slot, pl.ds(0, half), :]

    def ag_pass(buf, a, slot):
        remote(
            buf.at[slot], buf.at[slot + 1], ag_s.at[a, slot + 1], ag_r.at[a, slot + 1], sib, f
        ).start()

    def ag_step(buf, a, i):
        @pl.when(i == 1)
        def _():
            wait_recv(buf.at[1], ag_r.at[a, 1])

        @pl.when(i == 2)
        def _():
            wait_recv(buf.at[2], ag_r.at[a, 2])
            remote(
                ag_cut(buf, 2, 0), ag_cut(buf, 6, 0), ag_s.at[a, 6], ag_r.at[a, 6], yn, f
            ).start()
            ag_pass(buf, a, 2)

        @pl.when(i == 3)
        def _():
            wait_recv(buf.at[4], ag_r.at[a, 4])
            remote(
                ag_cut(buf, 4, 1), ag_cut(buf, 6, 1), ag_s.at[a, 8], ag_r.at[a, 8], xn, f
            ).start()
            ag_pass(buf, a, 4)
            wait_recv(buf.at[3], ag_r.at[a, 3])

        @pl.when(i == 5)
        def _():
            wait_recv(buf.at[5], ag_r.at[a, 5])

        @pl.when(i == 6)
        def _():
            wait_recv(ag_cut(buf, 6, 0), ag_r.at[a, 6])
            wait_recv(ag_cut(buf, 6, 1), ag_r.at[a, 8])
            ag_pass(buf, a, 6)

        @pl.when(i == 7)
        def _():
            wait_recv(buf.at[7], ag_r.at[a, 7])

    def ag_done(buf, a):
        for k in (1, 2, 3, 4, 5, 7):
            wait_send(buf.at[0], ag_s.at[a, k])
        wait_send(ag_cut(buf, 6, 0), ag_s.at[a, 6])
        wait_send(ag_cut(buf, 6, 1), ag_s.at[a, 8])

    def rs_step(buf, q, s, i):
        @pl.when(lax.rem(i, 2) == 1)
        def _():
            sib_send(buf, q, s, i)

        @pl.when((lax.rem(i, 2) == 0) & (i >= 4))
        def _():
            rs_send(buf, q, s, i // 2 - 1)

    def rs_send(buf, q, s, p):
        wait_recv(sr.at[s, p], sib_r.at[q, p])
        buf[2 * p] = (buf[2 * p].astype(F32) + sr[s, p].astype(F32)).astype(BF)
        low = lax.rem(p, 2)
        high = p // 2
        to = r + low * (2 - 4 * b1) + high * (4 - 8 * b2)
        remote(buf.at[2 * p], rr.at[s, p - 1], rem_s.at[q, p], rem_r.at[q, p], to, f).start()

    def rs_total(buf, q, s):
        wait_recv(sr.at[s, 0], sib_r.at[q, 0])
        total = buf[0].astype(F32) + sr[s, 0].astype(F32)
        for p in range(1, 4):
            wait_recv(rr.at[s, p - 1], rem_r.at[q, p])
            total = total + rr[s, p - 1].astype(F32)
        return total

    def rs_done(buf, q):
        for p in range(4):
            wait_send(buf.at[2 * p + 1], sib_s.at[q, p])
            if p > 0:
                wait_send(buf.at[2 * p], rem_s.at[q, p])

    upper, lower = pl.ds(0, half), pl.ds(half, half)

    def relay_send(buf, q, s, p, own):
        at = 2 * p
        if p == 3:
            wait_recv(sr.at[s, p], sib_r.at[q, p])
            buf[at] = (buf[at].astype(F32) + sr[s, p].astype(F32)).astype(BF)
            for cut, to, sem in ((upper, xn, 3), (lower, yn, 0)):
                remote(
                    buf.at[at, cut, :], rr.at[s, 2, cut, :], rem_s.at[q, sem], rem_r.at[q, sem], to, f
                ).start()
            return
        keep, add, to, sem = (upper, lower, xn, 0) if p == 1 else (lower, upper, yn, 3)
        cut = keep if own else add
        if own:
            wait_recv(sr.at[s, p], sib_r.at[q, p])
        else:
            wait_recv(rr.at[s, 2, add, :], rem_r.at[q, sem])
        total = buf[at, cut, :].astype(F32) + sr[s, p, cut, :].astype(F32)
        if not own:
            total = total + rr[s, 2, add, :].astype(F32)
        buf[at, cut, :] = total.astype(BF)
        sem = p if own else p + 3
        remote(
            buf.at[at, cut, :], rr.at[s, p - 1, cut, :], rem_s.at[q, sem], rem_r.at[q, sem], to, f
        ).start()

    def relay_total(buf, q, s):
        wait_recv(sr.at[s, 0], sib_r.at[q, 0])
        for sem in (1, 2, 4, 5):
            wait_recv(rr.at[s, 0, upper, :], rem_r.at[q, sem])
        return (
            buf[0].astype(F32)
            + sr[s, 0].astype(F32)
            + rr[s, 0].astype(F32)
            + rr[s, 1].astype(F32)
        )

    def relay_done(buf, q):
        for p in range(4):
            wait_send(buf.at[2 * p + 1], sib_s.at[q, p])
        for sem in range(6):
            wait_send(buf.at[6, upper, :], rem_s.at[q, sem])

    def sib_send(buf, q, s, i):
        remote(
            buf.at[i], sr.at[s, i // 2], sib_s.at[q, i // 2], sib_r.at[q, i // 2], sib, f
        ).start()

    row_ids = lax.broadcasted_iota(jnp.int32, (B, 1), 0)
    lanes_b = lax.broadcasted_iota(jnp.int32, (1, D), 1)
    end = doc_ref[0, 0]
    meta = jnp.where(lanes_b == 0, end, 0)
    slots = doc_ref.shape[1]
    for i in range(1, slots):
        end = end + doc_ref[0, i]
        meta = meta + jnp.where(lanes_b == i, end, 0)
    live = row_ids < end
    tokens = tok_ref[...].astype(F32)
    first_scale = lax.rsqrt(jnp.mean(tokens * tokens, axis=1, keepdims=True) + EPS)

    def norms_wait(d, _, fs):
        wait_recv(normsb.at[fs], nz_r.at[d])

    others(norms_wait)
    gain_one = jnp.concatenate([normsb[j, 0:1, :] for j in range(F)], axis=1)
    gain_two = jnp.concatenate([normsb[j, 1:2, :] for j in range(F)], axis=1)
    ag1[0, 0:B, :] = (tokens * first_scale * gain_one).astype(BF)
    ag1[0, B : B + 16, :] = jnp.broadcast_to(meta.astype(F32), (16, D)).astype(BF)
    ag_start(ag1, 0)
    ag3[0] = jnp.where(live, cot_ref[...].astype(F32), 0.0).astype(BF)

    gain_q = hn_ref[0:1, :].astype(F32)
    gain_k = hn_ref[1:2, :].astype(F32)
    score_scale = HEAD ** (-0.5)

    def block_layout(i):
        ends = ag1[i, B : B + 16, :][0:1, 0:HEAD].astype(F32)
        rows = lax.broadcasted_iota(jnp.int32, (B, 1), 0).astype(F32)
        cols = lax.broadcasted_iota(jnp.int32, (1, B), 1).astype(F32)
        seg_row = jnp.zeros((B, 1), F32)
        seg_col = jnp.zeros((1, B), F32)
        start = jnp.zeros((B, 1), F32)
        for n in range(slots):
            e = ends[:, n : n + 1]
            past = rows >= e
            seg_row = seg_row + past.astype(F32)
            seg_col = seg_col + (cols >= e).astype(F32)
            start = jnp.maximum(start, jnp.where(past, e, 0.0))
        alive = rows < ends[:, slots - 1 : slots]
        position = rows - jnp.where(alive, start, 0.0)
        return rows, cols, seg_row, seg_col, alive, position

    def rope_rows(position, cols):
        pick = (cols == position).astype(F32).astype(BF)
        table = mm(pick, table_ref[...])
        return table[:, 0:HEAD] + table[:, HEAD : 2 * HEAD] + table[:, 2 * HEAD : 3 * HEAD]

    def turns(i):
        x = turn[i]
        y = pltpu.roll(x, HEAD // 2, 1)
        first = lax.broadcasted_iota(jnp.int32, x.shape, 1) < HEAD // 2
        return jnp.where(first, x, y), jnp.where(first, -y, x)

    def rotate(x, cos, sin):
        return x * cos + pltpu.roll(x, HEAD // 2, 1) * sin

    def head_scale(x):
        return lax.rsqrt(jnp.mean(x * x, axis=1, keepdims=True) + EPS)

    def prepare(i, carry):
        rows, cols, seg_row, seg_col, alive, position = block_layout(i)
        turn[i] = rope_rows(position, cols)
        allowed = ((seg_row == seg_col) & (cols <= rows) & alive) | (cols == rows)
        ag4[i, :, 0:B] = jnp.where(allowed, 0.0, NEG_FILL).astype(BF)
        return carry

    def wave(m, first):
        cols_step(first, (wqkv, None, wgu)[first], Dz, m)
        rows_step(first + 1, (wo, None, wd)[first], m)

    wave(1, 0)
    for i in (1, 2, 3):
        ag_step(ag1, 0, i)
    for m in range(2, min(F, 3)):
        wave(m, 0)
    ag_start(ag3, 2)
    lax.fori_loop(0, 5, prepare, 0)
    for m in range(3, F):
        wave(m, 0)
    for c in loads[3:]:
        c.wait()
    cols_start(2, wgu, Dz)
    rows_start(3, wd)
    for i in (5, 6, 7):
        ag_step(ag1, 0, i)
    lax.fori_loop(5, T, prepare, 0)

    def forward_block(j, carry):
        pair = j // 2
        pair = pair + 3 * ((3 - pair) // 3) - 3 * (pair // 3)
        i = 2 * pair + lax.rem(j, 2)

        @pl.when(j == 4)
        def _():
            wave(1, 2)

        cos, sin = turns(i)
        pre = mm(ag1[i, 0:B, :], wqkv[...])
        qkpre[i] = pre[:, 0 : QT + HEAD]
        parts = []
        for n in range(3):
            x = pre[:, n * HEAD : (n + 1) * HEAD]
            x = x * head_scale(x) * (gain_q if n < 2 else gain_k)
            parts.append(rotate(x, cos, sin).astype(BF))
        v = pre[:, QT + HEAD : QT + 2 * HEAD].astype(BF)
        for n in range(3):
            rot[i, :, n * HEAD : (n + 1) * HEAD] = parts[n]
        rot[i, :, 3 * HEAD : 4 * HEAD] = v
        mask = ag4[i, :, 0:B].astype(F32)
        for n in range(2):
            scores = mm_nt(parts[n], parts[2]) * score_scale + mask
            expd = jnp.exp(scores - jnp.max(scores, axis=1, keepdims=True))
            prob = (expd * (1.0 / jnp.sum(expd, axis=1, keepdims=True))).astype(BF)
            probs[i, n * B : (n + 1) * B, :] = prob
            att[i, :, n * HEAD : (n + 1) * HEAD] = mm(prob, v).astype(BF)
        st[i] = mm(att[i], wo[...]).astype(BF)

        @pl.when(lax.rem(i, 2) == 1)
        def _():
            sib_send(st, 0, 0, i)

        for when, p, first in ((2, 3, 1), (4, 1, 1), (6, 2, 1), (6, 1, 0), (7, 2, 0)):

            @pl.when(j == when)
            def _():
                relay_send(st, 0, 0, p, first)

        return carry

    lax.fori_loop(0, T, forward_block, 0)
    for i in (1, 2, 3):
        ag_step(ag3, 2, i)
    wave(2, 2)
    hid = tokens + relay_total(st, 0, 0)
    relay_done(st, 0)
    hidden[...] = hid
    second_scale = lax.rsqrt(jnp.mean(hid * hid, axis=1, keepdims=True) + EPS)
    ag2[0] = (hid * second_scale * gain_two).astype(BF)
    ag_start(ag2, 1)
    for i in (5, 6, 7):
        ag_step(ag3, 2, i)
    for m in range(3, F):
        wave(m, 2)

    def ffn_block(i, carry):
        ag_step(ag2, 1, i)
        up_gate = mm(ag2[i], wgu[...])
        gate, up = up_gate[:, 0:FT], up_gate[:, FT : 2 * FT]
        sig = 1.0 / (1.0 + jnp.exp(-gate))
        silu = gate * sig
        actd[i, :, 0:FT] = (silu * up).astype(BF)
        d_act = mm_nt(ag3[i], wd[...])
        actd[i, :, FT : 2 * FT] = (d_act * up * (sig + silu * (1.0 - sig))).astype(BF)
        actd[i, :, 2 * FT : 3 * FT] = (d_act * silu).astype(BF)
        st[i] = mm_nt(actd[i, :, FT : 3 * FT], wgu[...]).astype(BF)
        @pl.when(lax.rem(i, 2) == 1)
        def _():
            sib_send(st, 1, 1, i)

        for when, p in ((4, 1), (6, 2)):

            @pl.when(i == when)
            def _():
                relay_send(st, 1, 1, p, 1)

        return carry

    lax.fori_loop(0, T, ffn_block, 0)
    relay_send(st, 1, 1, 3, 1)
    cols_done(2, wgu, Dz)

    step = 256

    def grad_gu(m, carry):
        at = pl.ds(pl.multiple_of(m * step, step), step)
        left, right = ag2[:, :, at], actd[:, :, FT : 3 * FT]
        total = mm_tn(
            left.reshape(T * B, left.shape[2]), right.reshape(T * B, right.shape[2])
        )
        wgu[at, :] = total.astype(BF)
        return carry

    lax.fori_loop(0, D // step, grad_gu, 0)

    def scatter(item, buf, slots_ref, cut):
        def send(d, to, _):
            at = pl.ds(pl.multiple_of(to * Dz, Dz), Dz)
            remote(
                buf.at[at, cut],
                slots_ref.at[f, :, cut],
                zg_s.at[item, 0, d],
                zg_r.at[item, 0, d],
                r,
                to,
            ).start()

        others(send)

    def scatter_total(item, buf, slots_ref, cut):
        total = buf[own(Dz), cut].astype(F32)
        others(lambda d, to, fs: wait_recv(slots_ref.at[fs, :, cut], zg_r.at[item, 0, d]))
        for d in range(1, F):
            total = total + slots_ref[lax.rem(f + d, F), :, cut].astype(F32)
        buf[own(Dz), cut] = total.astype(BF)

    def scatter_done(item, buf, cut):
        others(lambda d, to, fs: wait_send(buf.at[own(Dz), cut], zg_s.at[item, 0, d]))

    def hop(item, buf, slots_ref, s, up, to):
        slot = s if up else s + (F - s) * (1 - (to - s + F - 1) // F)
        return remote(
            buf.at[pl.ds(pl.multiple_of(s * Dz, Dz), Dz), :],
            slots_ref.at[slot],
            zg_s.at[item, up, s],
            zg_r.at[item, up, s],
            r,
            to,
        )

    def hop_add(item, buf, slots_ref, s, up, slot):
        wait_recv(slots_ref.at[slot], zg_r.at[item, up, s])
        at = pl.ds(pl.multiple_of(s * Dz, Dz), Dz)
        buf[at, :] = (buf[at, :].astype(F32) + slots_ref[slot].astype(F32)).astype(BF)

    def hops_start(item, buf, slots_ref):
        @pl.when(f == 0)
        def _():
            for s in range(F - 1, 0, -1):
                hop(item, buf, slots_ref, s, 1, f + 1).start()

        @pl.when(f == F - 1)
        def _():
            for s in range(F - 1):
                hop(item, buf, slots_ref, s, 0, f - 1).start()

    def hops_step(item, buf, slots_ref, n):
        s = F - n

        @pl.when((f > 0) & (f < s))
        def _():
            hop_add(item, buf, slots_ref, s, 1, s)
            hop(item, buf, slots_ref, s, 1, f + 1).start()

        z = n - 1

        @pl.when((f < F - 1) & (f > z))
        def _():
            hop_add(item, buf, slots_ref, z, 0, z)
            hop(item, buf, slots_ref, z, 0, f - 1).start()

    def hops_total(item, buf, slots_ref):
        @pl.when(f > 0)
        def _():
            hop_add(item, buf, slots_ref, f, 1, f)

        @pl.when(f < F - 1)
        def _():
            hop_add(item, buf, slots_ref, f, 0, F)

    def hops_done(item, buf):
        part = buf.at[pl.ds(0, Dz), :]
        for s in range(F):

            @pl.when(f < s)
            def _():
                wait_send(part, zg_s.at[item, 1, s])

            @pl.when(f > s)
            def _():
                wait_send(part, zg_s.at[item, 0, s])

    def row_hop(item, buf, slots_ref, up, to):
        return remote(buf, slots_ref.at[up], zg_s.at[item, up, 0], zg_r.at[item, up, 0], r, to)

    def row_add(item, buf, slots_ref, up):
        wait_recv(slots_ref.at[up], zg_r.at[item, up, 0])
        buf[...] = (buf[...].astype(F32) + slots_ref[up].astype(F32)).astype(BF)

    def row_hops_start(item, buf, slots_ref):
        @pl.when((f == 0) & (fg > 0))
        def _():
            row_hop(item, buf, slots_ref, 1, f + 1).start()

        @pl.when((f == F - 1) & (fg < F - 1))
        def _():
            row_hop(item, buf, slots_ref, 0, f - 1).start()

    def row_hops_step(item, buf, slots_ref, n):
        @pl.when((f < fg) & (f == n))
        def _():
            row_add(item, buf, slots_ref, 1)
            row_hop(item, buf, slots_ref, 1, f + 1).start()

        @pl.when((f > fg) & (F - 1 - f == n))
        def _():
            row_add(item, buf, slots_ref, 0)
            row_hop(item, buf, slots_ref, 0, f - 1).start()

    def row_hops_total(item, buf, slots_ref):
        @pl.when((f == fg) & (f > 0))
        def _():
            row_add(item, buf, slots_ref, 1)

        @pl.when((f == fg) & (f < F - 1))
        def _():
            row_add(item, buf, slots_ref, 0)

    def row_hops_done(item, buf):
        @pl.when(f < fg)
        def _():
            wait_send(buf, zg_s.at[item, 1, 0])

        @pl.when(f > fg)
        def _():
            wait_send(buf, zg_s.at[item, 0, 0])

    all_q, all_kv = pl.ds(0, QT), pl.ds(QT, 2 * HEAD)
    hops_start(0, wgu, zr_gu)
    ag_done(ag2, 1)

    def down_block(i, carry):
        ag2[i] = mm(actd[i, :, 0:FT], wd[...]).astype(BF)

        @pl.when(lax.rem(i, 2) == 1)
        def _():
            sib_send(ag2, 2, 0, i)

        return carry

    lax.fori_loop(0, T, down_block, 0)
    relay_send(st, 1, 1, 1, 0)
    relay_send(st, 1, 1, 2, 0)
    rows_done(3, wd)

    def grad_down(m, carry):
        at = pl.ds(pl.multiple_of(m * step, step), step)
        left, right = actd[:, :, 0:FT], ag3[:, :, at]
        total = mm_tn(
            left.reshape(T * B, left.shape[2]), right.reshape(T * B, right.shape[2])
        )
        wd[:, at] = total.astype(BF)
        return carry

    lax.fori_loop(0, D // step, grad_down, 0)

    row_hops_start(1, wd, zr_d)
    d_out = jnp.where(live, cot_ref[...].astype(F32), 0.0)
    for p in (3, 1, 2):
        relay_send(ag2, 2, 0, p, 1)
    pre_two = relay_total(st, 1, 1)
    hops_step(0, wgu, zr_gu, 1)
    relay_done(st, 1)
    hid = hidden[...]
    second_scale = lax.rsqrt(jnp.mean(hid * hid, axis=1, keepdims=True) + EPS)
    second_hat = hid * second_scale
    grad_two = jnp.sum(pre_two * second_hat, axis=0, keepdims=True)
    dn_two = pre_two * gain_two
    d_hid = d_out + second_scale * (
        dn_two - second_hat * jnp.mean(dn_two * second_hat, axis=1, keepdims=True)
    )
    dhid[...] = d_hid
    ag4[0] = d_hid.astype(BF)
    ag_start(ag4, 3)

    ag_done(ag3, 2)
    ghead[...] = jnp.zeros_like(ghead)

    def piece_at(item, out, rows, rank, cut=None):
        u = unit(rank)
        start, size = (0, rows) if cut is None else (cut * (rows // 2), rows // 2)
        if item == 0:
            return out.at[u, pl.ds(start, size), :]
        if item > 2:
            return out.at[u, pl.ds(start, size), all_q if item == 3 else all_kv]
        first = pl.multiple_of(lax.rem(u, GPF) * rows + start, rows // 2)
        return out.at[pl.ds(first, size), :]

    def has(item, rank, fn):
        if item in (0, 3, 4):
            fn()
        else:
            pl.when(unit(rank) // GPF == f)(fn)

    def fin_copy(item, src, dst, sem, to):
        return remote(src, dst, fin_s.at[item, sem], fin_r.at[item, sem], to, f)

    def fin_start(item, src, out, rows):
        def go():
            dst = piece_at(item, out, rows, t)
            fin_copy(item, src, dst, 2, xn).start()
            fin_copy(item, src, dst, 4, yn).start()
            fin_copy(item, src, dst, 1, sib).start()
            pltpu.make_async_copy(src, dst, fin_s.at[item, 0]).start()

        has(item, t, go)

    def fin_step(item, out, rows, k):
        rank = flip(k)
        full = piece_at(item, out, rows, rank)

        def go():
            if k < 6:
                wait_recv(full, fin_r.at[item, k])
                part = piece_at(item, out, rows, rank, k // 4)
                fin_copy(item, part, part, 4 + k, yn if k == 2 else xn).start()
            else:
                wait_recv(piece_at(item, out, rows, rank, 0), fin_r.at[item, 6])
                wait_recv(piece_at(item, out, rows, rank, 1), fin_r.at[item, 8])
            fin_copy(item, full, full, k + 1, sib).start()

        has(item, rank, go)

    def fin_end(item, src, out, rows):
        for k in (1, 3, 5, 7):
            full = piece_at(item, out, rows, flip(k))
            has(item, flip(k), lambda: wait_recv(full, fin_r.at[item, k]))

        def mine():
            for k in (1, 2, 4):
                wait_send(src, fin_s.at[item, k])
            pltpu.make_async_copy(src, piece_at(item, out, rows, t), fin_s.at[item, 0]).wait()

        has(item, t, mine)
        for k in (2, 4, 6):
            full = piece_at(item, out, rows, flip(k))
            part = piece_at(item, out, rows, flip(k), 0)

            def passed():
                wait_send(full, fin_s.at[item, k + 1])
                if k < 6:
                    wait_send(part, fin_s.at[item, 4 + k])

            has(item, flip(k), passed)

    gu_piece = wgu.at[own(Dz), :]
    q_piece, kv_piece = wqkv.at[own(Dz), all_q], wqkv.at[own(Dz), all_kv]
    go_piece = st.at[0]

    def grad_out(m, carry):
        at = pl.ds(pl.multiple_of(m * step, step), step)
        left, right = att[...], ag4[:, :, at]
        total = mm_tn(
            left.reshape(T * B, left.shape[2]), right.reshape(T * B, right.shape[2])
        )
        st[0, :, at] = total.astype(BF)
        return carry

    def backward_block(i, carry):
        ag_step(ag4, 3, i)

        @pl.when(i == 0)
        def _():
            if F > 2:
                hops_step(0, wgu, zr_gu, 2)

        @pl.when(i == 2)
        def _():
            for n in range(3, F):
                hops_step(0, wgu, zr_gu, n)

        @pl.when(i == 3)
        def _():
            row_hops_step(1, wd, zr_d, 1)

        @pl.when(i == 6)
        def _():
            hops_total(0, wgu, zr_gu)
            fin_start(0, gu_piece, ggu_out, Dz)

        @pl.when(i == 6)
        def _():
            for n in range(2, F - 1):
                row_hops_step(1, wd, zr_d, n)

        @pl.when(i == 7)
        def _():
            lax.fori_loop(0, D // step, grad_out, 0)
            row_hops_start(2, go_piece, zr_o)

        cos, sin = turns(i)
        d_att = mm_nt(ag4[i], wo[...]).astype(BF)
        k_rot = rot[i, :, QT : QT + HEAD]
        v = rot[i, :, QT + HEAD : QT + 2 * HEAD]
        d_v = jnp.zeros((B, HEAD), F32)
        d_k = jnp.zeros((B, HEAD), F32)
        d_pre = []
        sums = []

        def norm_back(grad, n, gain):
            x = qkpre[i, :, n * HEAD : (n + 1) * HEAD]
            scale = head_scale(x)
            hat = x * scale
            dn = rotate(grad, cos, -sin)
            total = jnp.sum(dn * hat, axis=0, keepdims=True)
            dn = dn * gain
            back = scale * (dn - hat * jnp.mean(dn * hat, axis=1, keepdims=True))
            return back.astype(BF), total

        for n in range(2):
            prob = probs[i, n * B : (n + 1) * B, :]
            q_rot = rot[i, :, n * HEAD : (n + 1) * HEAD]
            d_head = d_att[:, n * HEAD : (n + 1) * HEAD]
            d_prob = mm_nt(d_head, v)
            p32 = prob.astype(F32)
            center = jnp.sum(p32 * d_prob, axis=1, keepdims=True)
            d_score = (p32 * (d_prob - center)).astype(BF)
            d_v = d_v + mm_tn(prob, d_head)
            d_k = d_k + mm_tn(d_score, q_rot)
            back, total = norm_back(mm(d_score, k_rot) * score_scale, n, gain_q)
            d_pre.append(back)
            sums.append(total)
        back, total = norm_back(d_k * score_scale, 2, gain_k)
        d_pre.append(back)
        d_pre.append(d_v.astype(BF))
        ghead[0:1, :] += sums[0] + sums[1]
        ghead[1:2, :] += total
        for n in range(4):
            rot[i, :, n * HEAD : (n + 1) * HEAD] = d_pre[n]
        ag3[i] = mm_nt(rot[i], wqkv[...]).astype(BF)
        @pl.when(lax.rem(i, 2) == 1)
        def _():
            sib_send(ag3, 3, 1, i)

        for when, p in ((4, 1), (6, 2)):

            @pl.when(i == when)
            def _():
                relay_send(ag3, 3, 1, p, 1)

        for when, p, first in ((3, 1, 0), (3, 2, 0)):

            @pl.when(i == when)
            def _():
                relay_send(ag2, 2, 0, p, first)

        return carry

    lax.fori_loop(0, T, backward_block, 0)
    relay_send(ag3, 3, 1, 3, 1)
    row_hops_total(1, wd, zr_d)
    fin_start(1, wd, gd_out, FT)
    cols_done(0, wqkv, Dz)
    rows_done(1, wo)

    def grad_qkv(m, carry):
        at = pl.ds(pl.multiple_of(m * step, step), step)
        left, right = ag1[:, 0:B, at], rot[...]
        total = mm_tn(
            left.reshape(T * B, left.shape[2]), right.reshape(T * B, right.shape[2])
        )
        wqkv[at, :] = total.astype(BF)
        return carry

    lax.fori_loop(0, D // step, grad_qkv, 0)
    scatter(3, wqkv, zr_qkv, all_q)
    scatter(4, wqkv, zr_qkv, all_kv)
    relay_send(ag3, 3, 1, 1, 0)
    relay_send(ag3, 3, 1, 2, 0)

    row_hops_step(2, go_piece, zr_o, 1)
    for k in (2, 4):
        fin_step(0, ggu_out, Dz, k)

    pre_one = relay_total(ag3, 3, 1)
    tokens = tok_ref[...].astype(F32)
    first_scale = lax.rsqrt(jnp.mean(tokens * tokens, axis=1, keepdims=True) + EPS)
    first_hat = tokens * first_scale
    grad_one = jnp.sum(pre_one * first_hat, axis=0, keepdims=True)
    dn_one = pre_one * gain_one
    dtok_out[...] = (
        dhid[...]
        + first_scale
        * (dn_one - first_hat * jnp.mean(dn_one * first_hat, axis=1, keepdims=True))
    ).astype(BF)
    vz[f, 0:1, :] = grad_one
    vz[f, 1:2, :] = grad_two
    vz[f, 2:3, :] = jnp.concatenate(
        [ghead[0:1, :], ghead[1:2, :], jnp.zeros((1, D - 2 * HEAD), F32)], axis=1
    )
    vz[f, 3:8, :] = jnp.zeros((5, D), F32)

    def vec_send(d, to, _):
        remote(vz.at[f], vz.at[f], vz_s.at[d], vz_r.at[d], r, to).start()

    others(vec_send)
    for n in range(2, F - 1):
        row_hops_step(2, go_piece, zr_o, n)
    fin_step(0, ggu_out, Dz, 6)
    for k in (2, 4):
        fin_step(1, gd_out, FT, k)
    out = hidden[...] + relay_total(ag2, 2, 0)
    mixed_out[...] = jnp.where(live, out, 0.0).astype(BF)
    scatter_total(3, wqkv, zr_qkv, all_q)
    fin_start(3, q_piece, gqkv_out, Dz)

    def vec_recv(d, to, fs):
        wait_recv(vz.at[fs], vz_r.at[d])

    others(vec_recv)
    total = vz[0]
    for j in range(1, F):
        total = total + vz[j]
    vp[t] = total
    for k in range(1, T):
        remote(vp.at[t], vp.at[t], vp_s.at[k], vp_r.at[k], base + flip(k), f).start()
    row_hops_total(2, go_piece, zr_o)
    fin_start(2, go_piece, go_out, QT)
    fin_step(1, gd_out, FT, 6)
    scatter_total(4, wqkv, zr_qkv, all_kv)
    fin_start(4, kv_piece, gqkv_out, Dz)
    for k in range(1, T):
        wait_recv(vp.at[flip(k)], vp_r.at[k])
    total = vp[0]
    for j in range(1, T):
        total = total + vp[j]
    mine = jnp.zeros((8, Dz), F32)
    for j in range(F):
        mine = mine + jnp.where(f == j, total[:, j * Dz : (j + 1) * Dz], 0.0)
    vec_out[:, 0:Dz] = mine
    vec_out[:, Dz : Dz + 2 * HEAD] = total[:, 0 : 2 * HEAD]
    for k in (2, 4, 6):
        fin_step(3, gqkv_out, Dz, k)
        fin_step(2, go_out, QT, k)
        fin_step(4, gqkv_out, Dz, k)
    fin_end(0, gu_piece, ggu_out, Dz)
    fin_end(1, wd, gd_out, FT)
    fin_end(3, q_piece, gqkv_out, Dz)
    fin_end(2, go_piece, go_out, QT)
    fin_end(4, kv_piece, gqkv_out, Dz)

    ag_done(ag1, 0)
    ag_done(ag4, 3)
    relay_done(ag2, 2)
    relay_done(ag3, 3)
    hops_done(0, wgu)
    scatter_done(3, wqkv, all_q)
    scatter_done(4, wqkv, all_kv)
    row_hops_done(1, wd)
    row_hops_done(2, go_piece)
    for d in range(1, F):
        wait_send(normsb.at[0], nz_s.at[d])
        wait_send(vz.at[0], vz_s.at[d])
    for k in range(1, T):
        wait_send(vp.at[0], vp_s.at[k])


def finish_kernel(
    scale, gqkv, ggu, go, gd, vec, mixed, dtok, oq, ok, ov, og, ou, oo, od, o1, o2, oh, om, ot
):
    n = gqkv.shape[0]
    w, v = oq.shape[1] // n, og.shape[1] // n
    for i in range(n):
        x = gqkv[i].astype(F32) * scale
        oq[:, i * w : (i + 1) * w] = x[:, 0:w]
        ok[:, i * HEAD : (i + 1) * HEAD] = x[:, w : w + HEAD]
        ov[:, i * HEAD : (i + 1) * HEAD] = x[:, w + HEAD : w + 2 * HEAD]
        x = ggu[i].astype(F32) * scale
        og[:, i * v : (i + 1) * v] = x[:, 0:v]
        ou[:, i * v : (i + 1) * v] = x[:, v : 2 * v]
    oo[...] = go[...].astype(F32) * scale
    od[...] = gd[...].astype(F32) * scale
    om[...] = mixed[...]
    ot[...] = dtok[...]

    @pl.when(pl.program_id(0) == 0)
    def _():
        w = o1.shape[1]
        o1[...] = vec[0:1, 0:w] * scale
        o2[...] = vec[1:2, 0:w] * scale
        oh[0:1, :] = vec[2:3, w : w + HEAD] * scale
        oh[1:2, :] = vec[2:3, w + HEAD : w + 2 * HEAD] * scale


def per_device(
    F,
    G,
    tokens,
    doc_lengths,
    attn_norm,
    w_query,
    key_matrix,
    value_matrix,
    head_norms,
    w_out,
    ffn_norm,
    w_gate,
    w_up,
    w_down,
    cotangent,
):
    B, D = tokens.shape
    Dz = D // F
    QW, KW, FF = w_query.shape[1], key_matrix.shape[1], w_gate.shape[1]
    QT, FT = QW // T, FF // T
    QZ, FZ = w_out.shape[0], w_down.shape[0]
    norms = jnp.zeros((8, Dz), F32)
    norms = norms.at[0].set(attn_norm.astype(F32)).at[1].set(ffn_norm.astype(F32))
    table = jnp.asarray(rope_table(B))
    vmem = pl.BlockSpec(memory_space=pltpu.VMEM)
    hbm = pl.BlockSpec(memory_space=pl.ANY)
    dma = pltpu.SemaphoreType.DMA
    sds = jax.ShapeDtypeStruct
    outs = pl.pallas_call(
        functools.partial(layer_kernel, F, B, D),
        out_shape=(
            sds((T, Dz, QT + 2 * HEAD), BF),
            sds((T, Dz, 2 * FT), BF),
            sds((QZ, D), BF),
            sds((FZ, D), BF),
            sds((8, Dz + 2 * HEAD), F32),
            sds((B, D), BF),
            sds((B, D), BF),
        ),
        in_specs=[vmem, vmem, pl.BlockSpec(memory_space=pltpu.SMEM), vmem, vmem, vmem] + [hbm] * 7,
        out_specs=(hbm, hbm, hbm, hbm, vmem, vmem, vmem),
        scratch_shapes=[
            pltpu.VMEM((T, B + 16, D), BF),
            pltpu.VMEM((T, B, D), BF),
            pltpu.VMEM((T, B, D), BF),
            pltpu.VMEM((T, B, D), BF),
            pltpu.VMEM((T, B, D), BF),
            pltpu.VMEM((2, 4, B, D), BF),
            pltpu.VMEM((2, 3, B, D), BF),
            pltpu.VMEM((D, QT + 2 * HEAD), BF),
            pltpu.VMEM((D, 2 * FT), BF),
            pltpu.VMEM((QT, D), BF),
            pltpu.VMEM((FT, D), BF),
            pltpu.VMEM((T, B, QT + HEAD), F32),
            pltpu.VMEM((T, B, QT + 2 * HEAD), BF),
            pltpu.VMEM((T, 2 * B, B), BF),
            pltpu.VMEM((T, B, QT), BF),
            pltpu.VMEM((T, B, 3 * FT), BF),
            pltpu.VMEM((B, D), F32),
            pltpu.VMEM((B, D), F32),
            pltpu.VMEM((F, 8, Dz), F32),
            pltpu.VMEM((F + 1, Dz, 2 * FT), BF),
            pltpu.VMEM((2, FT, D), BF),
            pltpu.VMEM((2, QT, D), BF),
            pltpu.VMEM((F, Dz, QT + 2 * HEAD), BF),
            pltpu.VMEM((F, 8, D), F32),
            pltpu.VMEM((T, 8, D), F32),
            pltpu.VMEM((8, HEAD), F32),
            pltpu.VMEM((T, B, HEAD), F32),
            dma((4, 9)),
            dma((4, 9)),
            dma((4, 4)),
            dma((4, 4)),
            dma((4, 6)),
            dma((4, 6)),
            dma((4, 2, F)),
            dma((4, 2, F)),
            dma((F,)),
            dma((F,)),
            dma((8,)),
            dma((5, 2, F)),
            dma((5, 2, F)),
            dma((5, 9)),
            dma((5, 9)),
            dma((F,)),
            dma((F,)),
            dma((T,)),
            dma((T,)),
        ],
        compiler_params=pltpu.CompilerParams(
            collective_id=0, has_side_effects=True, vmem_limit_bytes=62 * 2**20
        ),
    )(
        tokens,
        cotangent,
        doc_lengths,
        norms,
        head_norms,
        table,
        w_query,
        key_matrix,
        value_matrix,
        w_out,
        w_gate,
        w_up,
        w_down,
    )
    gqkv, ggu, go, gd, vec, mixed, d_tokens = outs
    if G > 1:
        groups = [[t + T * n for n in range(G)] for t in range(T)]
        gqkv, ggu, go, gd = (
            lax.psum(x, "rep", axis_index_groups=groups) for x in (gqkv, ggu, go, gd)
        )
        vec = lax.psum(vec, "rep", axis_index_groups=groups)
    scale = 1.0 / math.sqrt(B * T * G * F)

    steps = 4
    n = T // steps
    qb, fb = QZ // steps, FZ // steps
    bb = B // steps
    oq, ok, ov, og, ou, oo, od, o1, o2, oh, mixed, d_tokens = pl.pallas_call(
        functools.partial(finish_kernel, scale),
        grid=(steps,),
        out_shape=(
            sds((Dz, QW), F32),
            sds((Dz, KW), F32),
            sds((Dz, KW), F32),
            sds((Dz, FF), F32),
            sds((Dz, FF), F32),
            sds((QZ, D), F32),
            sds((FZ, D), F32),
            sds((1, Dz), F32),
            sds((1, Dz), F32),
            sds((2, HEAD), F32),
            sds((B, D), BF),
            sds((B, D), BF),
        ),
        in_specs=[
            pl.BlockSpec((n, Dz, QT + 2 * HEAD), lambda u: (u, 0, 0)),
            pl.BlockSpec((n, Dz, 2 * FT), lambda u: (u, 0, 0)),
            pl.BlockSpec((qb, D), lambda u: (u, 0)),
            pl.BlockSpec((fb, D), lambda u: (u, 0)),
            pl.BlockSpec((8, Dz + 2 * HEAD), lambda u: (0, 0)),
            pl.BlockSpec((bb, D), lambda u: (u, 0)),
            pl.BlockSpec((bb, D), lambda u: (u, 0)),
        ],
        out_specs=(
            pl.BlockSpec((Dz, n * QT), lambda u: (0, u)),
            pl.BlockSpec((Dz, n * HEAD), lambda u: (0, u)),
            pl.BlockSpec((Dz, n * HEAD), lambda u: (0, u)),
            pl.BlockSpec((Dz, n * FT), lambda u: (0, u)),
            pl.BlockSpec((Dz, n * FT), lambda u: (0, u)),
            pl.BlockSpec((qb, D), lambda u: (u, 0)),
            pl.BlockSpec((fb, D), lambda u: (u, 0)),
            pl.BlockSpec((1, Dz), lambda u: (0, 0)),
            pl.BlockSpec((1, Dz), lambda u: (0, 0)),
            pl.BlockSpec((2, HEAD), lambda u: (0, 0)),
            pl.BlockSpec((bb, D), lambda u: (u, 0)),
            pl.BlockSpec((bb, D), lambda u: (u, 0)),
        ),
    )(gqkv, ggu, go, gd, vec, mixed, d_tokens)
    return (
        mixed,
        d_tokens,
        o1.reshape(Dz),
        oq,
        ok,
        ov,
        oh,
        oo,
        o2.reshape(Dz),
        og,
        ou,
        od,
    )


def solution(mesh):
    F = mesh.shape["fsdp"]
    G = mesh.shape["rep"] // T
    rows = P(("rep", "fsdp"), None)
    mat = P("fsdp", None)
    vec = P("fsdp")
    return jax.shard_map(
        functools.partial(per_device, F, G),
        mesh=mesh,
        in_specs=(rows, rows, vec, mat, mat, mat, P(), mat, vec, mat, mat, mat, rows),
        out_specs=(rows, rows, vec, mat, mat, mat, P(), mat, vec, mat, mat, mat),
        check_vma=False,
    )
```
